32 devices in a mesh: dp: 8 (over y, x, core), mp: 4 (over z).
Axes of the slice: x: 2, y: 2, z: 4, core: 2. Of those that a mesh axis runs over, the one named last changes fastest.
Arguments:
- tokens: bfloat16 [8192, 1024], P('dp'), may hold values from -30 to 30
- query_key_value_weight: bfloat16 [1024, 3072], P(None, 'mp'), may hold values from -0.1875 to 0.1875
- adapter_down_weight: bfloat16 [1024, 512], P(None, 'mp'), may hold values from -0.1875 to 0.1875
- adapter_up_weight: bfloat16 [512, 3072], P('mp'), may hold values from -0.75 to 0.75
- attention_out_weight: bfloat16 [1024, 1024], P('mp'), may hold values from -0.1875 to 0.1875
- first_norm_gain: float32 [1024], replicated, may hold values from 0.5 to 1.5
- first_norm_bias: float32 [1024], replicated, may hold values from -3 to 3
- first_feed_weight: bfloat16 [1024, 4096], P(None, 'mp'), may hold values from -0.1875 to 0.1875
- first_feed_bias: float32 [4096], P('mp'), may hold values from -3 to 3
- second_feed_weight: bfloat16 [4096, 1024], P('mp'), may hold values from -0.09375 to 0.09375
- second_feed_bias: float32 [1024], replicated, may hold values from -3 to 3
- second_norm_gain: float32 [1024], replicated, may hold values from 0.5 to 1.5
- second_norm_bias: float32 [1024], replicated, may hold values from -3 to 3
- following_qkv_weight: bfloat16 [1024, 3072], P(None, 'mp'), may hold values from -0.1875 to 0.1875
- following_bias: float32 [3072], P('mp'), may hold values from -3 to 3
- request_page_count: int32 [4], replicated, may hold values from 1 to 32, 64 in all
- page_slot_table: int32 [64], replicated, may hold values from 0 to 63, each once
- request_adapter: int32 [4], replicated, may hold values from 0 to 31, as said below
Outputs:
- layer_out: bfloat16 [8192, 1024], P(('dp', 'mp'))
- next_qkv: bfloat16 [8192, 3072], P('dp', 'mp')
The draws below stay inside these ranges and needn't reach their ends.
Inputs may be any that keep to these rules, and one draw needn't show every extreme that they name: `request_page_count`: the counts sum to 64; the longest request has exactly 32 pages. `page_slot_table`: names every page slot once. `request_adapter`: exactly min(16, 4) distinct adapters are named, adapters 0 and 31 among them; of the 8 adapters held by one index of mp at most 1 are named, and some index holds exactly 1 named ones.
All inputs are finite; a program needn't handle non-finite values.
Results may differ from the reference program's by a relative error of at most 0.015.
Values may be sent and summed in bfloat16 or wider, within the bound.
No kernel may reach another device: no remote copies, remote signals or barrier semaphores. Data moves between devices by JAX's collectives and lax.ppermute only.
A program may use at most 64 MiB of HBM per device.

```python
import math
import jax
import jax.numpy as jnp
import numpy as np
from jax import lax

MODEL_WIDTH = 1024
HEADS = 16
FF = 4096
HEAD_DIM = 64
ADAPTER_RANK = 16
PAGE = 128
ACTIVE = 16
ADAPTER_DEV = 8
REQS = 4
NPAGES = 64
MOST_PAGES = 32
TOKEN_TOTAL = 8192
ADAPTER_TOTAL = 32
N_MP = 4


def draw_tokens(key, part):
    first_key = jax.random.fold_in(key, 0)
    drawn = jax.random.truncated_normal(first_key, -6.0, 6.0, (TOKEN_TOTAL, MODEL_WIDTH), jnp.float32)
    return drawn.astype(jnp.bfloat16)


def draw_request_adapter(key, part):
    level_key, owner_key, assign_key, shuffle_key = jax.random.split(jax.random.fold_in(key, 17), 4)
    owners = ADAPTER_TOTAL // ADAPTER_DEV
    owner_keys = jax.random.split(level_key, owners)
    levels = jax.vmap(lambda single: jax.random.permutation(single, jnp.arange(ADAPTER_DEV, dtype=jnp.int32)))(owner_keys)
    owner_index = jnp.arange(owners, dtype=jnp.int32)
    anchor = jnp.where(owner_index == owners - 1, ADAPTER_DEV - 1, 0).astype(jnp.int32)
    anchor_level = jnp.take_along_axis(levels, anchor[:, None], axis=1)
    levels = ((levels - anchor_level) % ADAPTER_DEV).astype(jnp.int32)
    middle = jax.random.permutation(owner_key, jnp.arange(1, owners - 1, dtype=jnp.int32))
    owner_order = jnp.concatenate([jnp.array([0, owners - 1], jnp.int32), middle])
    owner_rank = jnp.argsort(owner_order, stable=True).astype(jnp.int32)
    order_key = (levels * owners + owner_rank[:, None]).reshape(-1)
    chosen = jnp.argsort(order_key, stable=True).astype(jnp.int32)
    distinct = min(ACTIVE, REQS)
    assigned = jax.random.randint(assign_key, (REQS,), 0, distinct, dtype=jnp.int32)
    request_index = jnp.arange(REQS, dtype=jnp.int32)
    assigned = jnp.where(request_index < distinct, request_index, assigned)
    assigned = jax.random.permutation(shuffle_key, assigned)
    return chosen[assigned].astype(jnp.int32)


def block_scale(key, dims, pieces, smallest, top_value):
    def one(axis_at, blocks):
        steps = jax.random.uniform(jax.random.fold_in(jax.random.fold_in(key, 6), axis_at), (blocks,), jnp.float32, smallest / len(pieces), top_value / len(pieces))
        return jnp.repeat(jnp.exp(steps), dims[axis_at] // blocks).reshape((-1,) + (1,) * (len(dims) - axis_at - 1))

    gain = one(*pieces[0])
    for cut in pieces[1:]:
        gain = gain * one(*cut)
    return gain


def split_up(amount, total, limit, slope):
    loads = [(1 << 20) // math.isqrt(grade ** slope) + 1 for grade in range(2, amount + 1)]
    spare, given = total - limit - (amount - 1), [1] * (amount - 1)
    while spare > 0:
        candidates = [i for i in range(amount - 1) if given[i] < limit]
        mass, budget = sum([loads[i] for i in candidates]), spare
        for i in candidates:
            extra = min(limit - given[i], max(1, budget * loads[i] // mass), spare)
            given[i] = given[i] + extra
            spare = spare - extra
    return np.array([limit] + given)


def uneven_parts(stream_key, count, total, limit, lean):
    if count == 2:
        one = jax.random.randint(stream_key, (), max(1, total - limit), min(limit, total - 1) + 1)
        return jnp.stack([one, total - one])
    sizes = jnp.asarray(split_up(count, total, limit, lean), jnp.int32)
    couples = (count - 1) // 2
    donor, receiver = sizes[1:1 + 2 * couples:2], sizes[2:2 + 2 * couples:2]
    slack = jnp.minimum(donor - 1, limit - receiver)
    moved = jax.random.randint(jax.random.fold_in(stream_key, 1), (couples,), 0, 1 << 20) % (slack + 1)
    sizes = sizes.at[1:1 + 2 * couples:2].set(donor - moved).at[2:2 + 2 * couples:2].set(receiver + moved)
    return sizes[jax.random.permutation(jax.random.fold_in(stream_key, 2), count)]


def noise(key, extent, deviation, limit, cuts=(), kind=jnp.bfloat16):
    values = deviation * jax.random.normal(key, extent, jnp.float32)
    if cuts:
        values = values * block_scale(key, extent, cuts, -0.22, 0.18)
    return jnp.clip(values, -limit, limit).astype(kind)


def setup_inputs(seed: int = 0) -> dict:
    keys = jax.random.split(jax.random.key(seed), 19)
    tokens = draw_tokens(jax.random.fold_in(keys[18], 71), 0)
    query_key_value_weight = noise(keys[1], (MODEL_WIDTH, 3 * MODEL_WIDTH), MODEL_WIDTH ** -0.5, 0.1875, ((1, 4),))
    adapter_down_weight = noise(keys[2], (MODEL_WIDTH, ADAPTER_TOTAL * ADAPTER_RANK), MODEL_WIDTH ** -0.5, 0.1875, ((1, 4),))
    adapter_up_weight = noise(keys[3], (ADAPTER_TOTAL * ADAPTER_RANK, 3 * MODEL_WIDTH), (4 * ADAPTER_RANK) ** -0.5, 0.75, ((0, 4),))
    attention_out_weight = noise(keys[4], (MODEL_WIDTH, MODEL_WIDTH), MODEL_WIDTH ** -0.5, 0.1875, ((0, 4),))
    first_norm_gain = jnp.clip(1.0 + 0.1 * jax.random.normal(keys[5], (MODEL_WIDTH,), jnp.float32), 0.5, 1.5)
    first_norm_bias = noise(keys[6], (MODEL_WIDTH,), 0.5, 3.0, (), jnp.float32)
    first_feed_weight = noise(keys[7], (MODEL_WIDTH, FF), MODEL_WIDTH ** -0.5, 0.1875, ((1, 4),))
    first_feed_bias = noise(keys[8], (FF,), 0.5, 3.0, ((0, 4),), jnp.float32)
    second_feed_weight = noise(keys[9], (FF, MODEL_WIDTH), FF ** -0.5, 0.09375, ((0, 4),))
    second_feed_bias = noise(keys[10], (MODEL_WIDTH,), 0.5, 3.0, (), jnp.float32)
    second_norm_gain = jnp.clip(1.0 + 0.1 * jax.random.normal(keys[11], (MODEL_WIDTH,), jnp.float32), 0.5, 1.5)
    second_norm_bias = noise(keys[12], (MODEL_WIDTH,), 0.5, 3.0, (), jnp.float32)
    following_qkv_weight = noise(keys[13], (MODEL_WIDTH, 3 * MODEL_WIDTH), MODEL_WIDTH ** -0.5, 0.1875, ((1, 4),))
    following_bias = noise(keys[14], (3 * MODEL_WIDTH,), 0.5, 3.0, ((0, 4),), jnp.float32)
    request_page_count = uneven_parts(keys[15], REQS, NPAGES, MOST_PAGES, 2).astype(jnp.int32)
    page_slot_table = jax.random.permutation(keys[16], NPAGES).astype(jnp.int32)
    request_adapter = draw_request_adapter(jax.random.fold_in(keys[18], 71), 0)
    return {"tokens": tokens, "query_key_value_weight": query_key_value_weight, "adapter_down_weight": adapter_down_weight, "adapter_up_weight": adapter_up_weight, "attention_out_weight": attention_out_weight, "first_norm_gain": first_norm_gain, "first_norm_bias": first_norm_bias, "first_feed_weight": first_feed_weight, "first_feed_bias": first_feed_bias, "second_feed_weight": second_feed_weight, "second_feed_bias": second_feed_bias, "second_norm_gain": second_norm_gain, "second_norm_bias": second_norm_bias, "following_qkv_weight": following_qkv_weight, "following_bias": following_bias, "request_page_count": request_page_count, "page_slot_table": page_slot_table, "request_adapter": request_adapter}


def request_slots(request_page_count, page_slot_table):
    page_ends = jnp.cumsum(request_page_count).astype(jnp.int32)
    logical = jnp.arange(NPAGES, dtype=jnp.int32)
    request_of = lax.optimization_barrier(jnp.sum((logical[:, None] >= page_ends[None, :]).astype(jnp.int32), axis=1)).astype(jnp.int32)
    matched = (page_slot_table[:, None] == logical[None, :]).astype(jnp.int32)
    return lax.optimization_barrier(jnp.sum(matched * request_of[:, None], axis=0)).astype(jnp.int32)

def layer_norm(values, gain_row, bias_row):
    average = lax.optimization_barrier(jnp.mean(values, axis=-1, keepdims=True))
    centered = values - average
    variance = lax.optimization_barrier(jnp.mean(centered * centered, axis=-1, keepdims=True))
    return centered * lax.rsqrt(variance + 1e-05) * gain_row + bias_row

def grouped_sum(left, right, groups):
    group_width = left.shape[1] // groups
    summed = jnp.zeros((left.shape[0], right.shape[1]), jnp.float32)
    for group_index in range(groups):
        lower = group_index * group_width
        partial_term = jnp.dot(left[:, lower:lower + group_width], right[lower:lower + group_width], preferred_element_type=jnp.float32)
        rounded = lax.optimization_barrier(partial_term.astype(jnp.bfloat16))
        summed = summed + rounded.astype(jnp.float32)
    return summed

def reference(tokens, query_key_value_weight, adapter_down_weight, adapter_up_weight, attention_out_weight, first_norm_gain, first_norm_bias, first_feed_weight, first_feed_bias, second_feed_weight, second_feed_bias, second_norm_gain, second_norm_bias, following_qkv_weight, following_bias, request_page_count, page_slot_table, request_adapter):
    slot_req = request_slots(request_page_count, page_slot_table)
    tok_req = jnp.repeat(slot_req, PAGE, total_repeat_length=TOKEN_TOTAL)
    tok_adapter = request_adapter[tok_req]
    one_hot = tok_adapter[:, None] == jnp.arange(ADAPTER_TOTAL, dtype=jnp.int32)[None, :]
    grid_positions = jnp.dot(tokens, adapter_down_weight, preferred_element_type=jnp.float32).reshape(TOKEN_TOTAL, ADAPTER_TOTAL, ADAPTER_RANK)
    low_rank = lax.optimization_barrier(jnp.sum(jnp.where(one_hot[:, :, None], grid_positions, jnp.float32(0.0)), axis=1)).astype(jnp.bfloat16)
    widened_rows = jnp.where(one_hot[:, :, None], low_rank[:, None, :], jnp.zeros((), jnp.bfloat16)).reshape(TOKEN_TOTAL, ADAPTER_TOTAL * ADAPTER_RANK)
    projected_rows = (jnp.dot(tokens, query_key_value_weight, preferred_element_type=jnp.float32) + jnp.dot(widened_rows, adapter_up_weight, preferred_element_type=jnp.float32)).astype(jnp.bfloat16)
    per_head = projected_rows.reshape(TOKEN_TOTAL, HEADS, 3, HEAD_DIM)
    queries = per_head[:, :, 0]
    key_all = per_head[:, :, 1]
    value_all = per_head[:, :, 2]
    page_ends = jnp.cumsum(request_page_count).astype(jnp.int32)
    page_starts = page_ends - request_page_count
    score_scale = HEAD_DIM ** (-0.5)

    def attend_slot(slot_index):
        request = slot_req[slot_index]
        first_page = page_starts[request]
        last_page = page_ends[request]
        logical = first_page + jnp.arange(MOST_PAGES, dtype=jnp.int32)
        usable = logical < last_page
        key_pages = page_slot_table[jnp.minimum(logical, NPAGES - 1)]
        key_rows = (key_pages[:, None] * PAGE + jnp.arange(PAGE, dtype=jnp.int32)[None, :]).reshape(-1)
        key_mask = jnp.repeat(usable, PAGE, total_repeat_length=MOST_PAGES * PAGE)
        key_block = key_all[key_rows].astype(jnp.float32)
        value_block = value_all[key_rows].astype(jnp.float32)
        slot_queries = lax.dynamic_slice_in_dim(queries, (slot_index * PAGE).astype(jnp.int32), PAGE, 0).astype(jnp.float32)
        scores = jnp.einsum('qhe,khe->hqk', slot_queries, key_block) * score_scale
        masked = jnp.where(key_mask[None, None, :], scores, jnp.float32(-1e+30))
        row_max = lax.optimization_barrier(jnp.max(masked, axis=2, keepdims=True))
        weights = jnp.where(key_mask[None, None, :], jnp.exp(masked - row_max), jnp.float32(0.0))
        denominator = lax.optimization_barrier(jnp.sum(weights, axis=2))
        numerator = jnp.einsum('hqk,khe->qhe', weights.astype(jnp.bfloat16).astype(jnp.float32), value_block)
        return (numerator / jnp.transpose(denominator)[:, :, None]).astype(jnp.bfloat16)
    context = lax.map(attend_slot, jnp.arange(NPAGES, dtype=jnp.int32)).reshape(TOKEN_TOTAL, MODEL_WIDTH)
    attention = grouped_sum(context, attention_out_weight, N_MP)
    normed = layer_norm(tokens.astype(jnp.float32) + attention, first_norm_gain, first_norm_bias).astype(jnp.bfloat16)
    hidden = jax.nn.gelu(jnp.dot(normed, first_feed_weight, preferred_element_type=jnp.float32) + first_feed_bias, approximate=False).astype(jnp.bfloat16)
    feed = grouped_sum(hidden, second_feed_weight, N_MP)
    layer_out = layer_norm(normed.astype(jnp.float32) + feed + second_feed_bias, second_norm_gain, second_norm_bias).astype(jnp.bfloat16)
    next_qkv = (jnp.dot(layer_out, following_qkv_weight, preferred_element_type=jnp.float32) + following_bias).astype(jnp.bfloat16)
    return (layer_out, next_qkv)
```

```python
import functools
import math

import jax
import jax.numpy as jnp
from jax import lax
from jax.experimental import pallas as pl
from jax.experimental.pallas import tpu as pltpu
from jax.sharding import PartitionSpec as P

HEAD_DIM = 64
ADAPTER_RANK = 16
PAGE = 128
PAIR = 2 * HEAD_DIM
NEG = -1e30
EXP_SCALE = math.log2(math.e) * HEAD_DIM**-0.5
MIB = 1 << 20


def params(vmem=48):
    return pltpu.CompilerParams(
        dimension_semantics=("arbitrary",), vmem_limit_bytes=vmem * MIB
    )


def request_of(k, counts, requests):
    end = counts[0]
    request = (k >= end).astype(jnp.int32)
    for r in range(1, requests - 1):
        end = end + counts[r]
        request = request + (k >= end).astype(jnp.int32)
    return request


def normalize(values, gain_row, bias_row):
    average = jnp.mean(values, axis=-1, keepdims=True)
    centered = values - average
    variance = jnp.mean(centered * centered, axis=-1, keepdims=True)
    return centered * lax.rsqrt(variance + 1e-05) * gain_row + bias_row


def project_kernel(
    counts, table, owners, bases, x_ref, w_ref, down_ref, up_ref, q_ref, kv_ref, page_owner,
    *, requests, slots, pages, per_piece,
):
    step = pl.program_id(0)

    @pl.when(step == 0)
    def _():
        def fill(k, carry):
            page_owner[table[k]] = owners[request_of(k, counts, requests)]
            return carry

        lax.fori_loop(0, slots, fill, 0)

    x = x_ref[...]
    low = jnp.dot(x, down_ref[...], preferred_element_type=jnp.float32)
    lane_owner = lax.broadcasted_iota(jnp.int32, (PAGE, low.shape[1]), 1) // ADAPTER_RANK
    kept = []
    for p in range(pages):
        page = step * pages + p
        slot = bases[page // per_piece] + page % per_piece
        kept.append(
            jnp.where(lane_owner == page_owner[slot], low[p * PAGE : (p + 1) * PAGE], 0.0)
        )
    low_rank = jnp.concatenate(kept, axis=0).astype(jnp.bfloat16)
    rows = jnp.dot(x, w_ref[...], preferred_element_type=jnp.float32) + jnp.dot(
        low_rank, up_ref[...], preferred_element_type=jnp.float32
    )
    rows = rows.astype(jnp.bfloat16)
    q_cols = q_ref.shape[1]
    q_ref[...] = rows[:, :q_cols]
    kv_ref[...] = rows[:, q_cols:]


def project(counts, table, owners, bases, x, weight, down, up, per_piece):
    tok, width = x.shape
    cols = weight.shape[1]
    pages = 2
    block = pages * PAGE
    slots = table.shape[0]
    whole = lambda i, *_: (0, 0)
    rows = lambda i, *_: (i, 0)
    return pl.pallas_call(
        functools.partial(
            project_kernel,
            requests=counts.shape[0], slots=slots, pages=pages, per_piece=per_piece,
        ),
        grid_spec=pltpu.PrefetchScalarGridSpec(
            num_scalar_prefetch=4,
            grid=(tok // block,),
            in_specs=[
                pl.BlockSpec((block, width), rows),
                pl.BlockSpec(weight.shape, whole),
                pl.BlockSpec(down.shape, whole),
                pl.BlockSpec(up.shape, whole),
            ],
            out_specs=[
                pl.BlockSpec((block, cols // 3), rows),
                pl.BlockSpec((block, 2 * cols // 3), rows),
            ],
            scratch_shapes=[pltpu.SMEM((slots,), jnp.int32)],
        ),
        out_shape=[
            jax.ShapeDtypeStruct((tok, cols // 3), jnp.bfloat16),
            jax.ShapeDtypeStruct((tok, 2 * cols // 3), jnp.bfloat16),
        ],
        compiler_params=params(),
        cost_estimate=pl.CostEstimate(
            flops=2 * tok * width * cols, bytes_accessed=2 * tok * (width + cols), transcendentals=0
        ),
        name="project",
    )(counts, table, owners, bases, x, weight, down, up)


def attend_kernel(
    counts, table, q_bases, kv_bases, q_ref, *refs,
    requests, slots, q_per_piece, sizes, first, last, group,
):
    refs = list(refs)
    kv_hbm = [refs.pop(0) for _ in sizes]
    if not first:
        acc_in, stat_in = refs.pop(0), refs.pop(0)
    if last:
        out_ref = refs.pop(0)
    else:
        acc_out, stat_out = refs.pop(0), refs.pop(0)
    kv, scores, listed, amount, page_req, sems = refs
    step = pl.program_id(0)

    @pl.when(step == 0)
    def _():
        copies = []
        offset = 0
        for i, size in enumerate(sizes):
            copy = pltpu.make_async_copy(
                kv_hbm[i], kv.at[pl.ds(offset * PAGE, size * PAGE)], sems.at[i]
            )
            copy.start()
            copies.append(copy)
            offset += size
        for r in range(requests):
            amount[r] = 0

        def clear(k, carry):
            for r in range(requests):
                listed[r, k] = 0
            return carry

        lax.fori_loop(0, sum(sizes) + group, clear, 0)

        def fill(k, carry):
            r = request_of(k, counts, requests)
            slot = table[k]
            page_req[slot] = r
            place = jnp.int32(-1)
            offset = 0
            for i, size in enumerate(sizes):
                local = slot - kv_bases[i]
                place = jnp.where((local >= 0) & (local < size), local + offset, place)
                offset += size
            n = amount[r]

            @pl.when(place >= 0)
            def _():
                listed[r, n] = place
                amount[r] = n + 1

            return carry

        lax.fori_loop(0, slots, fill, 0)
        for copy in copies:
            copy.wait()

    slot = q_bases[step // q_per_piece] + step % q_per_piece
    r = page_req[slot]
    n = amount[r]
    blocks = (n + group - 1) // group
    q = q_ref[...]
    lane = lax.broadcasted_iota(jnp.int32, (PAGE, PAIR), 1)
    zero = jnp.zeros_like(q)
    both = jnp.concatenate(
        [jnp.where(lane < HEAD_DIM, q, zero), jnp.where(lane < HEAD_DIM, zero, q)], axis=0
    )
    rows = 2 * PAGE

    def pages_of(j, low):
        parts = []
        for i in range(group):
            at = pl.multiple_of(listed[r, j * group + i] * PAGE, PAGE)
            parts.append(kv[pl.ds(at, PAGE), low : low + PAIR])
        return jnp.concatenate(parts, axis=0)

    def score(j, top):
        s = lax.dot_general(
            both, pages_of(j, 0), (((1,), (1,)), ((), ())), preferred_element_type=jnp.float32
        )
        for i in range(group):
            piece = s[:, i * PAGE : (i + 1) * PAGE]
            piece = jnp.where(j * group + i < n, piece, NEG)
            scores[j, :, i * PAGE : (i + 1) * PAGE] = piece
            top = jnp.maximum(top, piece)
        return top

    top = lax.fori_loop(0, blocks, score, jnp.full((rows, PAGE), NEG, jnp.float32))
    peak = jnp.max(top, axis=1, keepdims=True)
    if not first:
        old_peak = stat_in[:, 0:1]
        peak = jnp.maximum(peak, old_peak)
    shift = peak * EXP_SCALE

    def weigh(j, carry):
        total, acc = carry
        w = jnp.exp2(scores[j] * EXP_SCALE - shift)
        for i in range(group):
            total = total + w[:, i * PAGE : (i + 1) * PAGE]
        acc = acc + jnp.dot(
            w.astype(jnp.bfloat16), pages_of(j, PAIR), preferred_element_type=jnp.float32
        )
        return total, acc

    total, acc = lax.fori_loop(
        0, blocks, weigh,
        (jnp.zeros((rows, PAGE), jnp.float32), jnp.zeros((rows, PAIR), jnp.float32)),
    )
    total = jnp.sum(total, axis=1, keepdims=True)
    if not first:
        shrink = jnp.exp2((old_peak - peak) * EXP_SCALE)
        total = total + stat_in[:, 1:2] * shrink
        acc = acc + acc_in[...] * shrink
    if last:
        acc = acc / total
        out_ref[...] = jnp.where(lane < HEAD_DIM, acc[:PAGE], acc[PAGE:]).astype(jnp.bfloat16)
    else:
        acc_out[...] = acc
        wide = lax.broadcasted_iota(jnp.int32, (rows, PAGE), 1)
        stat_out[...] = jnp.where(wide == 0, peak, total)


def attend(counts, table, q_bases, kv_bases, q, pieces, state, last, q_per_piece):
    tok = q.shape[0]
    sizes = tuple(p.shape[0] // PAGE for p in pieces)
    first = state is None
    group = 4
    slots = table.shape[0]
    requests = counts.shape[0]
    rows = lambda i, *_: (i, 0)
    most = min(sum(sizes), slots)
    state_specs = [pl.BlockSpec((2 * PAGE, PAIR), rows), pl.BlockSpec((2 * PAGE, PAGE), rows)]
    state_shape = [
        jax.ShapeDtypeStruct((2 * tok, PAIR), jnp.float32),
        jax.ShapeDtypeStruct((2 * tok, PAGE), jnp.float32),
    ]
    flops = 2 * tok * sum(sizes) * PAGE * PAIR
    out = pl.pallas_call(
        functools.partial(
            attend_kernel,
            requests=requests, slots=slots, q_per_piece=q_per_piece, sizes=sizes,
            first=first, last=last, group=group,
        ),
        grid_spec=pltpu.PrefetchScalarGridSpec(
            num_scalar_prefetch=4,
            grid=(tok // PAGE,),
            in_specs=[pl.BlockSpec((PAGE, PAIR), rows)]
            + [pl.BlockSpec(memory_space=pl.ANY)] * len(pieces)
            + ([] if first else state_specs),
            out_specs=[pl.BlockSpec((PAGE, PAIR), rows)] if last else state_specs,
            scratch_shapes=[
                pltpu.VMEM((sum(sizes) * PAGE, 2 * PAIR), jnp.bfloat16),
                pltpu.VMEM(((most + group - 1) // group, 2 * PAGE, group * PAGE), jnp.float32),
                pltpu.SMEM((requests, sum(sizes) + group), jnp.int32),
                pltpu.SMEM((requests,), jnp.int32),
                pltpu.SMEM((slots,), jnp.int32),
                pltpu.SemaphoreType.DMA((len(pieces),)),
            ],
        ),
        out_shape=[jax.ShapeDtypeStruct((tok, PAIR), jnp.bfloat16)] if last else state_shape,
        compiler_params=params(),
        cost_estimate=pl.CostEstimate(
            flops=flops, bytes_accessed=4 * tok * PAIR + 4 * PAGE * PAIR * sum(sizes),
            transcendentals=tok * sum(sizes) * PAGE,
        ),
        name="attend",
    )(counts, table, q_bases, kv_bases, q, *pieces, *([] if first else state))
    return out[0] if last else out


def mix_kernel(x_ref, ctx_ref, wo_ref, gain_ref, bias_ref, out_ref):
    mixed = x_ref[...].astype(jnp.float32)
    for j in range(ctx_ref.shape[0]):
        mixed = mixed + jnp.dot(ctx_ref[j], wo_ref[j], preferred_element_type=jnp.float32)
    out_ref[...] = normalize(mixed, gain_ref[...], bias_ref[...]).astype(jnp.bfloat16)


def mix(x, ctx, wo, gain, bias):
    tok, width = x.shape
    groups, _, cols = ctx.shape
    block = 256
    rows = lambda i: (i, 0)
    return pl.pallas_call(
        mix_kernel,
        grid=(tok // block,),
        in_specs=[
            pl.BlockSpec((block, width), rows),
            pl.BlockSpec((groups, block, cols), lambda i: (0, i, 0)),
            pl.BlockSpec(wo.shape, lambda i: (0, 0, 0)),
            pl.BlockSpec((1, width), lambda i: (0, 0)),
            pl.BlockSpec((1, width), lambda i: (0, 0)),
        ],
        out_specs=pl.BlockSpec((block, width), rows),
        out_shape=jax.ShapeDtypeStruct((tok, width), jnp.bfloat16),
        compiler_params=params(),
        cost_estimate=pl.CostEstimate(
            flops=2 * tok * width * groups * cols, bytes_accessed=8 * tok * width, transcendentals=0
        ),
        name="mix",
    )(x, ctx, wo, gain[None], bias[None])


def layer_norm(values, gain_row, bias_row):
    return normalize(values, gain_row, bias_row)


def local(
    tokens,
    query_key_value_weight,
    adapter_down_weight,
    adapter_up_weight,
    attention_out_weight,
    first_norm_gain,
    first_norm_bias,
    first_feed_weight,
    first_feed_bias,
    second_feed_weight,
    second_feed_bias,
    second_norm_gain,
    second_norm_bias,
    following_qkv_weight,
    following_bias,
    request_page_count,
    page_slot_table,
    request_adapter,
):
    tok_rows, width = tokens.shape
    dp_count = lax.axis_size("dp")
    mp_count = lax.axis_size("mp")
    dp_index = lax.axis_index("dp")
    mp_index = lax.axis_index("mp")
    kept_values = adapter_down_weight.shape[1] // ADAPTER_RANK
    heads_dev = query_key_value_weight.shape[1] // (3 * HEAD_DIM)
    pages = tok_rows // PAGE
    shared = dp_count == 8 and heads_dev == 4

    owners = request_adapter // kept_values
    level = jnp.sum(jnp.where(owners == mp_index, request_adapter % kept_values, 0))
    down = lax.dynamic_slice_in_dim(
        adapter_down_weight, level * ADAPTER_RANK, ADAPTER_RANK, 1
    )
    up = lax.dynamic_slice_in_dim(adapter_up_weight, level * ADAPTER_RANK, ADAPTER_RANK, 0)
    up_cols = up.shape[1] // mp_count
    sent = jnp.concatenate(
        [
            jnp.broadcast_to(down.T[:, None, :], (ADAPTER_RANK, mp_count, width)),
            up.reshape(ADAPTER_RANK, mp_count, up_cols),
        ],
        axis=2,
    ).reshape(ADAPTER_RANK, mp_count * (width + up_cols))
    got = lax.all_to_all(sent, "mp", split_axis=1, concat_axis=0, tiled=True)
    downs = got[:, :width].T
    ups = got[:, width:]

    def by_kind(matrix):
        split = matrix.reshape(matrix.shape[0], heads_dev, 3, HEAD_DIM)
        if shared:
            split = lax.dynamic_slice_in_dim(split, (dp_index % 2) * 2, 2, 1)
        return jnp.swapaxes(split, 1, 2).reshape(matrix.shape[0], -1)

    weight = by_kind(query_key_value_weight)
    ups = by_kind(ups)
    if shared:
        swap = [(i, i ^ 1) for i in range(8)]
        across = [(i, i ^ 2) for i in range(8)]
        along = [(i, i ^ 4) for i in range(8)]
        move = lambda value, pairs: lax.ppermute(value, "dp", pairs)
        x = jnp.concatenate([tokens, move(tokens, swap)], axis=0)
        at = lambda flip: (dp_index ^ flip) * pages
        bases = jnp.stack([at(0), at(1)])
    else:
        x = tokens
        bases = jnp.stack([dp_index * pages])
    args = (request_page_count, page_slot_table)
    q, kv = project(*args, owners, bases, x, weight, downs, ups, pages)
    if shared:
        kv_x = move(kv, across)
        kv_y = move(kv, along)
        kv_d0 = move(kv_y[:tok_rows], across)
        kv_d1 = move(kv_x[tok_rows:], along)
        step = functools.partial(attend, *args, bases)
        state = step(
            bases, q, [kv[:tok_rows], kv[tok_rows:]], None, False, pages
        )
        near = jnp.stack([at(2), at(3), at(4), at(5)])
        state = step(
            near, q, [kv_x[:tok_rows], kv_x[tok_rows:], kv_y[:tok_rows], kv_y[tok_rows:]],
            state, False, pages,
        )
        far = jnp.stack([at(6), at(7)])
        context = step(far, q, [kv_d0, kv_d1], state, True, pages)
        mine, theirs = context[:tok_rows], move(context[tok_rows:], swap)
        even = dp_index % 2 == 0
        context = jnp.concatenate(
            [jnp.where(even, mine, theirs), jnp.where(even, theirs, mine)], axis=1
        )
    else:
        everything = lax.all_gather(kv, "dp", axis=0, tiled=True)
        context = attend(
            *args, bases, jnp.zeros((1,), jnp.int32), q, [everything], None, True, pages
        )
    out_weight = lax.all_gather(attention_out_weight, "mp", axis=0)
    contexts = lax.all_gather(context, "mp", axis=0)
    normed = mix(tokens, contexts, out_weight, first_norm_gain, first_norm_bias)
    share_rows = tok_rows // mp_count
    row_base = mp_index * share_rows
    hidden = jax.nn.gelu(
        jnp.dot(normed, first_feed_weight, preferred_element_type=jnp.float32) + first_feed_bias,
        approximate=False,
    ).astype(jnp.bfloat16)
    feed = lax.psum(
        jnp.dot(hidden, second_feed_weight, preferred_element_type=jnp.float32).astype(
            jnp.bfloat16
        ),
        "mp",
    ).astype(jnp.float32)
    layer_full = layer_norm(
        normed.astype(jnp.float32) + feed + second_feed_bias, second_norm_gain, second_norm_bias
    ).astype(jnp.bfloat16)
    next_proj = (
        jnp.dot(layer_full, following_qkv_weight, preferred_element_type=jnp.float32)
        + following_bias
    ).astype(jnp.bfloat16)
    layer_rows = lax.dynamic_slice_in_dim(layer_full, row_base, share_rows, 0)
    return (layer_rows, next_proj)


def solution(mesh):
    placed = (
        P("dp", None),
        P(None, "mp"),
        P(None, "mp"),
        P("mp", None),
        P("mp", None),
        P(),
        P(),
        P(None, "mp"),
        P("mp"),
        P("mp", None),
        P(),
        P(),
        P(),
        P(None, "mp"),
        P("mp"),
        P(),
        P(),
        P(),
    )
    return jax.shard_map(
        local,
        mesh=mesh,
        in_specs=placed,
        out_specs=(P(("dp", "mp"), None), P("dp", "mp")),
        check_vma=False,
    )
```

```python
import functools
import math

import jax
import jax.numpy as jnp
from jax import lax
from jax.experimental import pallas as pl
from jax.experimental.pallas import tpu as pltpu
from jax.sharding import PartitionSpec as P

HEAD_DIM = 64
ADAPTER_RANK = 16
PAGE = 128
PAIR = 2 * HEAD_DIM
NEG = -1e30
EXP_SCALE = math.log2(math.e) * HEAD_DIM**-0.5
MIB = 1 << 20


def params(vmem=48):
    return pltpu.CompilerParams(
        dimension_semantics=("arbitrary",), vmem_limit_bytes=vmem * MIB
    )


def request_of(k, counts, requests):
    end = counts[0]
    request = (k >= end).astype(jnp.int32)
    for r in range(1, requests - 1):
        end = end + counts[r]
        request = request + (k >= end).astype(jnp.int32)
    return request


def normalize(values, gain_row, bias_row):
    average = jnp.mean(values, axis=-1, keepdims=True)
    centered = values - average
    variance = jnp.mean(centered * centered, axis=-1, keepdims=True)
    return centered * lax.rsqrt(variance + 1e-05) * gain_row + bias_row


def project_kernel(
    counts, table, owners, bases, *refs, requests, slots, pages, per_piece, parts,
):
    x_refs = refs[:parts]
    w_ref, down_ref, up_ref, q_ref, kv_ref, joined, page_owner = refs[parts:]
    step = pl.program_id(0)
    cols = w_ref.shape[1]

    @pl.when(step == 0)
    def _():
        joined[:, :cols] = w_ref[...]
        joined[:, cols:] = down_ref[...]

        def fill(k, carry):
            page_owner[table[k]] = owners[request_of(k, counts, requests)]
            return carry

        lax.fori_loop(0, slots, fill, 0)

    piece = step * pages // per_piece

    def block(x_ref):
        both = jnp.dot(x_ref[...], joined[...], preferred_element_type=jnp.float32)
        low = both[:, cols:]
        lane_owner = lax.broadcasted_iota(jnp.int32, (PAGE, low.shape[1]), 1) // ADAPTER_RANK
        kept = []
        for p in range(pages):
            page = step * pages + p
            slot = bases[page // per_piece] + page % per_piece
            kept.append(
                jnp.where(lane_owner == page_owner[slot], low[p * PAGE : (p + 1) * PAGE], 0.0)
            )
        low_rank = jnp.concatenate(kept, axis=0).astype(jnp.bfloat16)
        rows = both[:, :cols] + jnp.dot(
            low_rank, up_ref[...], preferred_element_type=jnp.float32
        )
        rows = rows.astype(jnp.bfloat16)
        q_cols = q_ref.shape[1]
        q_ref[...] = rows[:, :q_cols]
        kv_ref[...] = rows[:, q_cols:]

    for i in range(parts):
        pl.when(piece == i)(functools.partial(block, x_refs[i]))


def project(counts, table, owners, bases, xs, weight, down, up, per_piece):
    tok, width = xs[0].shape
    cols = weight.shape[1]
    pages = 2
    rows_step = pages * PAGE
    slots = table.shape[0]
    parts = len(xs)
    each = tok // rows_step
    total = tok * parts
    whole = lambda i, *_: (0, 0)
    rows = lambda i, *_: (i, 0)

    def own(part):
        return lambda i, *_: (jnp.clip(i - part * each, 0, each - 1), 0)

    return pl.pallas_call(
        functools.partial(
            project_kernel,
            requests=counts.shape[0], slots=slots, pages=pages, per_piece=per_piece, parts=parts,
        ),
        grid_spec=pltpu.PrefetchScalarGridSpec(
            num_scalar_prefetch=4,
            grid=(total // rows_step,),
            in_specs=[pl.BlockSpec((rows_step, width), own(i)) for i in range(parts)]
            + [
                pl.BlockSpec(weight.shape, whole),
                pl.BlockSpec(down.shape, whole),
                pl.BlockSpec(up.shape, whole),
            ],
            out_specs=[
                pl.BlockSpec((rows_step, cols // 3), rows),
                pl.BlockSpec((rows_step, 2 * cols // 3), rows),
            ],
            scratch_shapes=[
                pltpu.VMEM((width, cols + down.shape[1]), jnp.bfloat16),
                pltpu.SMEM((slots,), jnp.int32),
            ],
        ),
        out_shape=[
            jax.ShapeDtypeStruct((total, cols // 3), jnp.bfloat16),
            jax.ShapeDtypeStruct((total, 2 * cols // 3), jnp.bfloat16),
        ],
        compiler_params=params(),
        cost_estimate=pl.CostEstimate(
            flops=2 * total * width * cols, bytes_accessed=2 * total * (width + cols),
            transcendentals=0,
        ),
        name="project",
    )(counts, table, owners, bases, *xs, weight, down, up)


def attend_kernel(
    counts, table, q_bases, kv_bases, q_ref, *refs,
    requests, slots, q_size, sizes, first, last, group,
):
    refs = list(refs)
    kv_hbm = [refs.pop(0) for _ in sizes]
    if not first:
        acc_in, stat_in = refs.pop(0), refs.pop(0)
    if last:
        out_ref = refs.pop(0)
    else:
        acc_out, stat_out = refs.pop(0), refs.pop(0)
    kv, scores, listed, amount, asked, q_amount, sems = refs
    copies = []
    offset = 0
    for i, size in enumerate(sizes):
        copy = pltpu.make_async_copy(
            kv_hbm[i], kv.at[pl.ds(offset * PAGE, size * PAGE)], sems.at[i]
        )
        copy.start()
        copies.append(copy)
        offset += size
    for r in range(requests):
        amount[r] = 0
        q_amount[r] = 0

    def place_of(slot, bases, extents):
        place = jnp.int32(-1)
        offset = 0
        for i, size in enumerate(extents):
            near = slot - bases[i]
            place = jnp.where((near >= 0) & (near < size), near + offset, place)
            offset += size
        return place

    q_sizes = (q_size,) * (q_ref.shape[0] // (q_size * PAGE))

    def fill(k, carry):
        r = request_of(k, counts, requests)
        slot = table[k]
        place = place_of(slot, kv_bases, sizes)
        q_place = place_of(slot, q_bases, q_sizes)

        @pl.when(place >= 0)
        def _():
            n = amount[r]
            listed[r, n] = place
            amount[r] = n + 1

        @pl.when(q_place >= 0)
        def _():
            n = q_amount[r]
            asked[r, n] = q_place
            q_amount[r] = n + 1

        return carry

    lax.fori_loop(0, slots, fill, 0)
    for copy in copies:
        copy.wait()
    lane = lax.broadcasted_iota(jnp.int32, (PAGE, PAIR), 1)
    low_lane = lane < HEAD_DIM
    rows = 4 * PAGE

    def one_pair(r, p):
        n = amount[r]
        full = n // group
        blocks = (n + group - 1) // group
        count = q_amount[r]
        a = asked[r, 2 * p]
        b = asked[r, jnp.minimum(2 * p + 1, count - 1)]
        spots = [pl.ds(pl.multiple_of(t * PAGE, PAGE), PAGE) for t in (a, b)]
        parts = []
        for spot in spots:
            q = q_ref[spot, :]
            zero = jnp.zeros_like(q)
            parts += [jnp.where(low_lane, q, zero), jnp.where(low_lane, zero, q)]
        stacked = jnp.concatenate(parts, axis=0)

        def pages_of(j, low):
            found = []
            for i in range(group):
                index = jnp.minimum(j * group + i, n - 1)
                at = pl.multiple_of(listed[r, index] * PAGE, PAGE)
                found.append(kv[pl.ds(at, PAGE), low : low + PAIR])
            return jnp.concatenate(found, axis=0)

        def score(masked, j, top):
            s = lax.dot_general(
                stacked, pages_of(j, 0), (((1,), (1,)), ((), ())),
                preferred_element_type=jnp.float32,
            )
            for i in range(group):
                piece = s[:, i * PAGE : (i + 1) * PAGE]
                if masked and i:
                    piece = jnp.where(j * group + i < n, piece, NEG)
                scores[j, :, i * PAGE : (i + 1) * PAGE] = piece
                top = jnp.maximum(top, piece)
            return top

        top = jnp.full((rows, PAGE), NEG, jnp.float32)
        top = lax.fori_loop(0, full, functools.partial(score, False), top)
        top = lax.fori_loop(full, blocks, functools.partial(score, True), top)
        peak = jnp.max(top, axis=1, keepdims=True)
        if not first:
            old = jnp.concatenate(
                [stat_in[spot, h : h + 1] for spot in spots for h in (0, 1)], axis=0
            )
            peak = jnp.maximum(peak, old)
        shift = peak * EXP_SCALE

        def weigh(j, carry):
            total, acc = carry
            w = jnp.exp2(scores[j] * EXP_SCALE - shift)
            for i in range(group):
                total = total + w[:, i * PAGE : (i + 1) * PAGE]
            acc = acc + jnp.dot(
                w.astype(jnp.bfloat16), pages_of(j, PAIR), preferred_element_type=jnp.float32
            )
            return total, acc

        total, acc = lax.fori_loop(
            0, blocks, weigh,
            (jnp.zeros((rows, PAGE), jnp.float32), jnp.zeros((rows, PAIR), jnp.float32)),
        )
        total = jnp.sum(total, axis=1, keepdims=True)
        if not first:
            shrink = jnp.exp2((old - peak) * EXP_SCALE)
            total = total + shrink * jnp.concatenate(
                [stat_in[spot, h : h + 1] for spot in spots for h in (2, 3)], axis=0
            )
        for t, spot in enumerate(spots):
            h0 = slice(2 * t * PAGE, (2 * t + 1) * PAGE)
            h1 = slice((2 * t + 1) * PAGE, (2 * t + 2) * PAGE)
            value = jnp.where(low_lane, acc[h0], acc[h1])
            if not first:
                value = value + acc_in[spot, :] * jnp.where(low_lane, shrink[h0], shrink[h1])
            if last:
                value = value / jnp.where(low_lane, total[h0], total[h1])
                out_ref[spot, :] = value.astype(jnp.bfloat16)
            else:
                acc_out[spot, :] = value
                stat = jnp.where(lane == 0, peak[h0], peak[h1])
                stat = jnp.where(lane == 2, total[h0], stat)
                stat_out[spot, :] = jnp.where(lane == 3, total[h1], stat)

    def visit_request(r, carry):
        def visit(p, inner):
            one_pair(r, p)
            return inner

        return lax.fori_loop(0, (q_amount[r] + 1) // 2, visit, carry)

    lax.fori_loop(0, requests, visit_request, 0)


def attend(counts, table, q_bases, kv_bases, q, pieces, state, last, q_size):
    tok = q.shape[0]
    sizes = tuple(p.shape[0] // PAGE for p in pieces)
    first = state is None
    group = 4
    slots = table.shape[0]
    requests = counts.shape[0]
    most = min(sum(sizes), slots)
    vmem = pl.BlockSpec(memory_space=pltpu.VMEM)
    state_shape = [jax.ShapeDtypeStruct((tok, PAIR), jnp.float32)] * 2
    out = pl.pallas_call(
        functools.partial(
            attend_kernel,
            requests=requests, slots=slots, q_size=q_size, sizes=sizes,
            first=first, last=last, group=group,
        ),
        grid_spec=pltpu.PrefetchScalarGridSpec(
            num_scalar_prefetch=4,
            grid=(1,),
            in_specs=[pl.BlockSpec((tok, PAIR), lambda i, *_: (0, 0))]
            + [pl.BlockSpec(memory_space=pl.ANY)] * len(pieces)
            + ([] if first else [pl.BlockSpec((tok, PAIR), lambda i, *_: (0, 0))] * 2),
            out_specs=[pl.BlockSpec((tok, PAIR), lambda i, *_: (0, 0))] * (1 if last else 2),
            scratch_shapes=[
                pltpu.VMEM((sum(sizes) * PAGE, 2 * PAIR), jnp.bfloat16),
                pltpu.VMEM(((most + group - 1) // group, 4 * PAGE, group * PAGE), jnp.float32),
                pltpu.SMEM((requests, sum(sizes)), jnp.int32),
                pltpu.SMEM((requests,), jnp.int32),
                pltpu.SMEM((requests, tok // PAGE), jnp.int32),
                pltpu.SMEM((requests,), jnp.int32),
                pltpu.SemaphoreType.DMA((len(pieces),)),
            ],
        ),
        out_shape=[jax.ShapeDtypeStruct((tok, PAIR), jnp.bfloat16)] if last else state_shape,
        compiler_params=params(),
        cost_estimate=pl.CostEstimate(
            flops=2 * tok * sum(sizes) * PAGE * PAIR,
            bytes_accessed=4 * tok * PAIR + 4 * PAGE * PAIR * sum(sizes),
            transcendentals=tok * sum(sizes) * PAGE,
        ),
        name="attend",
    )(counts, table, q_bases, kv_bases, q, *pieces, *([] if first else state))
    return out[0] if last else out


def mix_kernel(x_ref, ctx_ref, wo_ref, gain_ref, bias_ref, out_ref):
    mixed = x_ref[...].astype(jnp.float32)
    for j in range(ctx_ref.shape[0]):
        mixed = mixed + jnp.dot(ctx_ref[j], wo_ref[j], preferred_element_type=jnp.float32)
    out_ref[...] = normalize(mixed, gain_ref[...], bias_ref[...]).astype(jnp.bfloat16)


def mix(x, ctx, wo, gain, bias):
    tok, width = x.shape
    groups, _, cols = ctx.shape
    block = 256
    rows = lambda i: (i, 0)
    return pl.pallas_call(
        mix_kernel,
        grid=(tok // block,),
        in_specs=[
            pl.BlockSpec((block, width), rows),
            pl.BlockSpec((groups, block, cols), lambda i: (0, i, 0)),
            pl.BlockSpec(wo.shape, lambda i: (0, 0, 0)),
            pl.BlockSpec((1, width), lambda i: (0, 0)),
            pl.BlockSpec((1, width), lambda i: (0, 0)),
        ],
        out_specs=pl.BlockSpec((block, width), rows),
        out_shape=jax.ShapeDtypeStruct((tok, width), jnp.bfloat16),
        compiler_params=params(),
        cost_estimate=pl.CostEstimate(
            flops=2 * tok * width * groups * cols, bytes_accessed=8 * tok * width, transcendentals=0
        ),
        name="mix",
    )(x, ctx, wo, gain[None], bias[None])


def layer_norm(values, gain_row, bias_row):
    return normalize(values, gain_row, bias_row)


def local(
    tokens,
    query_key_value_weight,
    adapter_down_weight,
    adapter_up_weight,
    attention_out_weight,
    first_norm_gain,
    first_norm_bias,
    first_feed_weight,
    first_feed_bias,
    second_feed_weight,
    second_feed_bias,
    second_norm_gain,
    second_norm_bias,
    following_qkv_weight,
    following_bias,
    request_page_count,
    page_slot_table,
    request_adapter,
):
    tok_rows, width = tokens.shape
    dp_count = lax.axis_size("dp")
    mp_count = lax.axis_size("mp")
    dp_index = lax.axis_index("dp")
    mp_index = lax.axis_index("mp")
    kept_values = adapter_down_weight.shape[1] // ADAPTER_RANK
    heads_dev = query_key_value_weight.shape[1] // (3 * HEAD_DIM)
    pages = tok_rows // PAGE
    shared = dp_count == 8 and heads_dev == 4

    owners = request_adapter // kept_values
    level = jnp.sum(jnp.where(owners == mp_index, request_adapter % kept_values, 0))
    down = lax.dynamic_slice_in_dim(
        adapter_down_weight, level * ADAPTER_RANK, ADAPTER_RANK, 1
    )
    up = lax.dynamic_slice_in_dim(adapter_up_weight, level * ADAPTER_RANK, ADAPTER_RANK, 0)
    up_cols = up.shape[1] // mp_count
    sent = jnp.concatenate(
        [
            jnp.broadcast_to(down.T[:, None, :], (ADAPTER_RANK, mp_count, width)),
            up.reshape(ADAPTER_RANK, mp_count, up_cols),
        ],
        axis=2,
    ).reshape(ADAPTER_RANK, mp_count * (width + up_cols))
    got = lax.all_to_all(sent, "mp", split_axis=1, concat_axis=0, tiled=True)
    downs = got[:, :width].T
    ups = got[:, width:]

    def by_kind(matrix):
        split = matrix.reshape(matrix.shape[0], heads_dev, 3, HEAD_DIM)
        if shared:
            split = lax.dynamic_slice_in_dim(split, (dp_index % 2) * 2, 2, 1)
        return jnp.swapaxes(split, 1, 2).reshape(matrix.shape[0], -1)

    weight = by_kind(query_key_value_weight)
    ups = by_kind(ups)
    if shared:
        swap = [(i, i ^ 1) for i in range(8)]
        across = [(i, i ^ 2) for i in range(8)]
        along = [(i, i ^ 4) for i in range(8)]
        move = lambda value, pairs: lax.ppermute(value, "dp", pairs)
        xs = [tokens, move(tokens, swap)]
        at = lambda flip: (dp_index ^ flip) * pages
        bases = jnp.stack([at(0), at(1)])
    else:
        xs = [tokens]
        bases = jnp.stack([dp_index * pages])
    args = (request_page_count, page_slot_table)
    q, kv = project(*args, owners, bases, xs, weight, downs, ups, pages)
    if shared:
        kv_x = move(kv, across)
        kv_y = move(kv, along)
        step = functools.partial(attend, *args, bases)
        state = step(bases, q, [kv[:tok_rows], kv[tok_rows:]], None, False, pages)
        kv_x, kv_y, state = lax.optimization_barrier((kv_x, kv_y, state))
        kv_d0 = move(kv_y[:tok_rows], across)
        kv_d1 = move(kv_x[tok_rows:], along)
        near = jnp.stack([at(2), at(3), at(4), at(5)])
        state = step(
            near, q, [kv_x[:tok_rows], kv_x[tok_rows:], kv_y[:tok_rows], kv_y[tok_rows:]],
            state, False, pages,
        )
        far = jnp.stack([at(6), at(7)])
        context = step(far, q, [kv_d0, kv_d1], state, True, pages)
        mine, theirs = context[:tok_rows], move(context[tok_rows:], swap)
        even = dp_index % 2 == 0
        context = jnp.concatenate(
            [jnp.where(even, mine, theirs), jnp.where(even, theirs, mine)], axis=1
        )
    else:
        everything = lax.all_gather(kv, "dp", axis=0, tiled=True)
        context = attend(
            *args, bases, jnp.zeros((1,), jnp.int32), q, [everything], None, True, pages
        )
    out_weight = lax.all_gather(attention_out_weight, "mp", axis=0)
    contexts = lax.all_gather(context, "mp", axis=0)
    normed = mix(tokens, contexts, out_weight, first_norm_gain, first_norm_bias)
    share_rows = tok_rows // mp_count
    row_base = mp_index * share_rows
    hidden = jax.nn.gelu(
        jnp.dot(normed, first_feed_weight, preferred_element_type=jnp.float32) + first_feed_bias,
        approximate=False,
    ).astype(jnp.bfloat16)
    feed = lax.psum(
        jnp.dot(hidden, second_feed_weight, preferred_element_type=jnp.float32).astype(
            jnp.bfloat16
        ),
        "mp",
    ).astype(jnp.float32)
    layer_full = layer_norm(
        normed.astype(jnp.float32) + feed + second_feed_bias, second_norm_gain, second_norm_bias
    ).astype(jnp.bfloat16)
    next_proj = (
        jnp.dot(layer_full, following_qkv_weight, preferred_element_type=jnp.float32)
        + following_bias
    ).astype(jnp.bfloat16)
    layer_rows = lax.dynamic_slice_in_dim(layer_full, row_base, share_rows, 0)
    return (layer_rows, next_proj)


def solution(mesh):
    placed = (
        P("dp", None),
        P(None, "mp"),
        P(None, "mp"),
        P("mp", None),
        P("mp", None),
        P(),
        P(),
        P(None, "mp"),
        P("mp"),
        P("mp", None),
        P(),
        P(),
        P(),
        P(None, "mp"),
        P("mp"),
        P(),
        P(),
        P(),
    )
    return jax.shard_map(
        local,
        mesh=mesh,
        in_specs=placed,
        out_specs=(P(("dp", "mp"), None), P("dp", "mp")),
        check_vma=False,
    )
```

```python
import functools
import math

import jax
import jax.numpy as jnp
from jax import lax
from jax.experimental import pallas as pl
from jax.experimental.pallas import tpu as pltpu
from jax.sharding import PartitionSpec as P

HEAD_DIM = 64
ADAPTER_RANK = 16
PAGE = 128
PAIR = 2 * HEAD_DIM
NEG = -1e30
EXP_SCALE = math.log2(math.e) * HEAD_DIM**-0.5
MIB = 1 << 20


def params(vmem=48):
    return pltpu.CompilerParams(
        dimension_semantics=("arbitrary",), vmem_limit_bytes=vmem * MIB
    )


def request_of(k, counts, requests):
    end = counts[0]
    request = (k >= end).astype(jnp.int32)
    for r in range(1, requests - 1):
        end = end + counts[r]
        request = request + (k >= end).astype(jnp.int32)
    return request


def normalize(values, gain_row, bias_row):
    average = jnp.mean(values, axis=-1, keepdims=True)
    centered = values - average
    variance = jnp.mean(centered * centered, axis=-1, keepdims=True)
    return centered * lax.rsqrt(variance + 1e-05) * gain_row + bias_row


def project_kernel(
    counts, table, owners, bases, *refs, requests, slots, pages, per_piece, parts,
):
    x_refs = refs[:parts]
    w_ref, down_ref, up_ref, q_ref, kv_ref, joined, page_owner = refs[parts:]
    step = pl.program_id(0)
    cols = w_ref.shape[1]

    @pl.when(step == 0)
    def _():
        joined[:, :cols] = w_ref[...]
        joined[:, cols:] = down_ref[...]

        def fill(k, carry):
            page_owner[table[k]] = owners[request_of(k, counts, requests)]
            return carry

        lax.fori_loop(0, slots, fill, 0)

    piece = step * pages // per_piece

    def block(x_ref):
        both = jnp.dot(x_ref[...], joined[...], preferred_element_type=jnp.float32)
        low = both[:, cols:]
        lane_owner = lax.broadcasted_iota(jnp.int32, (PAGE, low.shape[1]), 1) // ADAPTER_RANK
        kept = []
        for p in range(pages):
            page = step * pages + p
            slot = bases[page // per_piece] + page % per_piece
            kept.append(
                jnp.where(lane_owner == page_owner[slot], low[p * PAGE : (p + 1) * PAGE], 0.0)
            )
        low_rank = jnp.concatenate(kept, axis=0).astype(jnp.bfloat16)
        rows = both[:, :cols] + jnp.dot(
            low_rank, up_ref[...], preferred_element_type=jnp.float32
        )
        rows = rows.astype(jnp.bfloat16)
        q_cols = q_ref.shape[1]
        q_ref[...] = rows[:, :q_cols]
        kv_ref[...] = rows[:, q_cols:]

    for i in range(parts):
        pl.when(piece == i)(functools.partial(block, x_refs[i]))


def project(counts, table, owners, bases, xs, weight, down, up, per_piece):
    tok, width = xs[0].shape
    cols = weight.shape[1]
    pages = 2
    rows_step = pages * PAGE
    slots = table.shape[0]
    parts = len(xs)
    each = tok // rows_step
    total = tok * parts
    whole = lambda i, *_: (0, 0)
    rows = lambda i, *_: (i, 0)

    def own(part):
        return lambda i, *_: (jnp.clip(i - part * each, 0, each - 1), 0)

    return pl.pallas_call(
        functools.partial(
            project_kernel,
            requests=counts.shape[0], slots=slots, pages=pages, per_piece=per_piece, parts=parts,
        ),
        grid_spec=pltpu.PrefetchScalarGridSpec(
            num_scalar_prefetch=4,
            grid=(total // rows_step,),
            in_specs=[pl.BlockSpec((rows_step, width), own(i)) for i in range(parts)]
            + [
                pl.BlockSpec(weight.shape, whole),
                pl.BlockSpec(down.shape, whole),
                pl.BlockSpec(up.shape, whole),
            ],
            out_specs=[
                pl.BlockSpec((rows_step, cols // 3), rows),
                pl.BlockSpec((rows_step, 2 * cols // 3), rows),
            ],
            scratch_shapes=[
                pltpu.VMEM((width, cols + down.shape[1]), jnp.bfloat16),
                pltpu.SMEM((slots,), jnp.int32),
            ],
        ),
        out_shape=[
            jax.ShapeDtypeStruct((total, cols // 3), jnp.bfloat16),
            jax.ShapeDtypeStruct((total, 2 * cols // 3), jnp.bfloat16),
        ],
        compiler_params=params(),
        cost_estimate=pl.CostEstimate(
            flops=2 * total * width * cols, bytes_accessed=2 * total * (width + cols),
            transcendentals=0,
        ),
        name="project",
    )(counts, table, owners, bases, *xs, weight, down, up)


def attend_kernel(
    counts, table, q_bases, kv_bases, q_ref, *refs,
    requests, slots, q_size, sizes, first, last, group,
):
    refs = list(refs)
    kv_hbm = [refs.pop(0) for _ in sizes]
    if not first:
        acc_in, stat_in = refs.pop(0), refs.pop(0)
    if last:
        out_ref = refs.pop(0)
    else:
        acc_out, stat_out = refs.pop(0), refs.pop(0)
    kv, scores, listed, amount, asked, q_amount, sems = refs
    copies = []
    offset = 0
    for i, size in enumerate(sizes):
        copy = pltpu.make_async_copy(
            kv_hbm[i], kv.at[pl.ds(offset * PAGE, size * PAGE)], sems.at[i]
        )
        copy.start()
        copies.append(copy)
        offset += size
    for r in range(requests):
        amount[r] = 0
        q_amount[r] = 0

    def place_of(slot, bases, extents):
        place = jnp.int32(-1)
        offset = 0
        for i, size in enumerate(extents):
            near = slot - bases[i]
            place = jnp.where((near >= 0) & (near < size), near + offset, place)
            offset += size
        return place

    q_sizes = (q_size,) * (q_ref.shape[0] // (q_size * PAGE))

    def fill(k, carry):
        r = request_of(k, counts, requests)
        slot = table[k]
        place = place_of(slot, kv_bases, sizes)
        q_place = place_of(slot, q_bases, q_sizes)

        @pl.when(place >= 0)
        def _():
            n = amount[r]
            listed[r, n] = place
            amount[r] = n + 1

        @pl.when(q_place >= 0)
        def _():
            n = q_amount[r]
            asked[r, n] = q_place
            q_amount[r] = n + 1

        return carry

    lax.fori_loop(0, slots, fill, 0)
    for copy in copies:
        copy.wait()
    lane = lax.broadcasted_iota(jnp.int32, (PAGE, PAIR), 1)
    low_lane = lane < HEAD_DIM
    rows = 4 * PAGE

    def one_pair(r, p):
        n = amount[r]
        full = n // group
        blocks = (n + group - 1) // group
        count = q_amount[r]
        a = asked[r, 2 * p]
        b = asked[r, jnp.minimum(2 * p + 1, count - 1)]
        spots = [pl.ds(pl.multiple_of(t * PAGE, PAGE), PAGE) for t in (a, b)]
        parts = []
        for spot in spots:
            q = q_ref[spot, :]
            zero = jnp.zeros_like(q)
            parts += [jnp.where(low_lane, q, zero), jnp.where(low_lane, zero, q)]
        stacked = jnp.concatenate(parts, axis=0)

        def pages_of(j, low):
            found = []
            for i in range(group):
                index = jnp.minimum(j * group + i, n - 1)
                at = pl.multiple_of(listed[r, index] * PAGE, PAGE)
                found.append(kv[pl.ds(at, PAGE), low : low + PAIR])
            return jnp.concatenate(found, axis=0)

        def score(masked, j, top):
            s = lax.dot_general(
                stacked, pages_of(j, 0), (((1,), (1,)), ((), ())),
                preferred_element_type=jnp.float32,
            )
            for i in range(group):
                piece = s[:, i * PAGE : (i + 1) * PAGE]
                if masked and i:
                    piece = jnp.where(j * group + i < n, piece, NEG)
                scores[j, :, i * PAGE : (i + 1) * PAGE] = piece
                top = jnp.maximum(top, piece)
            return top

        top = jnp.full((rows, PAGE), NEG, jnp.float32)
        top = lax.fori_loop(0, full, functools.partial(score, False), top)
        top = lax.fori_loop(full, blocks, functools.partial(score, True), top)
        peak = jnp.max(top, axis=1, keepdims=True)
        if not first:
            old = jnp.concatenate(
                [stat_in[spot, h : h + 1] for spot in spots for h in (0, 1)], axis=0
            )
            peak = jnp.maximum(peak, old)
        shift = peak * EXP_SCALE

        def weigh(j, carry):
            total, acc = carry
            w = jnp.exp2(scores[j] * EXP_SCALE - shift)
            for i in range(group):
                total = total + w[:, i * PAGE : (i + 1) * PAGE]
            acc = acc + jnp.dot(
                w.astype(jnp.bfloat16), pages_of(j, PAIR), preferred_element_type=jnp.float32
            )
            return total, acc

        total, acc = lax.fori_loop(
            0, blocks, weigh,
            (jnp.zeros((rows, PAGE), jnp.float32), jnp.zeros((rows, PAIR), jnp.float32)),
        )
        total = jnp.sum(total, axis=1, keepdims=True)
        if not first:
            shrink = jnp.exp2((old - peak) * EXP_SCALE)
            total = total + shrink * jnp.concatenate(
                [stat_in[spot, h : h + 1] for spot in spots for h in (2, 3)], axis=0
            )
        for t, spot in enumerate(spots):
            h0 = slice(2 * t * PAGE, (2 * t + 1) * PAGE)
            h1 = slice((2 * t + 1) * PAGE, (2 * t + 2) * PAGE)
            value = jnp.where(low_lane, acc[h0], acc[h1])
            if not first:
                value = value + acc_in[spot, :] * jnp.where(low_lane, shrink[h0], shrink[h1])
            if last:
                value = value / jnp.where(low_lane, total[h0], total[h1])
                out_ref[spot, :] = value.astype(jnp.bfloat16)
            else:
                acc_out[spot, :] = value
                stat = jnp.where(lane == 0, peak[h0], peak[h1])
                stat = jnp.where(lane == 2, total[h0], stat)
                stat_out[spot, :] = jnp.where(lane == 3, total[h1], stat)

    def visit_request(r, carry):
        def visit(p, inner):
            one_pair(r, p)
            return inner

        return lax.fori_loop(0, (q_amount[r] + 1) // 2, visit, carry)

    lax.fori_loop(0, requests, visit_request, 0)


def attend(counts, table, q_bases, kv_bases, q, pieces, state, last, q_size):
    tok = q.shape[0]
    sizes = tuple(p.shape[0] // PAGE for p in pieces)
    first = state is None
    group = 4
    slots = table.shape[0]
    requests = counts.shape[0]
    most = min(sum(sizes), slots)
    vmem = pl.BlockSpec(memory_space=pltpu.VMEM)
    state_shape = [jax.ShapeDtypeStruct((tok, PAIR), jnp.float32)] * 2
    out = pl.pallas_call(
        functools.partial(
            attend_kernel,
            requests=requests, slots=slots, q_size=q_size, sizes=sizes,
            first=first, last=last, group=group,
        ),
        grid_spec=pltpu.PrefetchScalarGridSpec(
            num_scalar_prefetch=4,
            grid=(1,),
            in_specs=[pl.BlockSpec((tok, PAIR), lambda i, *_: (0, 0))]
            + [pl.BlockSpec(memory_space=pl.ANY)] * len(pieces)
            + ([] if first else [pl.BlockSpec((tok, PAIR), lambda i, *_: (0, 0))] * 2),
            out_specs=[pl.BlockSpec((tok, PAIR), lambda i, *_: (0, 0))] * (1 if last else 2),
            scratch_shapes=[
                pltpu.VMEM((sum(sizes) * PAGE, 2 * PAIR), jnp.bfloat16),
                pltpu.VMEM(((most + group - 1) // group, 4 * PAGE, group * PAGE), jnp.float32),
                pltpu.SMEM((requests, sum(sizes)), jnp.int32),
                pltpu.SMEM((requests,), jnp.int32),
                pltpu.SMEM((requests, tok // PAGE), jnp.int32),
                pltpu.SMEM((requests,), jnp.int32),
                pltpu.SemaphoreType.DMA((len(pieces),)),
            ],
        ),
        out_shape=[jax.ShapeDtypeStruct((tok, PAIR), jnp.bfloat16)] if last else state_shape,
        compiler_params=params(),
        cost_estimate=pl.CostEstimate(
            flops=2 * tok * sum(sizes) * PAGE * PAIR,
            bytes_accessed=4 * tok * PAIR + 4 * PAGE * PAIR * sum(sizes),
            transcendentals=tok * sum(sizes) * PAGE,
        ),
        name="attend",
    )(counts, table, q_bases, kv_bases, q, *pieces, *([] if first else state))
    return out[0] if last else out


def mix_kernel(bases, x_ref, ctx_ref, *refs, plan):
    count = len({index for index, *_ in plan})
    wo_refs = refs[:count]
    gain_ref, bias_ref, out_ref, wo, sems = refs[count:]

    @pl.when(pl.program_id(0) == 0)
    def _():
        copies = []
        for n, (index, row, rows, half, flip, extra) in enumerate(plan):
            near = wo.shape[1] // 2
            at = half * near + (bases[0] ^ flip) * (near // bases_of(plan)) + extra
            copy = pltpu.make_async_copy(
                wo_refs[index].at[:, pl.ds(row, rows), :],
                wo.at[:, pl.ds(pl.multiple_of(at, 16), rows), :],
                sems.at[n],
            )
            copy.start()
            copies.append(copy)
        for copy in copies:
            copy.wait()

    mixed = x_ref[...].astype(jnp.float32)
    for j in range(ctx_ref.shape[0]):
        mixed = mixed + jnp.dot(ctx_ref[j], wo[j], preferred_element_type=jnp.float32)
    out_ref[...] = normalize(mixed, gain_ref[...], bias_ref[...]).astype(jnp.bfloat16)


def bases_of(plan):
    return max(flip for *_, flip, _ in plan) + 1


def mix(place, x, ctx, wo_arrays, plan, gain, bias):
    tok, width = x.shape
    groups, _, cols = ctx.shape
    block = 256
    rows = lambda i, *_: (i, 0)
    fixed = lambda i, *_: (0, 0)
    return pl.pallas_call(
        functools.partial(mix_kernel, plan=plan),
        grid_spec=pltpu.PrefetchScalarGridSpec(
            num_scalar_prefetch=1,
            grid=(tok // block,),
            in_specs=[
                pl.BlockSpec((block, width), rows),
                pl.BlockSpec((groups, block, cols), lambda i, *_: (0, i, 0)),
            ]
            + [pl.BlockSpec(memory_space=pl.ANY)] * len(wo_arrays)
            + [pl.BlockSpec((1, width), fixed)] * 2,
            out_specs=pl.BlockSpec((block, width), rows),
            scratch_shapes=[
                pltpu.VMEM((groups, cols, width), jnp.bfloat16),
                pltpu.SemaphoreType.DMA((len(plan),)),
            ],
        ),
        out_shape=jax.ShapeDtypeStruct((tok, width), jnp.bfloat16),
        compiler_params=params(),
        cost_estimate=pl.CostEstimate(
            flops=2 * tok * width * groups * cols, bytes_accessed=8 * tok * width, transcendentals=0
        ),
        name="mix",
    )(place, x, ctx, *wo_arrays, gain[None], bias[None])


def feed_kernel(place, normed_ref, bias_ref, *refs, halves, shape, last_step):
    refs = list(refs)
    sets = []
    for _ in range(halves):
        w1 = refs.pop(0)
        sets.append((w1, [refs.pop(0) for _ in shape]))
    b2_ref, gain_ref, bias2_ref, next_w_ref, next_b_ref = refs[:5]
    layer_ref, next_ref, acc, done = refs[5:]
    step = pl.program_id(0)
    tok = normed_ref.shape[0]
    block = min(256, tok)
    groups = (last_step + 1) // halves

    @pl.when(step == 0)
    def _():
        acc[...] = jnp.zeros_like(acc)

    def absorb(w1_ref, w2_refs):
        w1 = w1_ref[0]
        w2 = jnp.concatenate(
            [ref[0][:rows] for ref, rows in zip(w2_refs, shape)], axis=0
        )
        for t in range(tok // block):
            rows = slice(t * block, (t + 1) * block)
            pre = jnp.dot(normed_ref[rows, :], w1, preferred_element_type=jnp.float32)
            pre = pre + bias_ref[0]
            hidden = 0.5 * pre * (1.0 + lax.erf(pre * math.sqrt(0.5)))
            acc[rows, :] += jnp.dot(
                hidden.astype(jnp.bfloat16), w2, preferred_element_type=jnp.float32
            )

    for h in range(halves):
        pl.when(step // groups == h)(functools.partial(absorb, *sets[h]))

    @pl.when(step == last_step)
    def _():
        for t in range(tok // block):
            rows = slice(t * block, (t + 1) * block)
            total = normed_ref[rows, :].astype(jnp.float32) + acc[rows, :] + b2_ref[...]
            layer = normalize(total, gain_ref[...], bias2_ref[...]).astype(jnp.bfloat16)
            done[rows, :] = layer
            next_ref[rows, :] = (
                jnp.dot(layer, next_w_ref[...], preferred_element_type=jnp.float32)
                + next_b_ref[...]
            ).astype(jnp.bfloat16)
        share = layer_ref.shape[0]
        layer_ref[...] = done[pl.ds(pl.multiple_of(place[0] * share, share), share), :]


def feed(place, normed, bias, sets, shape, b2, gain, bias2, next_w, next_b, share):
    tok, width = normed.shape
    halves = len(sets)
    groups, _, cols = sets[0][0].shape
    steps = halves * groups
    fixed = lambda i, *_: (0, 0)
    specs, arrays = [], []
    for h, (w1, w2s) in enumerate(sets):
        at = lambda i, *_, h=h: (jnp.clip(i - h * groups, 0, groups - 1), 0, 0)
        for array in (w1, *w2s):
            specs.append(pl.BlockSpec((1,) + array.shape[1:], at))
            arrays.append(array)
    next_cols = next_w.shape[1]
    return pl.pallas_call(
        functools.partial(feed_kernel, halves=halves, shape=shape, last_step=steps - 1),
        grid_spec=pltpu.PrefetchScalarGridSpec(
            num_scalar_prefetch=1,
            grid=(steps,),
            in_specs=[
                pl.BlockSpec((tok, width), fixed),
                pl.BlockSpec((1, 1, cols), lambda i, *_: (i, 0, 0)),
            ]
            + specs
            + [
                pl.BlockSpec((1, width), fixed),
                pl.BlockSpec((1, width), fixed),
                pl.BlockSpec((1, width), fixed),
                pl.BlockSpec((width, next_cols), fixed),
                pl.BlockSpec((1, next_cols), fixed),
            ],
            out_specs=[
                pl.BlockSpec((share, width), fixed),
                pl.BlockSpec((tok, next_cols), fixed),
            ],
            scratch_shapes=[
                pltpu.VMEM((tok, width), jnp.float32),
                pltpu.VMEM((tok, width), jnp.bfloat16),
            ],
        ),
        out_shape=[
            jax.ShapeDtypeStruct((share, width), jnp.bfloat16),
            jax.ShapeDtypeStruct((tok, next_cols), jnp.bfloat16),
        ],
        compiler_params=params(),
        cost_estimate=pl.CostEstimate(
            flops=4 * tok * width * cols * steps, bytes_accessed=4 * width * cols * steps,
            transcendentals=tok * cols * steps,
        ),
        name="feed",
    )(
        place, normed, bias, *arrays,
        b2[None], gain[None], bias2[None], next_w, next_b[None],
    )


def three_parts(values):
    high = lax.reduce_precision(values, 8, 7)
    middle = lax.reduce_precision(values - high, 8, 7)
    rest = values - high - middle
    return [part.astype(jnp.bfloat16) for part in (high, middle, rest)]


def local(
    tokens,
    query_key_value_weight,
    adapter_down_weight,
    adapter_up_weight,
    attention_out_weight,
    first_norm_gain,
    first_norm_bias,
    first_feed_weight,
    first_feed_bias,
    second_feed_weight,
    second_feed_bias,
    second_norm_gain,
    second_norm_bias,
    following_qkv_weight,
    following_bias,
    request_page_count,
    page_slot_table,
    request_adapter,
):
    tok_rows, width = tokens.shape
    dp_count = lax.axis_size("dp")
    mp_count = lax.axis_size("mp")
    dp_index = lax.axis_index("dp")
    mp_index = lax.axis_index("mp")
    kept_values = adapter_down_weight.shape[1] // ADAPTER_RANK
    heads_dev = query_key_value_weight.shape[1] // (3 * HEAD_DIM)
    pages = tok_rows // PAGE
    shared = dp_count == 8 and heads_dev == 4

    owners = request_adapter // kept_values
    level = jnp.sum(jnp.where(owners == mp_index, request_adapter % kept_values, 0))
    down = lax.dynamic_slice_in_dim(
        adapter_down_weight, level * ADAPTER_RANK, ADAPTER_RANK, 1
    )
    up = lax.dynamic_slice_in_dim(adapter_up_weight, level * ADAPTER_RANK, ADAPTER_RANK, 0)
    up_cols = up.shape[1] // mp_count
    sent = jnp.concatenate(
        [
            jnp.broadcast_to(down.T[:, None, :], (ADAPTER_RANK, mp_count, width)),
            up.reshape(ADAPTER_RANK, mp_count, up_cols),
        ],
        axis=2,
    ).reshape(ADAPTER_RANK, mp_count * (width + up_cols))
    got = lax.all_to_all(sent, "mp", split_axis=1, concat_axis=0, tiled=True)
    downs = got[:, :width].T
    ups = got[:, width:]

    def by_kind(matrix):
        split = matrix.reshape(matrix.shape[0], heads_dev, 3, HEAD_DIM)
        if shared:
            split = lax.dynamic_slice_in_dim(split, (dp_index % 2) * 2, 2, 1)
        return jnp.swapaxes(split, 1, 2).reshape(matrix.shape[0], -1)

    place = jnp.stack([dp_index // 2 if shared else 0, mp_index]).astype(jnp.int32)
    hidden_dev = first_feed_weight.shape[1]
    if shared:
        core, chip = dp_index % 2, dp_index // 2
        unit = hidden_dev // 8
        out_unit = attention_out_weight.shape[0] // 8

        def half_columns(values, half):
            axis = values.ndim - 1
            return jnp.concatenate(
                [
                    lax.dynamic_slice_in_dim(values, (half * 4 + (chip ^ r)) * unit, unit, axis)
                    for r in range(4)
                ],
                axis=axis,
            )

        bias_parts = jnp.stack(
            three_parts(
                jnp.concatenate(
                    [half_columns(first_feed_bias, core), half_columns(first_feed_bias, 1 - core)]
                )
            )
        )
        spread = jnp.concatenate(
            [
                lax.dynamic_slice_in_dim(second_feed_weight, (core * 4 + chip) * unit, unit, 0),
                lax.dynamic_slice_in_dim(
                    attention_out_weight, (core * 4 + chip) * out_unit, out_unit, 0
                ),
                jnp.pad(bias_parts, ((0, 13), (0, 0))),
            ],
            axis=0,
        )
        spread = lax.all_gather(spread, "mp", axis=0)
        first_half = half_columns(first_feed_weight, core)
        first_half, spread = lax.optimization_barrier((first_half, spread))
        first_mine = lax.all_gather(first_half, "mp", axis=0)
        body = unit + out_unit
        bias_rows = jnp.sum(spread[:, body : body + 3].astype(jnp.float32), axis=1)
        feed_bias = jnp.swapaxes(bias_rows.reshape(mp_count, 2, 4 * unit), 0, 1)
        feed_bias = feed_bias.reshape(2 * mp_count, 1, 4 * unit)
        spread = spread[:, :body]

    weight = by_kind(query_key_value_weight)
    ups = by_kind(ups)
    if shared:
        swap = [(i, i ^ 1) for i in range(8)]
        across = [(i, i ^ 2) for i in range(8)]
        along = [(i, i ^ 4) for i in range(8)]
        move = lambda value, pairs: lax.ppermute(value, "dp", pairs)
        xs = [tokens, move(tokens, swap)]
        at = lambda flip: (dp_index ^ flip) * pages
        bases = jnp.stack([at(0), at(1)])
    else:
        xs = [tokens]
        bases = jnp.stack([dp_index * pages])
    args = (request_page_count, page_slot_table)
    q, kv = project(*args, owners, bases, xs, weight, downs, ups, pages)
    if shared:
        kv_x = move(kv, across)
        kv_y = move(kv, along)
        step = functools.partial(attend, *args, bases)
        state = step(bases, q, [kv[:tok_rows], kv[tok_rows:]], None, False, pages)
        kv_x, kv_y, state = lax.optimization_barrier((kv_x, kv_y, state))
        kv_d0 = move(kv_y[:tok_rows], across)
        kv_d1 = move(kv_x[tok_rows:], along)
        near = jnp.stack([at(2), at(3), at(4), at(5)])
        state = step(
            near, q, [kv_x[:tok_rows], kv_x[tok_rows:], kv_y[:tok_rows], kv_y[tok_rows:]],
            state, False, pages,
        )
        far = jnp.stack([at(6), at(7)])
        spread, kv_d0, kv_d1 = lax.optimization_barrier((spread, kv_d0, kv_d1))
        spread_x = move(spread, across)
        spread_y = move(spread, along)
        cut = body // 2
        spread_d0 = move(spread_y[:, :cut], across)
        spread_d1 = move(spread_x[:, cut:], along)
        mine = [spread, spread_x, spread_y, spread_d0, spread_d1]
        other = [move(piece, swap) for piece in mine]
        first_other = move(first_mine, swap)
        context = step(far, q, [kv_d0, kv_d1], state, True, pages)
        context = jnp.concatenate(
            [context[:tok_rows], move(context[tok_rows:], swap)], axis=1
        )
        shape = (unit, unit, unit, cut, unit - cut)
        sets = [(first_mine, mine), (first_other, other)]
        wo_arrays = mine + other
        plan = []
        for half in range(2):
            for n, flip in enumerate((0, 1, 2)):
                plan.append((5 * half + n, unit, out_unit, half, flip, 0))
            plan.append((5 * half + 4, unit - cut, out_unit, half, 3, 0))
        wo_used = sorted({index for index, *_ in plan})
        plan = tuple((wo_used.index(index), *rest) for index, *rest in plan)
        wo_arrays = [wo_arrays[index] for index in wo_used]
    else:
        everything = lax.all_gather(kv, "dp", axis=0, tiled=True)
        context = attend(
            *args, bases, jnp.zeros((1,), jnp.int32), q, [everything], None, True, pages
        )
        first_all = lax.all_gather(first_feed_weight, "mp", axis=0)
        second_all = lax.all_gather(second_feed_weight, "mp", axis=0)
        feed_bias = lax.all_gather(first_feed_bias, "mp", axis=0)[:, None]
        sets = [(first_all, [second_all])]
        shape = (hidden_dev,)
        wo_arrays = [lax.all_gather(attention_out_weight, "mp", axis=0)]
        plan = ((0, 0, attention_out_weight.shape[0], 0, 0, 0),)
    contexts = lax.all_gather(context, "mp", axis=0)
    normed = mix(place, tokens, contexts, wo_arrays, plan, first_norm_gain, first_norm_bias)
    layer_rows, next_proj = feed(
        place[1:], normed, feed_bias, sets, shape, second_feed_bias, second_norm_gain,
        second_norm_bias, following_qkv_weight, following_bias, tok_rows // mp_count,
    )
    return (layer_rows, next_proj)


def solution(mesh):
    placed = (
        P("dp", None),
        P(None, "mp"),
        P(None, "mp"),
        P("mp", None),
        P("mp", None),
        P(),
        P(),
        P(None, "mp"),
        P("mp"),
        P("mp", None),
        P(),
        P(),
        P(),
        P(None, "mp"),
        P("mp"),
        P(),
        P(),
        P(),
    )
    return jax.shard_map(
        local,
        mesh=mesh,
        in_specs=placed,
        out_specs=(P(("dp", "mp"), None), P("dp", "mp")),
        check_vma=False,
    )
```

```python
import functools
import math

import jax
import jax.numpy as jnp
from jax import lax
from jax.experimental import pallas as pl
from jax.experimental.pallas import tpu as pltpu
from jax.sharding import PartitionSpec as P

HEAD_DIM = 64
ADAPTER_RANK = 16
PAGE = 128
PAIR = 2 * HEAD_DIM
NEG = -1e30
EXP_SCALE = math.log2(math.e) * HEAD_DIM**-0.5
MIB = 1 << 20


def params(vmem=48):
    return pltpu.CompilerParams(
        dimension_semantics=("arbitrary",), vmem_limit_bytes=vmem * MIB
    )


def request_of(k, counts, requests):
    end = counts[0]
    request = (k >= end).astype(jnp.int32)
    for r in range(1, requests - 1):
        end = end + counts[r]
        request = request + (k >= end).astype(jnp.int32)
    return request


def normalize(values, gain_row, bias_row):
    average = jnp.mean(values, axis=-1, keepdims=True)
    centered = values - average
    variance = jnp.mean(centered * centered, axis=-1, keepdims=True)
    return centered * lax.rsqrt(variance + 1e-05) * gain_row + bias_row


def project_kernel(
    counts, table, owners, bases, *refs, requests, slots, pages, per_piece, parts,
):
    x_refs = refs[:parts]
    w_ref, down_ref, up_ref, q_ref, kv_ref, joined, page_owner = refs[parts:]
    step = pl.program_id(0)
    cols = w_ref.shape[1]

    @pl.when(step == 0)
    def _():
        joined[:, :cols] = w_ref[...]
        joined[:, cols:] = down_ref[...]

        def fill(k, carry):
            page_owner[table[k]] = owners[request_of(k, counts, requests)]
            return carry

        lax.fori_loop(0, slots, fill, 0)

    piece = step * pages // per_piece

    def block(x_ref):
        both = jnp.dot(x_ref[...], joined[...], preferred_element_type=jnp.float32)
        low = both[:, cols:]
        lane_owner = lax.broadcasted_iota(jnp.int32, (PAGE, low.shape[1]), 1) // ADAPTER_RANK
        kept = []
        for p in range(pages):
            page = step * pages + p
            slot = bases[page // per_piece] + page % per_piece
            kept.append(
                jnp.where(lane_owner == page_owner[slot], low[p * PAGE : (p + 1) * PAGE], 0.0)
            )
        low_rank = jnp.concatenate(kept, axis=0).astype(jnp.bfloat16)
        rows = both[:, :cols] + jnp.dot(
            low_rank, up_ref[...], preferred_element_type=jnp.float32
        )
        rows = rows.astype(jnp.bfloat16)
        q_cols = q_ref.shape[1]
        q_ref[...] = rows[:, :q_cols]
        kv_ref[...] = rows[:, q_cols:]

    for i in range(parts):
        pl.when(piece == i)(functools.partial(block, x_refs[i]))


def project(counts, table, owners, bases, xs, weight, down, up, per_piece):
    tok, width = xs[0].shape
    cols = weight.shape[1]
    pages = 2
    rows_step = pages * PAGE
    slots = table.shape[0]
    parts = len(xs)
    each = tok // rows_step
    total = tok * parts
    whole = lambda i, *_: (0, 0)
    rows = lambda i, *_: (i, 0)

    def own(part):
        return lambda i, *_: (jnp.clip(i - part * each, 0, each - 1), 0)

    return pl.pallas_call(
        functools.partial(
            project_kernel,
            requests=counts.shape[0], slots=slots, pages=pages, per_piece=per_piece, parts=parts,
        ),
        grid_spec=pltpu.PrefetchScalarGridSpec(
            num_scalar_prefetch=4,
            grid=(total // rows_step,),
            in_specs=[pl.BlockSpec((rows_step, width), own(i)) for i in range(parts)]
            + [
                pl.BlockSpec(weight.shape, whole),
                pl.BlockSpec(down.shape, whole),
                pl.BlockSpec(up.shape, whole),
            ],
            out_specs=[
                pl.BlockSpec((rows_step, cols // 3), rows),
                pl.BlockSpec((rows_step, 2 * cols // 3), rows),
            ],
            scratch_shapes=[
                pltpu.VMEM((width, cols + down.shape[1]), jnp.bfloat16),
                pltpu.SMEM((slots,), jnp.int32),
            ],
        ),
        out_shape=[
            jax.ShapeDtypeStruct((total, cols // 3), jnp.bfloat16),
            jax.ShapeDtypeStruct((total, 2 * cols // 3), jnp.bfloat16),
        ],
        compiler_params=params(),
        cost_estimate=pl.CostEstimate(
            flops=2 * total * width * cols, bytes_accessed=2 * total * (width + cols),
            transcendentals=0,
        ),
        name="project",
    )(counts, table, owners, bases, *xs, weight, down, up)


def attend_kernel(
    counts, table, q_bases, kv_bases, q_ref, *refs,
    requests, slots, q_size, sizes, first, last, group,
):
    refs = list(refs)
    kv_hbm = [refs.pop(0) for _ in sizes]
    if not first:
        acc_in, stat_in = refs.pop(0), refs.pop(0)
    if last:
        out_ref = refs.pop(0)
    else:
        acc_out, stat_out = refs.pop(0), refs.pop(0)
    kv, scores, listed, amount, asked, q_amount, sems = refs
    copies = []
    offset = 0
    for i, size in enumerate(sizes):
        copy = pltpu.make_async_copy(
            kv_hbm[i], kv.at[pl.ds(offset * PAGE, size * PAGE)], sems.at[i]
        )
        copy.start()
        copies.append(copy)
        offset += size
    for r in range(requests):
        amount[r] = 0
        q_amount[r] = 0

    def place_of(slot, bases, extents):
        place = jnp.int32(-1)
        offset = 0
        for i, size in enumerate(extents):
            near = slot - bases[i]
            place = jnp.where((near >= 0) & (near < size), near + offset, place)
            offset += size
        return place

    q_sizes = (q_size,) * (q_ref.shape[0] // (q_size * PAGE))

    def fill(k, carry):
        r = request_of(k, counts, requests)
        slot = table[k]
        place = place_of(slot, kv_bases, sizes)
        q_place = place_of(slot, q_bases, q_sizes)

        @pl.when(place >= 0)
        def _():
            n = amount[r]
            listed[r, n] = place
            amount[r] = n + 1

        @pl.when(q_place >= 0)
        def _():
            n = q_amount[r]
            asked[r, n] = q_place
            q_amount[r] = n + 1

        return carry

    lax.fori_loop(0, slots, fill, 0)
    for copy in copies:
        copy.wait()
    lane = lax.broadcasted_iota(jnp.int32, (PAGE, PAIR), 1)
    low_lane = lane < HEAD_DIM
    rows = 4 * PAGE

    def one_pair(r, p):
        n = amount[r]
        full = n // group
        blocks = (n + group - 1) // group
        count = q_amount[r]
        a = asked[r, 2 * p]
        b = asked[r, jnp.minimum(2 * p + 1, count - 1)]
        spots = [pl.ds(pl.multiple_of(t * PAGE, PAGE), PAGE) for t in (a, b)]
        parts = []
        for spot in spots:
            q = q_ref[spot, :]
            zero = jnp.zeros_like(q)
            parts += [jnp.where(low_lane, q, zero), jnp.where(low_lane, zero, q)]
        stacked = jnp.concatenate(parts, axis=0)

        def pages_of(j, low):
            found = []
            for i in range(group):
                index = jnp.minimum(j * group + i, n - 1)
                at = pl.multiple_of(listed[r, index] * PAGE, PAGE)
                found.append(kv[pl.ds(at, PAGE), low : low + PAIR])
            return jnp.concatenate(found, axis=0)

        def score(masked, j, top):
            s = lax.dot_general(
                stacked, pages_of(j, 0), (((1,), (1,)), ((), ())),
                preferred_element_type=jnp.float32,
            )
            for i in range(group):
                piece = s[:, i * PAGE : (i + 1) * PAGE]
                if masked and i:
                    piece = jnp.where(j * group + i < n, piece, NEG)
                scores[j, :, i * PAGE : (i + 1) * PAGE] = piece
                top = jnp.maximum(top, piece)
            return top

        top = jnp.full((rows, PAGE), NEG, jnp.float32)
        top = lax.fori_loop(0, full, functools.partial(score, False), top)
        top = lax.fori_loop(full, blocks, functools.partial(score, True), top)
        peak = jnp.max(top, axis=1, keepdims=True)
        if not first:
            old = jnp.concatenate(
                [stat_in[spot, h : h + 1] for spot in spots for h in (0, 1)], axis=0
            )
            peak = jnp.maximum(peak, old)
        shift = peak * EXP_SCALE

        def weigh(j, carry):
            total, acc = carry
            w = jnp.exp2(scores[j] * EXP_SCALE - shift)
            for i in range(group):
                total = total + w[:, i * PAGE : (i + 1) * PAGE]
            acc = acc + jnp.dot(
                w.astype(jnp.bfloat16), pages_of(j, PAIR), preferred_element_type=jnp.float32
            )
            return total, acc

        total, acc = lax.fori_loop(
            0, blocks, weigh,
            (jnp.zeros((rows, PAGE), jnp.float32), jnp.zeros((rows, PAIR), jnp.float32)),
        )
        total = jnp.sum(total, axis=1, keepdims=True)
        if not first:
            shrink = jnp.exp2((old - peak) * EXP_SCALE)
            total = total + shrink * jnp.concatenate(
                [stat_in[spot, h : h + 1] for spot in spots for h in (2, 3)], axis=0
            )
        for t, spot in enumerate(spots):
            h0 = slice(2 * t * PAGE, (2 * t + 1) * PAGE)
            h1 = slice((2 * t + 1) * PAGE, (2 * t + 2) * PAGE)
            value = jnp.where(low_lane, acc[h0], acc[h1])
            if not first:
                value = value + acc_in[spot, :] * jnp.where(low_lane, shrink[h0], shrink[h1])
            if last:
                value = value / jnp.where(low_lane, total[h0], total[h1])
                out_ref[spot, :] = value.astype(jnp.bfloat16)
            else:
                acc_out[spot, :] = value
                stat = jnp.where(lane == 0, peak[h0], peak[h1])
                stat = jnp.where(lane == 2, total[h0], stat)
                stat_out[spot, :] = jnp.where(lane == 3, total[h1], stat)

    def visit_request(r, carry):
        def visit(p, inner):
            one_pair(r, p)
            return inner

        return lax.fori_loop(0, (q_amount[r] + 1) // 2, visit, carry)

    lax.fori_loop(0, requests, visit_request, 0)


def attend(counts, table, q_bases, kv_bases, q, pieces, state, last, q_size):
    tok = q.shape[0]
    sizes = tuple(p.shape[0] // PAGE for p in pieces)
    first = state is None
    group = 4
    slots = table.shape[0]
    requests = counts.shape[0]
    most = min(sum(sizes), slots)
    vmem = pl.BlockSpec(memory_space=pltpu.VMEM)
    state_shape = [jax.ShapeDtypeStruct((tok, PAIR), jnp.float32)] * 2
    out = pl.pallas_call(
        functools.partial(
            attend_kernel,
            requests=requests, slots=slots, q_size=q_size, sizes=sizes,
            first=first, last=last, group=group,
        ),
        grid_spec=pltpu.PrefetchScalarGridSpec(
            num_scalar_prefetch=4,
            grid=(1,),
            in_specs=[pl.BlockSpec((tok, PAIR), lambda i, *_: (0, 0))]
            + [pl.BlockSpec(memory_space=pl.ANY)] * len(pieces)
            + ([] if first else [pl.BlockSpec((tok, PAIR), lambda i, *_: (0, 0))] * 2),
            out_specs=[pl.BlockSpec((tok, PAIR), lambda i, *_: (0, 0))] * (1 if last else 2),
            scratch_shapes=[
                pltpu.VMEM((sum(sizes) * PAGE, 2 * PAIR), jnp.bfloat16),
                pltpu.VMEM(((most + group - 1) // group, 4 * PAGE, group * PAGE), jnp.float32),
                pltpu.SMEM((requests, sum(sizes)), jnp.int32),
                pltpu.SMEM((requests,), jnp.int32),
                pltpu.SMEM((requests, tok // PAGE), jnp.int32),
                pltpu.SMEM((requests,), jnp.int32),
                pltpu.SemaphoreType.DMA((len(pieces),)),
            ],
        ),
        out_shape=[jax.ShapeDtypeStruct((tok, PAIR), jnp.bfloat16)] if last else state_shape,
        compiler_params=params(),
        cost_estimate=pl.CostEstimate(
            flops=2 * tok * sum(sizes) * PAGE * PAIR,
            bytes_accessed=4 * tok * PAIR + 4 * PAGE * PAIR * sum(sizes),
            transcendentals=tok * sum(sizes) * PAGE,
        ),
        name="attend",
    )(counts, table, q_bases, kv_bases, q, *pieces, *([] if first else state))
    return out[0] if last else out


def mix_kernel(x_ref, ctx_ref, *refs, parts):
    out_w_refs = refs[:parts]
    gain_ref, bias_ref, out_ref, joined = refs[parts:]

    @pl.when(pl.program_id(0) == 0)
    def _():
        near = out_w_refs[0].shape[1]
        for i in range(parts):
            joined[:, i * near : (i + 1) * near] = out_w_refs[i][...]

    mixed = x_ref[...].astype(jnp.float32)
    for j in range(ctx_ref.shape[0]):
        mixed = mixed + jnp.dot(ctx_ref[j], joined[j], preferred_element_type=jnp.float32)
    out_ref[...] = normalize(mixed, gain_ref[...], bias_ref[...]).astype(jnp.bfloat16)


def mix(x, ctx, outs, gain, bias):
    tok, width = x.shape
    groups, _, cols = ctx.shape
    block = 256
    rows = lambda i: (i, 0)
    fixed = lambda i: (0, 0)
    return pl.pallas_call(
        functools.partial(mix_kernel, parts=len(outs)),
        grid=(tok // block,),
        in_specs=[
            pl.BlockSpec((block, width), rows),
            pl.BlockSpec((groups, block, cols), lambda i: (0, i, 0)),
        ]
        + [pl.BlockSpec(w.shape, lambda i: (0, 0, 0)) for w in outs]
        + [pl.BlockSpec((1, width), fixed)] * 2,
        out_specs=pl.BlockSpec((block, width), rows),
        scratch_shapes=[pltpu.VMEM((groups, cols, width), jnp.bfloat16)],
        out_shape=jax.ShapeDtypeStruct((tok, width), jnp.bfloat16),
        compiler_params=params(),
        cost_estimate=pl.CostEstimate(
            flops=2 * tok * width * groups * cols, bytes_accessed=8 * tok * width, transcendentals=0
        ),
        name="mix",
    )(x, ctx, *outs, gain[None], bias[None])


def feed_kernel(place, normed_ref, bias_ref, *refs, counts, last_step):
    refs = list(refs)
    sets = []
    for n1, n2 in counts:
        w1s, refs = refs[:n1], refs[n1:]
        w2s, refs = refs[:n2], refs[n2:]
        sets.append((w1s, w2s))
    b2_ref, gain_ref, bias2_ref, next_w_ref, next_b_ref = refs[:5]
    layer_ref, next_ref, acc, done = refs[5:]
    step = pl.program_id(0)
    tok = normed_ref.shape[0]
    block = min(256, tok)
    halves = len(sets)
    groups = (last_step + 1) // halves

    @pl.when(step == 0)
    def _():
        acc[...] = jnp.zeros_like(acc)

    def absorb(h, w1_refs, w2_refs):
        if len(w1_refs) == 1:
            w1 = w1_refs[0][0]
            starts, cols = [0], w1.shape[1]
        else:
            diagonal = jnp.concatenate([w1_refs[3][0], w1_refs[4][0]], axis=0)
            w1 = jnp.concatenate([ref[0] for ref in w1_refs[:3]] + [diagonal], axis=1)
            cols = diagonal.shape[1]
            core = place[2] if h == 0 else 1 - place[2]
            starts = [
                pl.multiple_of((core * 4 + (place[1] ^ r)) * cols, cols) for r in range(4)
            ]
        w2 = jnp.concatenate([ref[0] for ref in w2_refs], axis=0)
        bias = jnp.concatenate(
            [
                jnp.sum(
                    bias_ref[0, :, pl.ds(start, cols)].astype(jnp.float32), axis=0, keepdims=True
                )
                for start in starts
            ],
            axis=1,
        )
        for t in range(tok // block):
            rows = slice(t * block, (t + 1) * block)
            pre = jnp.dot(normed_ref[rows, :], w1, preferred_element_type=jnp.float32) + bias
            hidden = 0.5 * pre * (1.0 + lax.erf(pre * math.sqrt(0.5)))
            acc[rows, :] += jnp.dot(
                hidden.astype(jnp.bfloat16), w2, preferred_element_type=jnp.float32
            )

    for h in range(halves):
        pl.when(step // groups == h)(functools.partial(absorb, h, *sets[h]))

    @pl.when(step == last_step)
    def _():
        for t in range(tok // block):
            rows = slice(t * block, (t + 1) * block)
            total = normed_ref[rows, :].astype(jnp.float32) + acc[rows, :] + b2_ref[...]
            layer = normalize(total, gain_ref[...], bias2_ref[...]).astype(jnp.bfloat16)
            done[rows, :] = layer
            next_ref[rows, :] = (
                jnp.dot(layer, next_w_ref[...], preferred_element_type=jnp.float32)
                + next_b_ref[...]
            ).astype(jnp.bfloat16)
        share = layer_ref.shape[0]
        layer_ref[...] = done[pl.ds(pl.multiple_of(place[0] * share, share), share), :]


def feed(place, normed, bias, sets, b2, gain, bias2, next_w, next_b, share):
    tok, width = normed.shape
    halves = len(sets)
    groups = bias.shape[0]
    cols = bias.shape[2] // halves
    steps = halves * groups
    fixed = lambda i, *_: (0, 0)
    specs, arrays = [], []
    for h, (w1s, w2s) in enumerate(sets):
        at = lambda i, *_, h=h: (jnp.clip(i - h * groups, 0, groups - 1), 0, 0)
        for array in (*w1s, *w2s):
            specs.append(pl.BlockSpec((1,) + array.shape[1:], at))
            arrays.append(array)
    next_cols = next_w.shape[1]
    return pl.pallas_call(
        functools.partial(
            feed_kernel,
            counts=tuple((len(w1s), len(w2s)) for w1s, w2s in sets),
            last_step=steps - 1,
        ),
        grid_spec=pltpu.PrefetchScalarGridSpec(
            num_scalar_prefetch=1,
            grid=(steps,),
            in_specs=[
                pl.BlockSpec((tok, width), fixed),
                pl.BlockSpec((1,) + bias.shape[1:], lambda i, *_: (i % groups, 0, 0)),
            ]
            + specs
            + [
                pl.BlockSpec((1, width), fixed),
                pl.BlockSpec((1, width), fixed),
                pl.BlockSpec((1, width), fixed),
                pl.BlockSpec((width, next_cols), fixed),
                pl.BlockSpec((1, next_cols), fixed),
            ],
            out_specs=[
                pl.BlockSpec((share, width), fixed),
                pl.BlockSpec((tok, next_cols), fixed),
            ],
            scratch_shapes=[
                pltpu.VMEM((tok, width), jnp.float32),
                pltpu.VMEM((tok, width), jnp.bfloat16),
            ],
        ),
        out_shape=[
            jax.ShapeDtypeStruct((share, width), jnp.bfloat16),
            jax.ShapeDtypeStruct((tok, next_cols), jnp.bfloat16),
        ],
        compiler_params=params(),
        cost_estimate=pl.CostEstimate(
            flops=4 * tok * width * cols * steps, bytes_accessed=4 * width * cols * steps,
            transcendentals=tok * cols * steps,
        ),
        name="feed",
    )(
        place, normed, bias, *arrays,
        b2[None], gain[None], bias2[None], next_w, next_b[None],
    )


def three_parts(values):
    high = lax.reduce_precision(values, 8, 7)
    middle = lax.reduce_precision(values - high, 8, 7)
    rest = values - high - middle
    return [part.astype(jnp.bfloat16) for part in (high, middle, rest)]


def local(
    tokens,
    query_key_value_weight,
    adapter_down_weight,
    adapter_up_weight,
    attention_out_weight,
    first_norm_gain,
    first_norm_bias,
    first_feed_weight,
    first_feed_bias,
    second_feed_weight,
    second_feed_bias,
    second_norm_gain,
    second_norm_bias,
    following_qkv_weight,
    following_bias,
    request_page_count,
    page_slot_table,
    request_adapter,
):
    tok_rows, width = tokens.shape
    dp_count = lax.axis_size("dp")
    mp_count = lax.axis_size("mp")
    dp_index = lax.axis_index("dp")
    mp_index = lax.axis_index("mp")
    kept_values = adapter_down_weight.shape[1] // ADAPTER_RANK
    heads_dev = query_key_value_weight.shape[1] // (3 * HEAD_DIM)
    pages = tok_rows // PAGE
    shared = dp_count == 8 and heads_dev == 4

    owners = request_adapter // kept_values
    level = jnp.sum(jnp.where(owners == mp_index, request_adapter % kept_values, 0))
    down = lax.dynamic_slice_in_dim(
        adapter_down_weight, level * ADAPTER_RANK, ADAPTER_RANK, 1
    )
    up = lax.dynamic_slice_in_dim(adapter_up_weight, level * ADAPTER_RANK, ADAPTER_RANK, 0)
    up_cols = up.shape[1] // mp_count
    sent = jnp.concatenate(
        [
            jnp.broadcast_to(down.T[:, None, :], (ADAPTER_RANK, mp_count, width)),
            up.reshape(ADAPTER_RANK, mp_count, up_cols),
        ],
        axis=2,
    ).reshape(ADAPTER_RANK, mp_count * (width + up_cols))
    got = lax.all_to_all(sent, "mp", split_axis=1, concat_axis=0, tiled=True)
    downs = got[:, :width].T
    ups = got[:, width:]

    def by_kind(matrix):
        split = matrix.reshape(matrix.shape[0], heads_dev, 3, HEAD_DIM)
        if shared:
            split = lax.dynamic_slice_in_dim(split, (dp_index % 2) * 2, 2, 1)
        return jnp.swapaxes(split, 1, 2).reshape(matrix.shape[0], -1)

    place = jnp.stack(
        [mp_index] + ([dp_index // 2, dp_index % 2] if shared else [0, 0])
    ).astype(jnp.int32)
    hidden_dev = first_feed_weight.shape[1]
    if shared:
        unit = hidden_dev // 8
        turn = (dp_index % 2) * 4 + dp_index // 2
        first = lax.dynamic_slice_in_dim(first_feed_weight, turn * unit, unit, 1)
        first = lax.all_gather(first, "mp", axis=0)

    weight = by_kind(query_key_value_weight)
    ups = by_kind(ups)
    if shared:
        swap = [(i, i ^ 1) for i in range(8)]
        across = [(i, i ^ 2) for i in range(8)]
        along = [(i, i ^ 4) for i in range(8)]
        move = lambda value, pairs: lax.ppermute(value, "dp", pairs)
        xs = [tokens, move(tokens, swap)]
        at = lambda flip: (dp_index ^ flip) * pages
        bases = jnp.stack([at(0), at(1)])
    else:
        xs = [tokens]
        bases = jnp.stack([dp_index * pages])
    args = (request_page_count, page_slot_table)
    q, kv = project(*args, owners, bases, xs, weight, downs, ups, pages)
    if shared:
        kv_x = move(kv, across)
        kv_y = move(kv, along)
        second = jnp.concatenate(
            [lax.dynamic_slice_in_dim(second_feed_weight, turn * unit, unit, 0)]
            + [jnp.pad(jnp.stack(three_parts(first_feed_bias)), ((0, 13), (0, 0)))],
            axis=0,
        )
        second, _ = lax.optimization_barrier((second, kv))
        second = lax.all_gather(second, "mp", axis=0)
        step = functools.partial(attend, *args, bases)
        state = step(bases, q, [kv[:tok_rows], kv[tok_rows:]], None, False, pages)
        kv_x, kv_y, state, first = lax.optimization_barrier((kv_x, kv_y, state, first))
        kv_d0 = move(kv_y[:tok_rows], across)
        kv_d1 = move(kv_x[tok_rows:], along)
        first_x = move(first, across)
        first_y = move(first, along)
        out_rows = attention_out_weight.shape[0] // 2
        out_half = lax.dynamic_slice_in_dim(
            attention_out_weight, (dp_index % 2) * out_rows, out_rows, 0
        )
        out_half, kv_x = lax.optimization_barrier((out_half, kv_x))
        out_mine = lax.all_gather(out_half, "mp", axis=0)
        near = jnp.stack([at(2), at(3), at(4), at(5)])
        state = step(
            near, q, [kv_x[:tok_rows], kv_x[tok_rows:], kv_y[:tok_rows], kv_y[tok_rows:]],
            state, False, pages,
        )
        kv_d0, kv_d1, first_x, first_y, state = lax.optimization_barrier(
            (kv_d0, kv_d1, first_x, first_y, state)
        )
        cut = width // 2
        first_d0 = move(first_y[:, :cut], across)
        first_d1 = move(first_x[:, cut:], along)
        first_near = [move(piece, swap) for piece in (first, first_x, first_y)]
        far = jnp.stack([at(6), at(7)])
        context = step(far, q, [kv_d0, kv_d1], state, True, pages)
        context, first_d0, first_d1, second, out_mine = lax.optimization_barrier(
            (context, first_d0, first_d1, second, out_mine)
        )
        bias_rows = second[:, unit:]
        second = second[:, :unit]
        second_x = move(second, across)
        second_y = move(second, along)
        context = jnp.concatenate(
            [context[:tok_rows], move(context[tok_rows:], swap)], axis=1
        )
        contexts = lax.all_gather(context, "mp", axis=0)
        out_other = move(out_mine, swap)
        firsts = [first, first_x, first_y, first_d0, first_d1]
        first_others = first_near + [move(first_d0, swap), move(first_d1, swap)]
        half = unit // 2
        second_d0 = move(second_y[:, :half], across)
        second_d1 = move(second_x[:, half:], along)
        seconds = [second, second_x, second_y, second_d0, second_d1]
        second_others = [move(piece, swap) for piece in seconds]
        sets = [(firsts, seconds), (first_others, second_others)]
        outs = [out_mine, out_other]
    else:
        everything = lax.all_gather(kv, "dp", axis=0, tiled=True)
        context = attend(
            *args, bases, jnp.zeros((1,), jnp.int32), q, [everything], None, True, pages
        )
        bias_rows = jnp.pad(jnp.stack(three_parts(first_feed_bias)), ((0, 13), (0, 0)))
        second = lax.all_gather(second_feed_weight, "mp", axis=0)
        bias_rows = lax.all_gather(bias_rows, "mp", axis=0)
        sets = [([lax.all_gather(first_feed_weight, "mp", axis=0)], [second])]
        outs = [lax.all_gather(attention_out_weight, "mp", axis=0)]
        contexts = lax.all_gather(context, "mp", axis=0)
    normed = mix(tokens, contexts, outs, first_norm_gain, first_norm_bias)
    layer_rows, next_proj = feed(
        place, normed, bias_rows, sets, second_feed_bias, second_norm_gain,
        second_norm_bias, following_qkv_weight, following_bias, tok_rows // mp_count,
    )
    return (layer_rows, next_proj)


def solution(mesh):
    placed = (
        P("dp", None),
        P(None, "mp"),
        P(None, "mp"),
        P("mp", None),
        P("mp", None),
        P(),
        P(),
        P(None, "mp"),
        P("mp"),
        P("mp", None),
        P(),
        P(),
        P(),
        P(None, "mp"),
        P("mp"),
        P(),
        P(),
        P(),
    )
    return jax.shard_map(
        local,
        mesh=mesh,
        in_specs=placed,
        out_specs=(P(("dp", "mp"), None), P("dp", "mp")),
        check_vma=False,
    )
```

```python
import functools
import math

import jax
import jax.numpy as jnp
from jax import lax
from jax.experimental import pallas as pl
from jax.experimental.pallas import tpu as pltpu
from jax.sharding import PartitionSpec as P

HEAD_DIM = 64
ADAPTER_RANK = 16
PAGE = 128
PAIR = 2 * HEAD_DIM
NEG = -1e30
EXP_SCALE = math.log2(math.e) * HEAD_DIM**-0.5
MIB = 1 << 20


def params(vmem=48):
    return pltpu.CompilerParams(
        dimension_semantics=("arbitrary",), vmem_limit_bytes=vmem * MIB
    )


def request_of(k, counts, requests):
    end = counts[0]
    request = (k >= end).astype(jnp.int32)
    for r in range(1, requests - 1):
        end = end + counts[r]
        request = request + (k >= end).astype(jnp.int32)
    return request


def normalize(values, gain_row, bias_row):
    average = jnp.mean(values, axis=-1, keepdims=True)
    centered = values - average
    variance = jnp.mean(centered * centered, axis=-1, keepdims=True)
    return centered * lax.rsqrt(variance + 1e-05) * gain_row + bias_row


def project_kernel(
    counts, table, owners, bases, *refs, requests, slots, pages, per_piece, parts,
):
    x_refs = refs[:parts]
    w_ref, down_ref, up_ref, q_ref, kv_ref, joined, page_owner = refs[parts:]
    step = pl.program_id(0)
    cols = w_ref.shape[1]

    @pl.when(step == 0)
    def _():
        joined[:, :cols] = w_ref[...]
        joined[:, cols:] = down_ref[...]

        def fill(k, carry):
            page_owner[table[k]] = owners[request_of(k, counts, requests)]
            return carry

        lax.fori_loop(0, slots, fill, 0)

    piece = step * pages // per_piece

    def block(x_ref):
        both = jnp.dot(x_ref[...], joined[...], preferred_element_type=jnp.float32)
        low = both[:, cols:]
        lane_owner = lax.broadcasted_iota(jnp.int32, (PAGE, low.shape[1]), 1) // ADAPTER_RANK
        kept = []
        for p in range(pages):
            page = step * pages + p
            slot = bases[page // per_piece] + page % per_piece
            kept.append(
                jnp.where(lane_owner == page_owner[slot], low[p * PAGE : (p + 1) * PAGE], 0.0)
            )
        low_rank = jnp.concatenate(kept, axis=0).astype(jnp.bfloat16)
        rows = both[:, :cols] + jnp.dot(
            low_rank, up_ref[...], preferred_element_type=jnp.float32
        )
        rows = rows.astype(jnp.bfloat16)
        q_cols = q_ref.shape[1]
        q_ref[...] = rows[:, :q_cols]
        keys = rows[:, q_cols : 2 * q_cols]
        values = rows[:, 2 * q_cols :]
        for p in range(pages):
            here = slice(p * PAGE, (p + 1) * PAGE)
            kv_ref[p, :PAIR, :] = keys[here].T
            kv_ref[p, PAIR:, :] = values[here]

    for i in range(parts):
        pl.when(piece == i)(functools.partial(block, x_refs[i]))


def project(counts, table, owners, bases, xs, weight, down, up, per_piece):
    tok, width = xs[0].shape
    cols = weight.shape[1]
    pages = 2
    rows_step = pages * PAGE
    slots = table.shape[0]
    parts = len(xs)
    each = tok // rows_step
    total = tok * parts
    whole = lambda i, *_: (0, 0)
    rows = lambda i, *_: (i, 0)

    def own(part):
        return lambda i, *_: (jnp.clip(i - part * each, 0, each - 1), 0)

    return pl.pallas_call(
        functools.partial(
            project_kernel,
            requests=counts.shape[0], slots=slots, pages=pages, per_piece=per_piece, parts=parts,
        ),
        grid_spec=pltpu.PrefetchScalarGridSpec(
            num_scalar_prefetch=4,
            grid=(total // rows_step,),
            in_specs=[pl.BlockSpec((rows_step, width), own(i)) for i in range(parts)]
            + [
                pl.BlockSpec(weight.shape, whole),
                pl.BlockSpec(down.shape, whole),
                pl.BlockSpec(up.shape, whole),
            ],
            out_specs=[
                pl.BlockSpec((rows_step, cols // 3), rows),
                pl.BlockSpec((pages, PAIR + PAGE, PAIR), lambda i, *_: (i, 0, 0)),
            ],
            scratch_shapes=[
                pltpu.VMEM((width, cols + down.shape[1]), jnp.bfloat16),
                pltpu.SMEM((slots,), jnp.int32),
            ],
        ),
        out_shape=[
            jax.ShapeDtypeStruct((total, cols // 3), jnp.bfloat16),
            jax.ShapeDtypeStruct((total // PAGE, PAIR + PAGE, PAIR), jnp.bfloat16),
        ],
        compiler_params=params(),
        cost_estimate=pl.CostEstimate(
            flops=2 * total * width * cols, bytes_accessed=2 * total * (width + cols),
            transcendentals=0,
        ),
        name="project",
    )(counts, table, owners, bases, *xs, weight, down, up)


def attend_kernel(
    counts, table, q_bases, kv_bases, q_ref, *refs,
    requests, slots, q_size, arrays, sizes, first, last, group,
):
    refs = list(refs)
    kv_hbm = [refs.pop(0) for _ in arrays]
    if not first:
        acc_in, stat_in = refs.pop(0), refs.pop(0)
    if last:
        out_ref = refs.pop(0)
    else:
        acc_out, stat_out = refs.pop(0), refs.pop(0)
    kv, scores, listed, amount, asked, q_amount, sems = refs
    copies = []
    offset = 0
    for i, size in enumerate(arrays):
        copy = pltpu.make_async_copy(kv_hbm[i], kv.at[pl.ds(offset, size)], sems.at[i])
        copy.start()
        copies.append(copy)
        offset += size
    for r in range(requests):
        amount[r] = 0
        q_amount[r] = 0

    def place_of(slot, bases, extents):
        place = jnp.int32(-1)
        offset = 0
        for i, size in enumerate(extents):
            near = slot - bases[i]
            place = jnp.where((near >= 0) & (near < size), near + offset, place)
            offset += size
        return place

    q_sizes = (q_size,) * (q_ref.shape[0] // (q_size * PAGE))

    def fill(k, carry):
        r = request_of(k, counts, requests)
        slot = table[k]
        place = place_of(slot, kv_bases, sizes)
        q_place = place_of(slot, q_bases, q_sizes)

        @pl.when(place >= 0)
        def _():
            n = amount[r]
            listed[r, n] = place
            amount[r] = n + 1

        @pl.when(q_place >= 0)
        def _():
            n = q_amount[r]
            asked[r, n] = q_place
            q_amount[r] = n + 1

        return carry

    lax.fori_loop(0, slots, fill, 0)
    for copy in copies:
        copy.wait()
    lane = lax.broadcasted_iota(jnp.int32, (PAGE, PAIR), 1)
    low_lane = lane < HEAD_DIM
    rows = 4 * PAGE

    def one_pair(r, p):
        n = amount[r]
        full = n // group
        blocks = (n + group - 1) // group
        count = q_amount[r]
        a = asked[r, 2 * p]
        b = asked[r, jnp.minimum(2 * p + 1, count - 1)]
        spots = [pl.ds(pl.multiple_of(t * PAGE, PAGE), PAGE) for t in (a, b)]
        parts = []
        for spot in spots:
            q = q_ref[spot, :]
            zero = jnp.zeros_like(q)
            parts += [jnp.where(low_lane, q, zero), jnp.where(low_lane, zero, q)]
        stacked = jnp.concatenate(parts, axis=0)

        def page_of(j, i):
            return listed[r, jnp.minimum(j * group + i, n - 1)]

        def score(masked, j, top):
            keys = jnp.concatenate(
                [kv[page_of(j, i), :PAIR, :] for i in range(group)], axis=1
            )
            s = jnp.dot(stacked, keys, preferred_element_type=jnp.float32)
            for i in range(group):
                piece = s[:, i * PAGE : (i + 1) * PAGE]
                if masked and i:
                    piece = jnp.where(j * group + i < n, piece, NEG)
                scores[j, :, i * PAGE : (i + 1) * PAGE] = piece
                top = jnp.maximum(top, piece)
            return top

        top = jnp.full((rows, PAGE), NEG, jnp.float32)
        top = lax.fori_loop(0, full, functools.partial(score, False), top)
        top = lax.fori_loop(full, blocks, functools.partial(score, True), top)
        peak = jnp.max(top, axis=1, keepdims=True)
        if not first:
            old = jnp.concatenate(
                [stat_in[spot, h : h + 1] for spot in spots for h in (0, 1)], axis=0
            )
            peak = jnp.maximum(peak, old)
        shift = peak * EXP_SCALE

        def weigh(j, carry):
            total, acc = carry
            w = jnp.exp2(scores[j] * EXP_SCALE - shift)
            for i in range(group):
                total = total + w[:, i * PAGE : (i + 1) * PAGE]
            values = jnp.concatenate(
                [kv[page_of(j, i), PAIR:, :] for i in range(group)], axis=0
            )
            acc = acc + jnp.dot(
                w.astype(jnp.bfloat16), values, preferred_element_type=jnp.float32
            )
            return total, acc

        total, acc = lax.fori_loop(
            0, blocks, weigh,
            (jnp.zeros((rows, PAGE), jnp.float32), jnp.zeros((rows, PAIR), jnp.float32)),
        )
        total = jnp.sum(total, axis=1, keepdims=True)
        if not first:
            shrink = jnp.exp2((old - peak) * EXP_SCALE)
            total = total + shrink * jnp.concatenate(
                [stat_in[spot, h : h + 1] for spot in spots for h in (2, 3)], axis=0
            )
        for t, spot in enumerate(spots):
            h0 = slice(2 * t * PAGE, (2 * t + 1) * PAGE)
            h1 = slice((2 * t + 1) * PAGE, (2 * t + 2) * PAGE)
            value = jnp.where(low_lane, acc[h0], acc[h1])
            if not first:
                value = value + acc_in[spot, :] * jnp.where(low_lane, shrink[h0], shrink[h1])
            if last:
                value = value / jnp.where(low_lane, total[h0], total[h1])
                out_ref[spot, :] = value.astype(jnp.bfloat16)
            else:
                acc_out[spot, :] = value
                stat = jnp.where(lane == 0, peak[h0], peak[h1])
                stat = jnp.where(lane == 2, total[h0], stat)
                stat_out[spot, :] = jnp.where(lane == 3, total[h1], stat)

    def visit_request(r, carry):
        def visit(p, inner):
            one_pair(r, p)
            return inner

        return lax.fori_loop(0, (q_amount[r] + 1) // 2, visit, carry)

    lax.fori_loop(0, requests, visit_request, 0)


def attend(counts, table, q_bases, kv_bases, q, pieces, state, last, q_size):
    tok = q.shape[0]
    arrays = tuple(p.shape[0] for p in pieces)
    sizes = (sum(arrays) // kv_bases.shape[0],) * kv_bases.shape[0]
    first = state is None
    group = 4
    slots = table.shape[0]
    requests = counts.shape[0]
    most = min(sum(sizes), slots)
    vmem = pl.BlockSpec(memory_space=pltpu.VMEM)
    state_shape = [jax.ShapeDtypeStruct((tok, PAIR), jnp.float32)] * 2
    out = pl.pallas_call(
        functools.partial(
            attend_kernel,
            requests=requests, slots=slots, q_size=q_size, arrays=arrays, sizes=sizes,
            first=first, last=last, group=group,
        ),
        grid_spec=pltpu.PrefetchScalarGridSpec(
            num_scalar_prefetch=4,
            grid=(1,),
            in_specs=[pl.BlockSpec((tok, PAIR), lambda i, *_: (0, 0))]
            + [pl.BlockSpec(memory_space=pl.ANY)] * len(pieces)
            + ([] if first else [pl.BlockSpec((tok, PAIR), lambda i, *_: (0, 0))] * 2),
            out_specs=[pl.BlockSpec((tok, PAIR), lambda i, *_: (0, 0))] * (1 if last else 2),
            scratch_shapes=[
                pltpu.VMEM((sum(sizes), PAIR + PAGE, PAIR), jnp.bfloat16),
                pltpu.VMEM(((most + group - 1) // group, 4 * PAGE, group * PAGE), jnp.float32),
                pltpu.SMEM((requests, sum(sizes)), jnp.int32),
                pltpu.SMEM((requests,), jnp.int32),
                pltpu.SMEM((requests, tok // PAGE), jnp.int32),
                pltpu.SMEM((requests,), jnp.int32),
                pltpu.SemaphoreType.DMA((len(pieces),)),
            ],
        ),
        out_shape=[jax.ShapeDtypeStruct((tok, PAIR), jnp.bfloat16)] if last else state_shape,
        compiler_params=params(),
        cost_estimate=pl.CostEstimate(
            flops=tok * PAIR, bytes_accessed=4 * tok * PAIR, transcendentals=0,
        ),
        name="attend",
    )(counts, table, q_bases, kv_bases, q, *pieces, *([] if first else state))
    return out[0] if last else out


def mix_kernel(x_ref, ctx_ref, *refs, parts):
    out_w_refs = refs[:parts]
    gain_ref, bias_ref, out_ref, joined = refs[parts:]

    @pl.when(pl.program_id(0) == 0)
    def _():
        near = out_w_refs[0].shape[1]
        for i in range(parts):
            joined[:, i * near : (i + 1) * near] = out_w_refs[i][...]

    mixed = x_ref[...].astype(jnp.float32)
    for j in range(ctx_ref.shape[0]):
        mixed = mixed + jnp.dot(ctx_ref[j], joined[j], preferred_element_type=jnp.float32)
    out_ref[...] = normalize(mixed, gain_ref[...], bias_ref[...]).astype(jnp.bfloat16)


def mix(x, ctx, outs, gain, bias):
    tok, width = x.shape
    groups, _, cols = ctx.shape
    block = 256
    rows = lambda i: (i, 0)
    fixed = lambda i: (0, 0)
    return pl.pallas_call(
        functools.partial(mix_kernel, parts=len(outs)),
        grid=(tok // block,),
        in_specs=[
            pl.BlockSpec((block, width), rows),
            pl.BlockSpec((groups, block, cols), lambda i: (0, i, 0)),
        ]
        + [pl.BlockSpec(w.shape, lambda i: (0, 0, 0)) for w in outs]
        + [pl.BlockSpec((1, width), fixed)] * 2,
        out_specs=pl.BlockSpec((block, width), rows),
        scratch_shapes=[pltpu.VMEM((groups, cols, width), jnp.bfloat16)],
        out_shape=jax.ShapeDtypeStruct((tok, width), jnp.bfloat16),
        compiler_params=params(),
        cost_estimate=pl.CostEstimate(
            flops=2 * tok * width * groups * cols, bytes_accessed=8 * tok * width, transcendentals=0
        ),
        name="mix",
    )(x, ctx, *outs, gain[None], bias[None])


def feed_kernel(place, normed_ref, bias_ref, *refs, counts, last_step):
    refs = list(refs)
    sets = []
    for n1, n2 in counts:
        w1s, refs = refs[:n1], refs[n1:]
        w2s, refs = refs[:n2], refs[n2:]
        sets.append((w1s, w2s))
    b2_ref, gain_ref, bias2_ref, next_w_ref, next_b_ref = refs[:5]
    layer_ref, next_ref, acc, done = refs[5:]
    step = pl.program_id(0)
    tok = normed_ref.shape[0]
    block = min(256, tok)
    halves = len(sets)
    groups = (last_step + 1) // halves

    @pl.when(step == 0)
    def _():
        acc[...] = jnp.zeros_like(acc)

    def absorb(h, w1_refs, w2_refs):
        if len(w1_refs) == 1:
            w1 = w1_refs[0][0]
            starts, cols = [0], w1.shape[1]
        else:
            diagonal = jnp.concatenate([w1_refs[3][0], w1_refs[4][0]], axis=0)
            w1 = jnp.concatenate([ref[0] for ref in w1_refs[:3]] + [diagonal], axis=1)
            cols = diagonal.shape[1]
            core = place[2] if h == 0 else 1 - place[2]
            starts = [
                pl.multiple_of((core * 4 + (place[1] ^ r)) * cols, cols) for r in range(4)
            ]
        w2 = jnp.concatenate([ref[0] for ref in w2_refs], axis=0)
        bias = jnp.concatenate(
            [
                jnp.sum(
                    bias_ref[0, :, pl.ds(start, cols)].astype(jnp.float32), axis=0, keepdims=True
                )
                for start in starts
            ],
            axis=1,
        )
        for t in range(tok // block):
            rows = slice(t * block, (t + 1) * block)
            pre = jnp.dot(normed_ref[rows, :], w1, preferred_element_type=jnp.float32) + bias
            hidden = 0.5 * pre * (1.0 + lax.erf(pre * math.sqrt(0.5)))
            acc[rows, :] += jnp.dot(
                hidden.astype(jnp.bfloat16), w2, preferred_element_type=jnp.float32
            )

    for h in range(halves):
        pl.when(step // groups == h)(functools.partial(absorb, h, *sets[h]))

    @pl.when(step == last_step)
    def _():
        for t in range(tok // block):
            rows = slice(t * block, (t + 1) * block)
            total = normed_ref[rows, :].astype(jnp.float32) + acc[rows, :] + b2_ref[...]
            layer = normalize(total, gain_ref[...], bias2_ref[...]).astype(jnp.bfloat16)
            done[rows, :] = layer
            next_ref[rows, :] = (
                jnp.dot(layer, next_w_ref[...], preferred_element_type=jnp.float32)
                + next_b_ref[...]
            ).astype(jnp.bfloat16)
        share = layer_ref.shape[0]
        layer_ref[...] = done[pl.ds(pl.multiple_of(place[0] * share, share), share), :]


def feed(place, normed, bias, sets, b2, gain, bias2, next_w, next_b, share):
    tok, width = normed.shape
    halves = len(sets)
    groups = bias.shape[0]
    cols = bias.shape[2] // halves
    steps = halves * groups
    fixed = lambda i, *_: (0, 0)
    specs, arrays = [], []
    for h, (w1s, w2s) in enumerate(sets):
        at = lambda i, *_, h=h: (jnp.clip(i - h * groups, 0, groups - 1), 0, 0)
        for array in (*w1s, *w2s):
            specs.append(pl.BlockSpec((1,) + array.shape[1:], at))
            arrays.append(array)
    next_cols = next_w.shape[1]
    return pl.pallas_call(
        functools.partial(
            feed_kernel,
            counts=tuple((len(w1s), len(w2s)) for w1s, w2s in sets),
            last_step=steps - 1,
        ),
        grid_spec=pltpu.PrefetchScalarGridSpec(
            num_scalar_prefetch=1,
            grid=(steps,),
            in_specs=[
                pl.BlockSpec((tok, width), fixed),
                pl.BlockSpec((1,) + bias.shape[1:], lambda i, *_: (i % groups, 0, 0)),
            ]
            + specs
            + [
                pl.BlockSpec((1, width), fixed),
                pl.BlockSpec((1, width), fixed),
                pl.BlockSpec((1, width), fixed),
                pl.BlockSpec((width, next_cols), fixed),
                pl.BlockSpec((1, next_cols), fixed),
            ],
            out_specs=[
                pl.BlockSpec((share, width), fixed),
                pl.BlockSpec((tok, next_cols), fixed),
            ],
            scratch_shapes=[
                pltpu.VMEM((tok, width), jnp.float32),
                pltpu.VMEM((tok, width), jnp.bfloat16),
            ],
        ),
        out_shape=[
            jax.ShapeDtypeStruct((share, width), jnp.bfloat16),
            jax.ShapeDtypeStruct((tok, next_cols), jnp.bfloat16),
        ],
        compiler_params=params(),
        cost_estimate=pl.CostEstimate(
            flops=4 * tok * width * cols * steps, bytes_accessed=4 * width * cols * steps,
            transcendentals=tok * cols * steps,
        ),
        name="feed",
    )(
        place, normed, bias, *arrays,
        b2[None], gain[None], bias2[None], next_w, next_b[None],
    )


def three_parts(values):
    high = lax.reduce_precision(values, 8, 7)
    middle = lax.reduce_precision(values - high, 8, 7)
    rest = values - high - middle
    return [part.astype(jnp.bfloat16) for part in (high, middle, rest)]


def local(
    tokens,
    query_key_value_weight,
    adapter_down_weight,
    adapter_up_weight,
    attention_out_weight,
    first_norm_gain,
    first_norm_bias,
    first_feed_weight,
    first_feed_bias,
    second_feed_weight,
    second_feed_bias,
    second_norm_gain,
    second_norm_bias,
    following_qkv_weight,
    following_bias,
    request_page_count,
    page_slot_table,
    request_adapter,
):
    tok_rows, width = tokens.shape
    dp_count = lax.axis_size("dp")
    mp_count = lax.axis_size("mp")
    dp_index = lax.axis_index("dp")
    mp_index = lax.axis_index("mp")
    kept_values = adapter_down_weight.shape[1] // ADAPTER_RANK
    heads_dev = query_key_value_weight.shape[1] // (3 * HEAD_DIM)
    pages = tok_rows // PAGE
    shared = dp_count == 8 and heads_dev == 4

    owners = request_adapter // kept_values
    level = jnp.sum(jnp.where(owners == mp_index, request_adapter % kept_values, 0))
    down = lax.dynamic_slice_in_dim(
        adapter_down_weight, level * ADAPTER_RANK, ADAPTER_RANK, 1
    )
    up = lax.dynamic_slice_in_dim(adapter_up_weight, level * ADAPTER_RANK, ADAPTER_RANK, 0)
    up_cols = up.shape[1] // mp_count
    sent = jnp.concatenate(
        [
            jnp.broadcast_to(down.T[:, None, :], (ADAPTER_RANK, mp_count, width)),
            up.reshape(ADAPTER_RANK, mp_count, up_cols),
        ],
        axis=2,
    ).reshape(ADAPTER_RANK, mp_count * (width + up_cols))
    got = lax.all_to_all(sent, "mp", split_axis=1, concat_axis=0, tiled=True)

    def by_kind(matrix):
        split = matrix.reshape(matrix.shape[0], heads_dev, 3, HEAD_DIM)
        if shared:
            split = lax.dynamic_slice_in_dim(split, (dp_index % 2) * 2, 2, 1)
        return jnp.swapaxes(split, 1, 2).reshape(matrix.shape[0], -1)

    place = jnp.stack(
        [mp_index] + ([dp_index // 2, dp_index % 2] if shared else [0, 0])
    ).astype(jnp.int32)
    hidden_dev = first_feed_weight.shape[1]
    if shared:
        unit = hidden_dev // 8
        turn = (dp_index % 2) * 4 + dp_index // 2
        first = lax.dynamic_slice_in_dim(first_feed_weight, turn * unit, unit, 1)
        first, got = lax.optimization_barrier((first, got))
        first = lax.all_gather(first, "mp", axis=0)

    downs = got[:, :width].T
    ups = got[:, width:]
    weight = by_kind(query_key_value_weight)
    ups = by_kind(ups)
    if shared:
        swap = [(i, i ^ 1) for i in range(8)]
        across = [(i, i ^ 2) for i in range(8)]
        along = [(i, i ^ 4) for i in range(8)]
        move = lambda value, pairs: lax.ppermute(value, "dp", pairs)
        xs = [tokens, move(tokens, swap)]
        at = lambda flip: (dp_index ^ flip) * pages
        bases = jnp.stack([at(0), at(1)])
    else:
        xs = [tokens]
        bases = jnp.stack([dp_index * pages])
    args = (request_page_count, page_slot_table)
    q, kv = project(*args, owners, bases, xs, weight, downs, ups, pages)
    if shared:
        kv_x = move(kv, across)
        kv_y = move(kv, along)
        second = jnp.concatenate(
            [lax.dynamic_slice_in_dim(second_feed_weight, turn * unit, unit, 0)]
            + [jnp.pad(jnp.stack(three_parts(first_feed_bias)), ((0, 13), (0, 0)))],
            axis=0,
        )
        second, _ = lax.optimization_barrier((second, kv))
        second = lax.all_gather(second, "mp", axis=0)
        step = functools.partial(attend, *args, bases)
        state = step(bases, q, [kv], None, False, pages)
        kv_x, kv_y, state, first = lax.optimization_barrier((kv_x, kv_y, state, first))
        kv_d0 = move(kv_y[:pages], across)
        kv_d1 = move(kv_x[pages:], along)
        first_x = move(first, across)
        first_y = move(first, along)
        out_rows = attention_out_weight.shape[0] // 2
        out_half = lax.dynamic_slice_in_dim(
            attention_out_weight, (dp_index % 2) * out_rows, out_rows, 0
        )
        out_half, kv_x = lax.optimization_barrier((out_half, kv_x))
        out_mine = lax.all_gather(out_half, "mp", axis=0)
        near = jnp.stack([at(2), at(3), at(4), at(5)])
        state = step(near, q, [kv_x, kv_y], state, False, pages)
        kv_d0, kv_d1, state = lax.optimization_barrier((kv_d0, kv_d1, state))
        far = jnp.stack([at(6), at(7)])
        context = step(far, q, [kv_d0, kv_d1], state, True, pages)
        context, first_x, first_y, second, out_mine = lax.optimization_barrier(
            (context, first_x, first_y, second, out_mine)
        )
        cut = width // 2
        first_d0 = move(first_y[:, :cut], across)
        first_d1 = move(first_x[:, cut:], along)
        first_near = [move(piece, swap) for piece in (first, first_x, first_y)]
        bias_rows = second[:, unit:]
        second = second[:, :unit]
        second_x = move(second, across)
        second_y = move(second, along)
        context = jnp.concatenate(
            [context[:tok_rows], move(context[tok_rows:], swap)], axis=1
        )
        contexts = lax.all_gather(context, "mp", axis=0)
        out_other = move(out_mine, swap)
        firsts = [first, first_x, first_y, first_d0, first_d1]
        first_others = first_near + [move(first_d0, swap), move(first_d1, swap)]
        half = unit // 2
        second_d0 = move(second_y[:, :half], across)
        second_d1 = move(second_x[:, half:], along)
        seconds = [second, second_x, second_y, second_d0, second_d1]
        second_others = [move(piece, swap) for piece in seconds]
        sets = [(firsts, seconds), (first_others, second_others)]
        outs = [out_mine, out_other]
    else:
        everything = lax.all_gather(kv, "dp", axis=0, tiled=True)
        context = attend(
            *args, bases, jnp.zeros((1,), jnp.int32), q, [everything], None, True, pages
        )
        bias_rows = jnp.pad(jnp.stack(three_parts(first_feed_bias)), ((0, 13), (0, 0)))
        second = lax.all_gather(second_feed_weight, "mp", axis=0)
        bias_rows = lax.all_gather(bias_rows, "mp", axis=0)
        sets = [([lax.all_gather(first_feed_weight, "mp", axis=0)], [second])]
        outs = [lax.all_gather(attention_out_weight, "mp", axis=0)]
        contexts = lax.all_gather(context, "mp", axis=0)
    normed = mix(tokens, contexts, outs, first_norm_gain, first_norm_bias)
    layer_rows, next_proj = feed(
        place, normed, bias_rows, sets, second_feed_bias, second_norm_gain,
        second_norm_bias, following_qkv_weight, following_bias, tok_rows // mp_count,
    )
    return (layer_rows, next_proj)


def solution(mesh):
    placed = (
        P("dp", None),
        P(None, "mp"),
        P(None, "mp"),
        P("mp", None),
        P("mp", None),
        P(),
        P(),
        P(None, "mp"),
        P("mp"),
        P("mp", None),
        P(),
        P(),
        P(),
        P(None, "mp"),
        P("mp"),
        P(),
        P(),
        P(),
    )
    return jax.shard_map(
        local,
        mesh=mesh,
        in_specs=placed,
        out_specs=(P(("dp", "mp"), None), P("dp", "mp")),
        check_vma=False,
    )
```

```python
import functools
import math

import jax
import jax.numpy as jnp
from jax import lax
from jax.experimental import pallas as pl
from jax.experimental.pallas import tpu as pltpu
from jax.sharding import PartitionSpec as P

HEAD_DIM = 64
ADAPTER_RANK = 16
PAGE = 128
PAIR = 2 * HEAD_DIM
NEG = -1e30
EXP_SCALE = math.log2(math.e) * HEAD_DIM**-0.5
MIB = 1 << 20


def params(vmem=48):
    return pltpu.CompilerParams(
        dimension_semantics=("arbitrary",), vmem_limit_bytes=vmem * MIB
    )


def request_of(k, counts, requests):
    end = counts[0]
    request = (k >= end).astype(jnp.int32)
    for r in range(1, requests - 1):
        end = end + counts[r]
        request = request + (k >= end).astype(jnp.int32)
    return request


def normalize(values, gain_row, bias_row):
    average = jnp.mean(values, axis=-1, keepdims=True)
    centered = values - average
    variance = jnp.mean(centered * centered, axis=-1, keepdims=True)
    return centered * lax.rsqrt(variance + 1e-05) * gain_row + bias_row


def project_kernel(
    counts, table, owners, bases, *refs, requests, slots, pages, per_piece, parts,
):
    x_refs = refs[:parts]
    w_ref, down_ref, up_ref, q_ref = refs[parts : parts + 4]
    kv_refs = refs[parts + 4 : 2 * parts + 4]
    joined, page_owner = refs[2 * parts + 4 :]
    step = pl.program_id(0)
    cols = w_ref.shape[1]

    @pl.when(step == 0)
    def _():
        joined[:, :cols] = w_ref[...]
        joined[:, cols:] = down_ref[...]

        def fill(k, carry):
            page_owner[table[k]] = owners[request_of(k, counts, requests)]
            return carry

        lax.fori_loop(0, slots, fill, 0)

    piece = step * pages // per_piece

    def block(x_ref, kv_ref):
        both = jnp.dot(x_ref[...], joined[...], preferred_element_type=jnp.float32)
        low = both[:, cols:]
        lane_owner = lax.broadcasted_iota(jnp.int32, (PAGE, low.shape[1]), 1) // ADAPTER_RANK
        kept = []
        for p in range(pages):
            page = step * pages + p
            slot = bases[page // per_piece] + page % per_piece
            kept.append(
                jnp.where(lane_owner == page_owner[slot], low[p * PAGE : (p + 1) * PAGE], 0.0)
            )
        low_rank = jnp.concatenate(kept, axis=0).astype(jnp.bfloat16)
        rows = both[:, :cols] + jnp.dot(
            low_rank, up_ref[...], preferred_element_type=jnp.float32
        )
        rows = rows.astype(jnp.bfloat16)
        q_cols = q_ref.shape[1]
        q_ref[...] = rows[:, :q_cols]
        keys = rows[:, q_cols : 2 * q_cols]
        values = rows[:, 2 * q_cols :]
        for p in range(pages):
            here = slice(p * PAGE, (p + 1) * PAGE)
            kv_ref[p, :PAIR, :] = keys[here].T
            kv_ref[p, PAIR:, :] = values[here]

    for i in range(parts):
        pl.when(piece == i)(functools.partial(block, x_refs[i], kv_refs[i]))


def project(counts, table, owners, bases, xs, weight, down, up, per_piece):
    tok, width = xs[0].shape
    cols = weight.shape[1]
    pages = 2
    rows_step = pages * PAGE
    slots = table.shape[0]
    parts = len(xs)
    each = tok // rows_step
    total = tok * parts
    whole = lambda i, *_: (0, 0)
    rows = lambda i, *_: (i, 0)

    def own(part, *zeros):
        return lambda i, *_: (jnp.clip(i - part * each, 0, each - 1), 0, *zeros)

    return pl.pallas_call(
        functools.partial(
            project_kernel,
            requests=counts.shape[0], slots=slots, pages=pages, per_piece=per_piece, parts=parts,
        ),
        grid_spec=pltpu.PrefetchScalarGridSpec(
            num_scalar_prefetch=4,
            grid=(total // rows_step,),
            in_specs=[pl.BlockSpec((rows_step, width), own(i)) for i in range(parts)]
            + [
                pl.BlockSpec(weight.shape, whole),
                pl.BlockSpec(down.shape, whole),
                pl.BlockSpec(up.shape, whole),
            ],
            out_specs=[
                pl.BlockSpec((rows_step, cols // 3), rows),
            ]
            + [pl.BlockSpec((pages, PAIR + PAGE, PAIR), own(i, 0)) for i in range(parts)],
            scratch_shapes=[
                pltpu.VMEM((width, cols + down.shape[1]), jnp.bfloat16),
                pltpu.SMEM((slots,), jnp.int32),
            ],
        ),
        out_shape=[
            jax.ShapeDtypeStruct((total, cols // 3), jnp.bfloat16),
        ]
        + [jax.ShapeDtypeStruct((tok // PAGE, PAIR + PAGE, PAIR), jnp.bfloat16)] * parts,
        compiler_params=params(),
        cost_estimate=pl.CostEstimate(
            flops=2 * total * width * cols, bytes_accessed=2 * total * (width + cols),
            transcendentals=0,
        ),
        name="project",
    )(counts, table, owners, bases, *xs, weight, down, up)


def attend_kernel(
    counts, table, q_bases, kv_bases, q_ref, *refs,
    requests, slots, q_size, arrays, sizes, first, last, group,
):
    refs = list(refs)
    kv_hbm = [refs.pop(0) for _ in arrays]
    if not first:
        acc_in, stat_in = refs.pop(0), refs.pop(0)
    if last:
        out_ref = refs.pop(0)
    else:
        acc_out, stat_out = refs.pop(0), refs.pop(0)
    kv, scores, listed, amount, asked, q_amount, sems = refs
    copies = []
    offset = 0
    for i, size in enumerate(arrays):
        copy = pltpu.make_async_copy(kv_hbm[i], kv.at[pl.ds(offset, size)], sems.at[i])
        copy.start()
        copies.append(copy)
        offset += size
    for r in range(requests):
        amount[r] = 0
        q_amount[r] = 0

    def place_of(slot, bases, extents):
        place = jnp.int32(-1)
        offset = 0
        for i, size in enumerate(extents):
            near = slot - bases[i]
            place = jnp.where((near >= 0) & (near < size), near + offset, place)
            offset += size
        return place

    q_sizes = (q_size,) * (q_ref.shape[0] // (q_size * PAGE))

    def fill(k, carry):
        r = request_of(k, counts, requests)
        slot = table[k]
        place = place_of(slot, kv_bases, sizes)
        q_place = place_of(slot, q_bases, q_sizes)

        @pl.when(place >= 0)
        def _():
            n = amount[r]
            listed[r, n] = place
            amount[r] = n + 1

        @pl.when(q_place >= 0)
        def _():
            n = q_amount[r]
            asked[r, n] = q_place
            q_amount[r] = n + 1

        return carry

    lax.fori_loop(0, slots, fill, 0)
    for copy in copies:
        copy.wait()
    lane = lax.broadcasted_iota(jnp.int32, (PAGE, PAIR), 1)
    low_lane = lane < HEAD_DIM
    rows = 4 * PAGE

    def one_pair(r, p):
        n = amount[r]
        full = n // group
        blocks = (n + group - 1) // group
        count = q_amount[r]
        a = asked[r, 2 * p]
        b = asked[r, jnp.minimum(2 * p + 1, count - 1)]
        spots = [pl.ds(pl.multiple_of(t * PAGE, PAGE), PAGE) for t in (a, b)]
        parts = []
        for spot in spots:
            q = q_ref[spot, :]
            zero = jnp.zeros_like(q)
            parts += [jnp.where(low_lane, q, zero), jnp.where(low_lane, zero, q)]
        stacked = jnp.concatenate(parts, axis=0)

        def page_of(j, i):
            return listed[r, jnp.minimum(j * group + i, n - 1)]

        def score(masked, j, top):
            keys = jnp.concatenate(
                [kv[page_of(j, i), :PAIR, :] for i in range(group)], axis=1
            )
            s = jnp.dot(stacked, keys, preferred_element_type=jnp.float32)
            for i in range(group):
                piece = s[:, i * PAGE : (i + 1) * PAGE]
                if masked and i:
                    piece = jnp.where(j * group + i < n, piece, NEG)
                scores[j, :, i * PAGE : (i + 1) * PAGE] = piece
                top = jnp.maximum(top, piece)
            return top

        top = jnp.full((rows, PAGE), NEG, jnp.float32)
        top = lax.fori_loop(0, full, functools.partial(score, False), top)
        top = lax.fori_loop(full, blocks, functools.partial(score, True), top)
        peak = jnp.max(top, axis=1, keepdims=True)
        if not first:
            old = jnp.concatenate(
                [stat_in[spot, h : h + 1] for spot in spots for h in (0, 1)], axis=0
            )
            peak = jnp.maximum(peak, old)
        shift = peak * EXP_SCALE

        def weigh(j, carry):
            total, acc = carry
            w = jnp.exp2(scores[j] * EXP_SCALE - shift)
            for i in range(group):
                total = total + w[:, i * PAGE : (i + 1) * PAGE]
            values = jnp.concatenate(
                [kv[page_of(j, i), PAIR:, :] for i in range(group)], axis=0
            )
            acc = acc + jnp.dot(
                w.astype(jnp.bfloat16), values, preferred_element_type=jnp.float32
            )
            return total, acc

        total, acc = lax.fori_loop(
            0, blocks, weigh,
            (jnp.zeros((rows, PAGE), jnp.float32), jnp.zeros((rows, PAIR), jnp.float32)),
        )
        total = jnp.sum(total, axis=1, keepdims=True)
        if not first:
            shrink = jnp.exp2((old - peak) * EXP_SCALE)
            total = total + shrink * jnp.concatenate(
                [stat_in[spot, h : h + 1] for spot in spots for h in (2, 3)], axis=0
            )
        for t, spot in enumerate(spots):
            h0 = slice(2 * t * PAGE, (2 * t + 1) * PAGE)
            h1 = slice((2 * t + 1) * PAGE, (2 * t + 2) * PAGE)
            value = jnp.where(low_lane, acc[h0], acc[h1])
            if not first:
                value = value + acc_in[spot, :] * jnp.where(low_lane, shrink[h0], shrink[h1])
            if last:
                value = value / jnp.where(low_lane, total[h0], total[h1])
                out_ref[spot, :] = value.astype(jnp.bfloat16)
            else:
                acc_out[spot, :] = value
                stat = jnp.where(lane == 0, peak[h0], peak[h1])
                stat = jnp.where(lane == 2, total[h0], stat)
                stat_out[spot, :] = jnp.where(lane == 3, total[h1], stat)

    def visit_request(r, carry):
        def visit(p, inner):
            one_pair(r, p)
            return inner

        return lax.fori_loop(0, (q_amount[r] + 1) // 2, visit, carry)

    lax.fori_loop(0, requests, visit_request, 0)


def attend(counts, table, q_bases, kv_bases, q, pieces, state, last, q_size):
    tok = q.shape[0]
    arrays = tuple(p.shape[0] for p in pieces)
    sizes = (sum(arrays) // kv_bases.shape[0],) * kv_bases.shape[0]
    first = state is None
    group = 4
    slots = table.shape[0]
    requests = counts.shape[0]
    most = min(sum(sizes), slots)
    vmem = pl.BlockSpec(memory_space=pltpu.VMEM)
    state_shape = [jax.ShapeDtypeStruct((tok, PAIR), jnp.float32)] * 2
    out = pl.pallas_call(
        functools.partial(
            attend_kernel,
            requests=requests, slots=slots, q_size=q_size, arrays=arrays, sizes=sizes,
            first=first, last=last, group=group,
        ),
        grid_spec=pltpu.PrefetchScalarGridSpec(
            num_scalar_prefetch=4,
            grid=(1,),
            in_specs=[pl.BlockSpec((tok, PAIR), lambda i, *_: (0, 0))]
            + [pl.BlockSpec(memory_space=pl.ANY)] * len(pieces)
            + ([] if first else [pl.BlockSpec((tok, PAIR), lambda i, *_: (0, 0))] * 2),
            out_specs=[pl.BlockSpec((tok, PAIR), lambda i, *_: (0, 0))] * (1 if last else 2),
            scratch_shapes=[
                pltpu.VMEM((sum(sizes), PAIR + PAGE, PAIR), jnp.bfloat16),
                pltpu.VMEM(((most + group - 1) // group, 4 * PAGE, group * PAGE), jnp.float32),
                pltpu.SMEM((requests, sum(sizes)), jnp.int32),
                pltpu.SMEM((requests,), jnp.int32),
                pltpu.SMEM((requests, tok // PAGE), jnp.int32),
                pltpu.SMEM((requests,), jnp.int32),
                pltpu.SemaphoreType.DMA((len(pieces),)),
            ],
        ),
        out_shape=[jax.ShapeDtypeStruct((tok, PAIR), jnp.bfloat16)] if last else state_shape,
        compiler_params=params(),
        cost_estimate=pl.CostEstimate(
            flops=tok * PAIR, bytes_accessed=4 * tok * PAIR, transcendentals=0,
        ),
        name="attend",
    )(counts, table, q_bases, kv_bases, q, *pieces, *([] if first else state))
    return out[0] if last else out


def mix_kernel(x_ref, ctx_ref, *refs, parts):
    out_w_refs = refs[:parts]
    gain_ref, bias_ref, out_ref, joined = refs[parts:]

    @pl.when(pl.program_id(0) == 0)
    def _():
        near = joined.shape[1] // parts
        for i in range(parts):
            joined[:, i * near : (i + 1) * near] = out_w_refs[i][:, :near]

    mixed = x_ref[...].astype(jnp.float32)
    for j in range(ctx_ref.shape[0]):
        mixed = mixed + jnp.dot(ctx_ref[j], joined[j], preferred_element_type=jnp.float32)
    out_ref[...] = normalize(mixed, gain_ref[...], bias_ref[...]).astype(jnp.bfloat16)


def mix(x, ctx, outs, gain, bias):
    tok, width = x.shape
    groups, _, cols = ctx.shape
    block = 256
    rows = lambda i: (i, 0)
    fixed = lambda i: (0, 0)
    return pl.pallas_call(
        functools.partial(mix_kernel, parts=len(outs)),
        grid=(tok // block,),
        in_specs=[
            pl.BlockSpec((block, width), rows),
            pl.BlockSpec((groups, block, cols), lambda i: (0, i, 0)),
        ]
        + [pl.BlockSpec(w.shape, lambda i: (0, 0, 0)) for w in outs]
        + [pl.BlockSpec((1, width), fixed)] * 2,
        out_specs=pl.BlockSpec((block, width), rows),
        scratch_shapes=[pltpu.VMEM((groups, cols, width), jnp.bfloat16)],
        out_shape=jax.ShapeDtypeStruct((tok, width), jnp.bfloat16),
        compiler_params=params(),
        cost_estimate=pl.CostEstimate(
            flops=2 * tok * width * groups * cols, bytes_accessed=8 * tok * width, transcendentals=0
        ),
        name="mix",
    )(x, ctx, *outs, gain[None], bias[None])


def feed_kernel(place, normed_ref, bias_ref, *refs, counts, last_step):
    refs = list(refs)
    sets = []
    for n1, n2 in counts:
        w1s, refs = refs[:n1], refs[n1:]
        w2s, refs = refs[:n2], refs[n2:]
        sets.append((w1s, w2s))
    b2_ref, gain_ref, bias2_ref, next_w_ref, next_b_ref = refs[:5]
    layer_ref, next_ref, acc, done = refs[5:]
    step = pl.program_id(0)
    tok = normed_ref.shape[0]
    block = min(256, tok)
    halves = len(sets)
    groups = (last_step + 1) // halves

    @pl.when(step == 0)
    def _():
        acc[...] = jnp.zeros_like(acc)

    def absorb(h, w1_refs, w2_refs):
        if len(w1_refs) == 1:
            w1 = w1_refs[0][0]
            starts, cols = [0], w1.shape[1]
        else:
            diagonal = jnp.concatenate([w1_refs[3][0], w1_refs[4][0]], axis=0)
            w1 = jnp.concatenate([ref[0] for ref in w1_refs[:3]] + [diagonal], axis=1)
            cols = diagonal.shape[1]
            core = place[2] if h == 0 else 1 - place[2]
            starts = [
                pl.multiple_of((core * 4 + (place[1] ^ r)) * cols, cols) for r in range(4)
            ]
        w2 = jnp.concatenate([ref[0] for ref in w2_refs], axis=0)
        bias = jnp.concatenate(
            [
                jnp.sum(
                    bias_ref[0, :, pl.ds(start, cols)].astype(jnp.float32), axis=0, keepdims=True
                )
                for start in starts
            ],
            axis=1,
        )
        for t in range(tok // block):
            rows = slice(t * block, (t + 1) * block)
            pre = jnp.dot(normed_ref[rows, :], w1, preferred_element_type=jnp.float32) + bias
            hidden = 0.5 * pre * (1.0 + lax.erf(pre * math.sqrt(0.5)))
            acc[rows, :] += jnp.dot(
                hidden.astype(jnp.bfloat16), w2, preferred_element_type=jnp.float32
            )

    for h in range(halves):
        pl.when(step // groups == h)(functools.partial(absorb, h, *sets[h]))

    @pl.when(step == last_step)
    def _():
        for t in range(tok // block):
            rows = slice(t * block, (t + 1) * block)
            total = normed_ref[rows, :].astype(jnp.float32) + acc[rows, :] + b2_ref[...]
            layer = normalize(total, gain_ref[...], bias2_ref[...]).astype(jnp.bfloat16)
            done[rows, :] = layer
            next_ref[rows, :] = (
                jnp.dot(layer, next_w_ref[...], preferred_element_type=jnp.float32)
                + next_b_ref[...]
            ).astype(jnp.bfloat16)
        share = layer_ref.shape[0]
        layer_ref[...] = done[pl.ds(pl.multiple_of(place[0] * share, share), share), :]


def feed(place, normed, bias, sets, b2, gain, bias2, next_w, next_b, share):
    tok, width = normed.shape
    halves = len(sets)
    groups = bias.shape[0]
    cols = bias.shape[2] // halves
    steps = halves * groups
    fixed = lambda i, *_: (0, 0)
    specs, arrays = [], []
    for h, (w1s, w2s) in enumerate(sets):
        at = lambda i, *_, h=h: (jnp.clip(i - h * groups, 0, groups - 1), 0, 0)
        for array in (*w1s, *w2s):
            specs.append(pl.BlockSpec((1,) + array.shape[1:], at))
            arrays.append(array)
    next_cols = next_w.shape[1]
    return pl.pallas_call(
        functools.partial(
            feed_kernel,
            counts=tuple((len(w1s), len(w2s)) for w1s, w2s in sets),
            last_step=steps - 1,
        ),
        grid_spec=pltpu.PrefetchScalarGridSpec(
            num_scalar_prefetch=1,
            grid=(steps,),
            in_specs=[
                pl.BlockSpec((tok, width), fixed),
                pl.BlockSpec(
                    (1, 16, bias.shape[2]),
                    lambda i, *_: (i % groups, bias.shape[1] // 16 - 1, 0),
                ),
            ]
            + specs
            + [
                pl.BlockSpec((1, width), fixed),
                pl.BlockSpec((1, width), fixed),
                pl.BlockSpec((1, width), fixed),
                pl.BlockSpec((width, next_cols), fixed),
                pl.BlockSpec((1, next_cols), fixed),
            ],
            out_specs=[
                pl.BlockSpec((share, width), fixed),
                pl.BlockSpec((tok, next_cols), fixed),
            ],
            scratch_shapes=[
                pltpu.VMEM((tok, width), jnp.float32),
                pltpu.VMEM((tok, width), jnp.bfloat16),
            ],
        ),
        out_shape=[
            jax.ShapeDtypeStruct((share, width), jnp.bfloat16),
            jax.ShapeDtypeStruct((tok, next_cols), jnp.bfloat16),
        ],
        compiler_params=params(),
        cost_estimate=pl.CostEstimate(
            flops=4 * tok * width * cols * steps, bytes_accessed=4 * width * cols * steps,
            transcendentals=tok * cols * steps,
        ),
        name="feed",
    )(
        place, normed, bias, *arrays,
        b2[None], gain[None], bias2[None], next_w, next_b[None],
    )


def three_parts(values):
    high = lax.reduce_precision(values, 8, 7)
    middle = lax.reduce_precision(values - high, 8, 7)
    rest = values - high - middle
    return [part.astype(jnp.bfloat16) for part in (high, middle, rest)]


def local(
    tokens,
    query_key_value_weight,
    adapter_down_weight,
    adapter_up_weight,
    attention_out_weight,
    first_norm_gain,
    first_norm_bias,
    first_feed_weight,
    first_feed_bias,
    second_feed_weight,
    second_feed_bias,
    second_norm_gain,
    second_norm_bias,
    following_qkv_weight,
    following_bias,
    request_page_count,
    page_slot_table,
    request_adapter,
):
    tok_rows, width = tokens.shape
    dp_count = lax.axis_size("dp")
    mp_count = lax.axis_size("mp")
    dp_index = lax.axis_index("dp")
    mp_index = lax.axis_index("mp")
    kept_values = adapter_down_weight.shape[1] // ADAPTER_RANK
    heads_dev = query_key_value_weight.shape[1] // (3 * HEAD_DIM)
    pages = tok_rows // PAGE
    shared = dp_count == 8 and heads_dev == 4

    owners = request_adapter // kept_values
    level = jnp.sum(jnp.where(owners == mp_index, request_adapter % kept_values, 0))
    down = lax.dynamic_slice_in_dim(
        adapter_down_weight, level * ADAPTER_RANK, ADAPTER_RANK, 1
    )
    up = lax.dynamic_slice_in_dim(adapter_up_weight, level * ADAPTER_RANK, ADAPTER_RANK, 0)
    up_cols = up.shape[1] // mp_count
    sent = jnp.concatenate(
        [
            jnp.broadcast_to(down.T[:, None, :], (ADAPTER_RANK, mp_count, width)),
            up.reshape(ADAPTER_RANK, mp_count, up_cols),
        ],
        axis=2,
    ).reshape(ADAPTER_RANK, mp_count * (width + up_cols))
    got = lax.all_to_all(sent, "mp", split_axis=1, concat_axis=0, tiled=True)

    def by_kind(matrix):
        split = matrix.reshape(matrix.shape[0], heads_dev, 3, HEAD_DIM)
        if shared:
            split = lax.dynamic_slice_in_dim(split, (dp_index % 2) * 2, 2, 1)
        return jnp.swapaxes(split, 1, 2).reshape(matrix.shape[0], -1)

    place = jnp.stack(
        [mp_index] + ([dp_index // 2, dp_index % 2] if shared else [0, 0])
    ).astype(jnp.int32)
    hidden_dev = first_feed_weight.shape[1]
    downs = got[:, :width].T
    ups = got[:, width:]
    weight = by_kind(query_key_value_weight)
    ups = by_kind(ups)
    if shared:
        swap = [(i, i ^ 1) for i in range(8)]
        across = [(i, i ^ 2) for i in range(8)]
        along = [(i, i ^ 4) for i in range(8)]
        move = lambda value, pairs: lax.ppermute(value, "dp", pairs)
        xs = [tokens, move(tokens, swap)]
        at = lambda flip: (dp_index ^ flip) * pages
        bases = jnp.stack([at(0), at(1)])
    else:
        xs = [tokens]
        bases = jnp.stack([dp_index * pages])
    args = (request_page_count, page_slot_table)
    q, *kvs = project(*args, owners, bases, xs, weight, downs, ups, pages)
    bias_rows = jnp.pad(jnp.stack(three_parts(first_feed_bias)), ((0, 13), (0, 0)))
    out_rows = attention_out_weight.shape[0]
    if shared:
        unit = hidden_dev // 8
        turn = (dp_index % 2) * 4 + dp_index // 2
        kv_x = [move(kv, across) for kv in kvs]
        kv_y = [move(kv, along) for kv in kvs]
        first = lax.dynamic_slice_in_dim(first_feed_weight, turn * unit, unit, 1)
        first, kvs = lax.optimization_barrier((first, kvs))
        first = lax.all_gather(first, "mp", axis=0)
        step = functools.partial(attend, *args, bases)
        state = step(bases, q, kvs, None, False, pages)
        second = lax.dynamic_slice_in_dim(second_feed_weight, turn * unit, unit, 0)
        out_half = jnp.concatenate(
            [
                lax.dynamic_slice_in_dim(
                    attention_out_weight, (dp_index % 2) * (out_rows // 2), out_rows // 2, 0
                ),
                bias_rows,
            ],
            axis=0,
        )
        kv_x, kv_y, state, first, second, out_half = lax.optimization_barrier(
            (kv_x, kv_y, state, first, second, out_half)
        )
        second = lax.all_gather(second, "mp", axis=0)
        out_mine = lax.all_gather(out_half, "mp", axis=0)
        kv_d0 = move(kv_y[0], across)
        kv_d1 = move(kv_x[1], along)
        first_x = move(first, across)
        first_y = move(first, along)
        near = jnp.stack([at(2), at(3), at(4), at(5)])
        state = step(near, q, [*kv_x, *kv_y], state, False, pages)
        kv_d0, kv_d1, first_x, first_y, state = lax.optimization_barrier(
            (kv_d0, kv_d1, first_x, first_y, state)
        )
        cut = width // 2
        first_d0 = move(first_y[:, :cut], across)
        first_d1 = move(first_x[:, cut:], along)
        far = jnp.stack([at(6), at(7)])
        near_others = [move(piece, swap) for piece in (first, first_x, first_y)]
        context = step(far, q, [kv_d0, kv_d1], state, True, pages)
        context, first_d0, first_d1, near_others, second, out_mine = lax.optimization_barrier(
            (context, first_d0, first_d1, near_others, second, out_mine)
        )
        second_x = move(second, across)
        second_y = move(second, along)
        context = jnp.concatenate(
            [context[:tok_rows], move(context[tok_rows:], swap)], axis=1
        )
        contexts = lax.all_gather(context, "mp", axis=0)
        bias_rows = out_mine
        firsts = [first, first_x, first_y, first_d0, first_d1]
        moved = [move(piece, swap) for piece in (first_d0, first_d1, second, out_mine)]
        second_x, second_y, moved = lax.optimization_barrier((second_x, second_y, moved))
        first_others = [*near_others, *moved[:2]]
        out_other = moved[3]
        half = unit // 2
        second_d0 = move(second_y[:, :half], across)
        second_d1 = move(second_x[:, half:], along)
        seconds = [second, second_x, second_y, second_d0, second_d1]
        second_others = [moved[2]] + [move(piece, swap) for piece in seconds[1:]]
        sets = [(firsts, seconds), (first_others, second_others)]
        outs = [out_mine, out_other]
    else:
        everything = lax.all_gather(kvs[0], "dp", axis=0, tiled=True)
        context = attend(
            *args, bases, jnp.zeros((1,), jnp.int32), q, [everything], None, True, pages
        )
        second = lax.all_gather(second_feed_weight, "mp", axis=0)
        bias_rows = lax.all_gather(bias_rows, "mp", axis=0)
        sets = [([lax.all_gather(first_feed_weight, "mp", axis=0)], [second])]
        outs = [lax.all_gather(attention_out_weight, "mp", axis=0)]
        contexts = lax.all_gather(context, "mp", axis=0)
    normed = mix(tokens, contexts, outs, first_norm_gain, first_norm_bias)
    layer_rows, next_proj = feed(
        place, normed, bias_rows, sets, second_feed_bias, second_norm_gain,
        second_norm_bias, following_qkv_weight, following_bias, tok_rows // mp_count,
    )
    return (layer_rows, next_proj)


def solution(mesh):
    placed = (
        P("dp", None),
        P(None, "mp"),
        P(None, "mp"),
        P("mp", None),
        P("mp", None),
        P(),
        P(),
        P(None, "mp"),
        P("mp"),
        P("mp", None),
        P(),
        P(),
        P(),
        P(None, "mp"),
        P("mp"),
        P(),
        P(),
        P(),
    )
    return jax.shard_map(
        local,
        mesh=mesh,
        in_specs=placed,
        out_specs=(P(("dp", "mp"), None), P("dp", "mp")),
        check_vma=False,
    )
```

```python
import functools
import math

import jax
import jax.numpy as jnp
from jax import lax
from jax.experimental import pallas as pl
from jax.experimental.pallas import tpu as pltpu
from jax.sharding import PartitionSpec as P

HEAD_DIM = 64
ADAPTER_RANK = 16
PAGE = 128
PAIR = 2 * HEAD_DIM
NEG = -1e30
EXP_SCALE = math.log2(math.e) * HEAD_DIM**-0.5
MIB = 1 << 20


def params(vmem):
    return pltpu.CompilerParams(
        dimension_semantics=("arbitrary",), vmem_limit_bytes=vmem * MIB
    )


def request_of(k, counts, requests):
    end = counts[0]
    request = (k >= end).astype(jnp.int32)
    for r in range(1, requests - 1):
        end = end + counts[r]
        request = request + (k >= end).astype(jnp.int32)
    return request


def normalize(values, gain_row, bias_row):
    average = jnp.mean(values, axis=-1, keepdims=True)
    centered = values - average
    variance = jnp.mean(centered * centered, axis=-1, keepdims=True)
    return centered * lax.rsqrt(variance + 1e-05) * gain_row + bias_row


def project_kernel(
    counts, table, owners, bases, *refs, requests, slots, pages, per_piece, parts,
):
    x_refs = refs[:parts]
    w_ref, down_ref, up_ref, q_ref = refs[parts : parts + 4]
    kv_refs = refs[parts + 4 : 2 * parts + 4]
    joined, page_owner = refs[2 * parts + 4 :]
    step = pl.program_id(0)
    cols = w_ref.shape[1]

    @pl.when(step == 0)
    def _():
        joined[:, :cols] = w_ref[...]
        joined[:, cols:] = down_ref[...]

        def fill(k, carry):
            page_owner[table[k]] = owners[request_of(k, counts, requests)]
            return carry

        lax.fori_loop(0, slots, fill, 0)

    piece = step * pages // per_piece

    def block(x_ref, kv_ref):
        both = jnp.dot(x_ref[...], joined[...], preferred_element_type=jnp.float32)
        low = both[:, cols:]
        lane_owner = lax.broadcasted_iota(jnp.int32, (PAGE, low.shape[1]), 1) // ADAPTER_RANK
        kept = []
        for p in range(pages):
            page = step * pages + p
            slot = bases[page // per_piece] + page % per_piece
            kept.append(
                jnp.where(lane_owner == page_owner[slot], low[p * PAGE : (p + 1) * PAGE], 0.0)
            )
        low_rank = jnp.concatenate(kept, axis=0).astype(jnp.bfloat16)
        rows = both[:, :cols] + jnp.dot(
            low_rank, up_ref[...], preferred_element_type=jnp.float32
        )
        rows = rows.astype(jnp.bfloat16)
        q_cols = q_ref.shape[1]
        q_ref[...] = rows[:, :q_cols]
        keys = rows[:, q_cols : 2 * q_cols]
        values = rows[:, 2 * q_cols :]
        for p in range(pages):
            here = slice(p * PAGE, (p + 1) * PAGE)
            kv_ref[p, :PAIR, :] = keys[here].T
            kv_ref[p, PAIR:, :] = values[here]

    for i in range(parts):
        pl.when(piece == i)(functools.partial(block, x_refs[i], kv_refs[i]))


def project(counts, table, owners, bases, xs, weight, down, up, per_piece):
    tok, width = xs[0].shape
    cols = weight.shape[1]
    pages = 2
    rows_step = pages * PAGE
    slots = table.shape[0]
    parts = len(xs)
    each = tok // rows_step
    total = tok * parts
    whole = lambda i, *_: (0, 0)
    rows = lambda i, *_: (i, 0)

    def own(part, *zeros):
        return lambda i, *_: (jnp.clip(i - part * each, 0, each - 1), 0, *zeros)

    return pl.pallas_call(
        functools.partial(
            project_kernel,
            requests=counts.shape[0], slots=slots, pages=pages, per_piece=per_piece, parts=parts,
        ),
        grid_spec=pltpu.PrefetchScalarGridSpec(
            num_scalar_prefetch=4,
            grid=(total // rows_step,),
            in_specs=[pl.BlockSpec((rows_step, width), own(i)) for i in range(parts)]
            + [
                pl.BlockSpec(weight.shape, whole),
                pl.BlockSpec(down.shape, whole),
                pl.BlockSpec(up.shape, whole),
            ],
            out_specs=[
                pl.BlockSpec((rows_step, cols // 3), rows),
            ]
            + [pl.BlockSpec((pages, PAIR + PAGE, PAIR), own(i, 0)) for i in range(parts)],
            scratch_shapes=[
                pltpu.VMEM((width, cols + down.shape[1]), jnp.bfloat16),
                pltpu.SMEM((slots,), jnp.int32),
            ],
        ),
        out_shape=[
            jax.ShapeDtypeStruct((total, cols // 3), jnp.bfloat16),
        ]
        + [jax.ShapeDtypeStruct((tok // PAGE, PAIR + PAGE, PAIR), jnp.bfloat16)] * parts,
        compiler_params=params(62),
        cost_estimate=pl.CostEstimate(
            flops=2 * total * width * cols, bytes_accessed=2 * total * (width + cols),
            transcendentals=0,
        ),
        name="project",
    )(counts, table, owners, bases, *xs, weight, down, up)


def attend_kernel(
    counts, table, q_bases, kv_bases, q_hbm, *refs,
    requests, slots, q_size, arrays, sizes, first, last, group,
):
    refs = list(refs)
    kv_hbm = [refs.pop(0) for _ in arrays]
    state_hbm = [] if first else [refs.pop(0), refs.pop(0)]
    if last:
        out_ref = refs.pop(0)
    else:
        acc_out, stat_out = refs.pop(0), refs.pop(0)
    kv, scores, listed, amount, asked, q_amount, sems, q_ref = refs[:8]
    if not first:
        acc_in, stat_in = refs[8:]
    targets = [(q_hbm, q_ref)]
    offset = 0
    for i, size in enumerate(arrays):
        targets.append((kv_hbm[i], kv.at[pl.ds(offset, size)]))
        offset += size
    targets += list(zip(state_hbm, refs[8:]))
    copies = [
        pltpu.make_async_copy(source, target, sems.at[n])
        for n, (source, target) in enumerate(targets)
    ]
    for copy in copies:
        copy.start()
    for r in range(requests):
        amount[r] = 0
        q_amount[r] = 0

    def place_of(slot, bases, extents):
        place = jnp.int32(-1)
        offset = 0
        for i, size in enumerate(extents):
            near = slot - bases[i]
            place = jnp.where((near >= 0) & (near < size), near + offset, place)
            offset += size
        return place

    q_sizes = (q_size,) * (q_ref.shape[0] // (q_size * PAGE))

    def fill(k, carry):
        r = request_of(k, counts, requests)
        slot = table[k]
        place = place_of(slot, kv_bases, sizes)
        q_place = place_of(slot, q_bases, q_sizes)

        @pl.when(place >= 0)
        def _():
            n = amount[r]
            listed[r, n] = place
            amount[r] = n + 1

        @pl.when(q_place >= 0)
        def _():
            n = q_amount[r]
            asked[r, n] = q_place
            q_amount[r] = n + 1

        return carry

    lax.fori_loop(0, slots, fill, 0)
    for copy in copies:
        copy.wait()
    lane = lax.broadcasted_iota(jnp.int32, (PAGE, PAIR), 1)
    low_lane = lane < HEAD_DIM
    rows = 4 * PAGE

    def one_pair(r, p):
        n = amount[r]
        full = n // group
        blocks = (n + group - 1) // group
        count = q_amount[r]
        a = asked[r, 2 * p]
        b = asked[r, jnp.minimum(2 * p + 1, count - 1)]
        spots = [pl.ds(pl.multiple_of(t * PAGE, PAGE), PAGE) for t in (a, b)]
        parts = []
        for spot in spots:
            q = q_ref[spot, :]
            zero = jnp.zeros_like(q)
            parts += [jnp.where(low_lane, q, zero), jnp.where(low_lane, zero, q)]
        stacked = jnp.concatenate(parts, axis=0)

        def page_of(j, i):
            return listed[r, jnp.minimum(j * group + i, n - 1)]

        def score(masked, j, top):
            keys = jnp.concatenate(
                [kv[page_of(j, i), :PAIR, :] for i in range(group)], axis=1
            )
            s = jnp.dot(stacked, keys, preferred_element_type=jnp.float32)
            for i in range(group):
                piece = s[:, i * PAGE : (i + 1) * PAGE]
                if masked and i:
                    piece = jnp.where(j * group + i < n, piece, NEG)
                scores[j, :, i * PAGE : (i + 1) * PAGE] = piece
                top = jnp.maximum(top, piece)
            return top

        top = jnp.full((rows, PAGE), NEG, jnp.float32)
        top = lax.fori_loop(0, full, functools.partial(score, False), top)
        top = lax.fori_loop(full, blocks, functools.partial(score, True), top)
        peak = jnp.max(top, axis=1, keepdims=True)
        if not first:
            old = jnp.concatenate(
                [stat_in[spot, h : h + 1] for spot in spots for h in (0, 1)], axis=0
            )
            peak = jnp.maximum(peak, old)
        shift = peak * EXP_SCALE

        def weigh(j, carry):
            total, acc = carry
            w = jnp.exp2(scores[j] * EXP_SCALE - shift)
            for i in range(group):
                total = total + w[:, i * PAGE : (i + 1) * PAGE]
            values = jnp.concatenate(
                [kv[page_of(j, i), PAIR:, :] for i in range(group)], axis=0
            )
            acc = acc + jnp.dot(
                w.astype(jnp.bfloat16), values, preferred_element_type=jnp.float32
            )
            return total, acc

        total, acc = lax.fori_loop(
            0, blocks, weigh,
            (jnp.zeros((rows, PAGE), jnp.float32), jnp.zeros((rows, PAIR), jnp.float32)),
        )
        total = jnp.sum(total, axis=1, keepdims=True)
        if not first:
            shrink = jnp.exp2((old - peak) * EXP_SCALE)
            total = total + shrink * jnp.concatenate(
                [stat_in[spot, h : h + 1] for spot in spots for h in (2, 3)], axis=0
            )
        for t, spot in enumerate(spots):
            h0 = slice(2 * t * PAGE, (2 * t + 1) * PAGE)
            h1 = slice((2 * t + 1) * PAGE, (2 * t + 2) * PAGE)
            value = jnp.where(low_lane, acc[h0], acc[h1])
            if not first:
                value = value + acc_in[spot, :] * jnp.where(low_lane, shrink[h0], shrink[h1])
            if last:
                value = value / jnp.where(low_lane, total[h0], total[h1])
                out_ref[spot, :] = value.astype(jnp.bfloat16)
            else:
                acc_out[spot, :] = value
                stat = jnp.where(lane == 0, peak[h0], peak[h1])
                stat = jnp.where(lane == 2, total[h0], stat)
                stat_out[spot, :] = jnp.where(lane == 3, total[h1], stat)

    def visit_request(r, carry):
        def visit(p, inner):
            one_pair(r, p)
            return inner

        return lax.fori_loop(0, (q_amount[r] + 1) // 2, visit, carry)

    lax.fori_loop(0, requests, visit_request, 0)


def attend(counts, table, q_bases, kv_bases, q, pieces, state, last, q_size):
    tok = q.shape[0]
    arrays = tuple(p.shape[0] for p in pieces)
    sizes = (sum(arrays) // kv_bases.shape[0],) * kv_bases.shape[0]
    first = state is None
    group = 4
    slots = table.shape[0]
    requests = counts.shape[0]
    most = min(sum(sizes), slots)
    state_shape = [jax.ShapeDtypeStruct((tok, PAIR), jnp.float32)] * 2
    out = pl.pallas_call(
        functools.partial(
            attend_kernel,
            requests=requests, slots=slots, q_size=q_size, arrays=arrays, sizes=sizes,
            first=first, last=last, group=group,
        ),
        grid_spec=pltpu.PrefetchScalarGridSpec(
            num_scalar_prefetch=4,
            grid=(1,),
            in_specs=[pl.BlockSpec(memory_space=pl.ANY)] * (len(pieces) + (1 if first else 3)),
            out_specs=[pl.BlockSpec((tok, PAIR), lambda i, *_: (0, 0))] * (1 if last else 2),
            scratch_shapes=[
                pltpu.VMEM((sum(sizes), PAIR + PAGE, PAIR), jnp.bfloat16),
                pltpu.VMEM(((most + group - 1) // group, 4 * PAGE, group * PAGE), jnp.float32),
                pltpu.SMEM((requests, sum(sizes)), jnp.int32),
                pltpu.SMEM((requests,), jnp.int32),
                pltpu.SMEM((requests, tok // PAGE), jnp.int32),
                pltpu.SMEM((requests,), jnp.int32),
                pltpu.SemaphoreType.DMA((len(pieces) + 3,)),
                pltpu.VMEM((tok, PAIR), jnp.bfloat16),
            ]
            + ([] if first else [pltpu.VMEM((tok, PAIR), jnp.float32)] * 2),
        ),
        out_shape=[jax.ShapeDtypeStruct((tok, PAIR), jnp.bfloat16)] if last else state_shape,
        compiler_params=params(62),
        cost_estimate=pl.CostEstimate(
            flops=tok * PAIR, bytes_accessed=4 * tok * PAIR, transcendentals=0,
        ),
        name="attend",
    )(counts, table, q_bases, kv_bases, q, *pieces, *([] if first else state))
    return out[0] if last else out


def finish_kernel(place, x_ref, ctx_ref, *refs, parts, counts, last_step):
    refs = list(refs)
    out_w_refs, refs = refs[:parts], refs[parts:]
    gain1_ref, bias1_ref, bias_ref = refs[:3]
    refs = refs[3:]
    sets = []
    for n1, n2 in counts:
        w1s, refs = refs[:n1], refs[n1:]
        w2s, refs = refs[:n2], refs[n2:]
        sets.append((w1s, w2s))
    b2_ref, gain_ref, bias2_ref, next_w_ref, next_b_ref = refs[:5]
    layer_ref, next_ref, joined, normed_ref, acc, done = refs[5:]
    step = pl.program_id(0)
    tok = normed_ref.shape[0]
    block = min(512, tok)
    halves = len(sets)
    groups = (last_step + 1) // halves

    @pl.when(step == 0)
    def _():
        near = joined.shape[1] // parts
        for i in range(parts):
            joined[:, i * near : (i + 1) * near] = out_w_refs[i][:, :near]
        for t in range(tok // block):
            rows = slice(t * block, (t + 1) * block)
            mixed = x_ref[rows, :].astype(jnp.float32)
            for j in range(ctx_ref.shape[0]):
                mixed = mixed + jnp.dot(
                    ctx_ref[j, rows, :], joined[j], preferred_element_type=jnp.float32
                )
            normed = normalize(mixed, gain1_ref[...], bias1_ref[...]).astype(jnp.bfloat16)
            normed_ref[rows, :] = normed
            acc[rows, :] = normed.astype(jnp.float32) + b2_ref[...]

    def absorb(h, w1_refs, w2_refs):
        if len(w1_refs) == 1:
            w1 = w1_refs[0][0]
            starts, cols = [0], w1.shape[1]
        else:
            diagonal = jnp.concatenate([w1_refs[3][0], w1_refs[4][0]], axis=0)
            w1 = jnp.concatenate([ref[0] for ref in w1_refs[:3]] + [diagonal], axis=1)
            cols = diagonal.shape[1]
            core = place[2] if h == 0 else 1 - place[2]
            starts = [
                pl.multiple_of((core * 4 + (place[1] ^ r)) * cols, cols) for r in range(4)
            ]
        w2 = jnp.concatenate([ref[0] for ref in w2_refs], axis=0)
        bias = jnp.concatenate(
            [
                jnp.sum(
                    bias_ref[0, :, pl.ds(start, cols)].astype(jnp.float32), axis=0, keepdims=True
                )
                for start in starts
            ],
            axis=1,
        )
        for t in range(tok // block):
            rows = slice(t * block, (t + 1) * block)
            pre = jnp.dot(normed_ref[rows, :], w1, preferred_element_type=jnp.float32) + bias
            hidden = 0.5 * pre * (1.0 + lax.erf(pre * math.sqrt(0.5)))
            acc[rows, :] += jnp.dot(
                hidden.astype(jnp.bfloat16), w2, preferred_element_type=jnp.float32
            )

    for h in range(halves):
        pl.when(step // groups == h)(functools.partial(absorb, h, *sets[h]))

    @pl.when(step == last_step)
    def _():
        for t in range(tok // block):
            rows = slice(t * block, (t + 1) * block)
            layer = normalize(acc[rows, :], gain_ref[...], bias2_ref[...]).astype(jnp.bfloat16)
            done[rows, :] = layer
            next_ref[rows, :] = (
                jnp.dot(layer, next_w_ref[...], preferred_element_type=jnp.float32)
                + next_b_ref[...]
            ).astype(jnp.bfloat16)
        share = layer_ref.shape[0]
        layer_ref[...] = done[pl.ds(pl.multiple_of(place[0] * share, share), share), :]


def finish(
    place, x, ctx, outs, gain1, bias1, bias, sets, b2, gain, bias2, next_w, next_b, share
):
    tok, width = x.shape
    halves = len(sets)
    groups, _, ctx_cols = ctx.shape
    cols = bias.shape[2] // halves
    steps = halves * groups

    def whole(array):
        return pl.BlockSpec(
            array.shape, lambda i, *_: (0,) * array.ndim, pipeline_mode=pl.Buffered(1)
        )

    specs, arrays = [], []
    for h, (w1s, w2s) in enumerate(sets):
        at = lambda i, *_, h=h: (jnp.clip(i - h * groups, 0, groups - 1), 0, 0)
        for array in (*w1s, *w2s):
            specs.append(pl.BlockSpec((1,) + array.shape[1:], at))
            arrays.append(array)
    head = [x, ctx, *outs, gain1[None], bias1[None]]
    tail = [b2[None], gain[None], bias2[None], next_w, next_b[None]]
    next_cols = next_w.shape[1]
    fixed = lambda i, *_: (0, 0)
    return pl.pallas_call(
        functools.partial(
            finish_kernel,
            parts=len(outs),
            counts=tuple((len(w1s), len(w2s)) for w1s, w2s in sets),
            last_step=steps - 1,
        ),
        grid_spec=pltpu.PrefetchScalarGridSpec(
            num_scalar_prefetch=1,
            grid=(steps,),
            in_specs=[whole(array) for array in head]
            + [
                pl.BlockSpec(
                    (1, 16, bias.shape[2]),
                    lambda i, *_: (i % groups, bias.shape[1] // 16 - 1, 0),
                ),
            ]
            + specs
            + [whole(array) for array in tail],
            out_specs=[
                pl.BlockSpec((share, width), fixed),
                pl.BlockSpec((tok, next_cols), fixed),
            ],
            scratch_shapes=[
                pltpu.VMEM((groups, ctx_cols, width), jnp.bfloat16),
                pltpu.VMEM((tok, width), jnp.bfloat16),
                pltpu.VMEM((tok, width), jnp.float32),
                pltpu.VMEM((tok, width), jnp.bfloat16),
            ],
        ),
        out_shape=[
            jax.ShapeDtypeStruct((share, width), jnp.bfloat16),
            jax.ShapeDtypeStruct((tok, next_cols), jnp.bfloat16),
        ],
        compiler_params=params(62),
        cost_estimate=pl.CostEstimate(
            flops=4 * tok * width * cols * steps, bytes_accessed=4 * width * cols * steps,
            transcendentals=tok * cols * steps,
        ),
        name="finish",
    )(place, *head, bias, *arrays, *tail)


def three_parts(values):
    high = lax.reduce_precision(values, 8, 7)
    middle = lax.reduce_precision(values - high, 8, 7)
    rest = values - high - middle
    return [part.astype(jnp.bfloat16) for part in (high, middle, rest)]


def local(
    tokens,
    query_key_value_weight,
    adapter_down_weight,
    adapter_up_weight,
    attention_out_weight,
    first_norm_gain,
    first_norm_bias,
    first_feed_weight,
    first_feed_bias,
    second_feed_weight,
    second_feed_bias,
    second_norm_gain,
    second_norm_bias,
    following_qkv_weight,
    following_bias,
    request_page_count,
    page_slot_table,
    request_adapter,
):
    tok_rows, width = tokens.shape
    dp_count = lax.axis_size("dp")
    mp_count = lax.axis_size("mp")
    dp_index = lax.axis_index("dp")
    mp_index = lax.axis_index("mp")
    kept_values = adapter_down_weight.shape[1] // ADAPTER_RANK
    heads_dev = query_key_value_weight.shape[1] // (3 * HEAD_DIM)
    pages = tok_rows // PAGE
    shared = dp_count == 8 and heads_dev == 4

    owners = request_adapter // kept_values
    level = jnp.sum(jnp.where(owners == mp_index, request_adapter % kept_values, 0))
    down = lax.dynamic_slice_in_dim(
        adapter_down_weight, level * ADAPTER_RANK, ADAPTER_RANK, 1
    )
    up = lax.dynamic_slice_in_dim(adapter_up_weight, level * ADAPTER_RANK, ADAPTER_RANK, 0)
    up_cols = up.shape[1] // mp_count
    sent = jnp.concatenate(
        [
            jnp.broadcast_to(down.T[:, None, :], (ADAPTER_RANK, mp_count, width)),
            up.reshape(ADAPTER_RANK, mp_count, up_cols),
        ],
        axis=2,
    ).reshape(ADAPTER_RANK, mp_count * (width + up_cols))
    got = lax.all_to_all(sent, "mp", split_axis=1, concat_axis=0, tiled=True)

    def by_kind(matrix):
        split = matrix.reshape(matrix.shape[0], heads_dev, 3, HEAD_DIM)
        if shared:
            split = lax.dynamic_slice_in_dim(split, (dp_index % 2) * 2, 2, 1)
        return jnp.swapaxes(split, 1, 2).reshape(matrix.shape[0], -1)

    place = jnp.stack(
        [mp_index] + ([dp_index // 2, dp_index % 2] if shared else [0, 0])
    ).astype(jnp.int32)
    hidden_dev = first_feed_weight.shape[1]
    downs = got[:, :width].T
    ups = got[:, width:]
    weight = by_kind(query_key_value_weight)
    ups = by_kind(ups)
    if shared:
        swap = [(i, i ^ 1) for i in range(8)]
        across = [(i, i ^ 2) for i in range(8)]
        along = [(i, i ^ 4) for i in range(8)]
        move = lambda value, pairs: lax.ppermute(value, "dp", pairs)
        xs = [tokens, move(tokens, swap)]
        at = lambda flip: (dp_index ^ flip) * pages
        bases = jnp.stack([at(0), at(1)])
    else:
        xs = [tokens]
        bases = jnp.stack([dp_index * pages])
    args = (request_page_count, page_slot_table)
    q, *kvs = project(*args, owners, bases, xs, weight, downs, ups, pages)
    bias_rows = jnp.pad(jnp.stack(three_parts(first_feed_bias)), ((0, 13), (0, 0)))
    out_rows = attention_out_weight.shape[0]
    if shared:
        unit = hidden_dev // 8
        turn = (dp_index % 2) * 4 + dp_index // 2
        kv_x = [move(kv, across) for kv in kvs]
        kv_y = [move(kv, along) for kv in kvs]
        first = lax.dynamic_slice_in_dim(first_feed_weight, turn * unit, unit, 1)
        first, kvs = lax.optimization_barrier((first, kvs))
        first = lax.all_gather(first, "mp", axis=0)
        step = functools.partial(attend, *args, bases)
        state = step(bases, q, kvs, None, False, pages)
        second = lax.dynamic_slice_in_dim(second_feed_weight, turn * unit, unit, 0)
        out_half = jnp.concatenate(
            [
                lax.dynamic_slice_in_dim(
                    attention_out_weight, (dp_index % 2) * (out_rows // 2), out_rows // 2, 0
                ),
                bias_rows,
            ],
            axis=0,
        )
        kv_x, kv_y, state, first, second, out_half = lax.optimization_barrier(
            (kv_x, kv_y, state, first, second, out_half)
        )
        second = lax.all_gather(second, "mp", axis=0)
        out_mine = lax.all_gather(out_half, "mp", axis=0)
        kv_d0 = move(kv_y[0], across)
        kv_d1 = move(kv_x[1], along)
        first_x = move(first, across)
        first_y = move(first, along)
        near = jnp.stack([at(2), at(3), at(4), at(5)])
        state = step(near, q, [*kv_x, *kv_y], state, False, pages)
        kv_d0, kv_d1, first_x, first_y, state = lax.optimization_barrier(
            (kv_d0, kv_d1, first_x, first_y, state)
        )
        cut = width // 2
        first_d0 = move(first_y[:, :cut], across)
        first_d1 = move(first_x[:, cut:], along)
        far = jnp.stack([at(6), at(7)])
        near_others = [move(piece, swap) for piece in (first, first_x, first_y)]
        context = step(far, q, [kv_d0, kv_d1], state, True, pages)
        context, first_d0, first_d1, near_others, second, out_mine = lax.optimization_barrier(
            (context, first_d0, first_d1, near_others, second, out_mine)
        )
        second_x = move(second, across)
        second_y = move(second, along)
        context = jnp.concatenate(
            [context[:tok_rows], move(context[tok_rows:], swap)], axis=1
        )
        contexts = lax.all_gather(context, "mp", axis=0)
        bias_rows = out_mine
        firsts = [first, first_x, first_y, first_d0, first_d1]
        moved = [move(piece, swap) for piece in (first_d0, first_d1, second, out_mine)]
        second_x, second_y, moved = lax.optimization_barrier((second_x, second_y, moved))
        first_others = [*near_others, *moved[:2]]
        out_other = moved[3]
        half = unit // 2
        second_d0 = move(second_y[:, :half], across)
        second_d1 = move(second_x[:, half:], along)
        seconds = [second, second_x, second_y, second_d0, second_d1]
        second_others = [moved[2]] + [move(piece, swap) for piece in seconds[1:]]
        sets = [(firsts, seconds), (first_others, second_others)]
        outs = [out_mine, out_other]
    else:
        everything = lax.all_gather(kvs[0], "dp", axis=0, tiled=True)
        context = attend(
            *args, bases, jnp.zeros((1,), jnp.int32), q, [everything], None, True, pages
        )
        second = lax.all_gather(second_feed_weight, "mp", axis=0)
        bias_rows = lax.all_gather(bias_rows, "mp", axis=0)
        sets = [([lax.all_gather(first_feed_weight, "mp", axis=0)], [second])]
        outs = [lax.all_gather(attention_out_weight, "mp", axis=0)]
        contexts = lax.all_gather(context, "mp", axis=0)
    layer_rows, next_proj = finish(
        place, tokens, contexts, outs, first_norm_gain, first_norm_bias, bias_rows, sets,
        second_feed_bias, second_norm_gain, second_norm_bias, following_qkv_weight,
        following_bias, tok_rows // mp_count,
    )
    return (layer_rows, next_proj)


def solution(mesh):
    placed = (
        P("dp", None),
        P(None, "mp"),
        P(None, "mp"),
        P("mp", None),
        P("mp", None),
        P(),
        P(),
        P(None, "mp"),
        P("mp"),
        P("mp", None),
        P(),
        P(),
        P(),
        P(None, "mp"),
        P("mp"),
        P(),
        P(),
        P(),
    )
    return jax.shard_map(
        local,
        mesh=mesh,
        in_specs=placed,
        out_specs=(P(("dp", "mp"), None), P("dp", "mp")),
        check_vma=False,
    )
```

```python
import functools
import math

import jax
import jax.numpy as jnp
from jax import lax
from jax.experimental import pallas as pl
from jax.experimental.pallas import tpu as pltpu
from jax.sharding import PartitionSpec as P

HEAD_DIM = 64
ADAPTER_RANK = 16
PAGE = 128
PAIR = 2 * HEAD_DIM
NEG = -1e30
EXP_SCALE = math.log2(math.e) * HEAD_DIM**-0.5
MIB = 1 << 20


def params(vmem):
    return pltpu.CompilerParams(
        dimension_semantics=("arbitrary",), vmem_limit_bytes=vmem * MIB
    )


def request_of(k, counts, requests):
    end = counts[0]
    request = (k >= end).astype(jnp.int32)
    for r in range(1, requests - 1):
        end = end + counts[r]
        request = request + (k >= end).astype(jnp.int32)
    return request


def normalize(values, gain_row, bias_row):
    average = jnp.mean(values, axis=-1, keepdims=True)
    centered = values - average
    variance = jnp.mean(centered * centered, axis=-1, keepdims=True)
    return centered * lax.rsqrt(variance + 1e-05) * gain_row + bias_row


def project_kernel(
    counts, table, owners, bases, *refs, requests, slots, pages, per_piece, parts,
):
    x_refs = refs[:parts]
    w_ref, down_ref, up_ref, q_ref = refs[parts : parts + 4]
    kv_refs = refs[parts + 4 : 2 * parts + 4]
    joined, page_owner = refs[2 * parts + 4 :]
    step = pl.program_id(0)
    cols = w_ref.shape[1]

    @pl.when(step == 0)
    def _():
        joined[:, :cols] = w_ref[...]
        joined[:, cols:] = down_ref[...]

        def fill(k, carry):
            page_owner[table[k]] = owners[request_of(k, counts, requests)]
            return carry

        lax.fori_loop(0, slots, fill, 0)

    piece = step * pages // per_piece

    def block(x_ref, kv_ref):
        both = jnp.dot(x_ref[...], joined[...], preferred_element_type=jnp.float32)
        low = both[:, cols:]
        lane_owner = lax.broadcasted_iota(jnp.int32, (PAGE, low.shape[1]), 1) // ADAPTER_RANK
        kept = []
        for p in range(pages):
            page = step * pages + p
            slot = bases[page // per_piece] + page % per_piece
            kept.append(
                jnp.where(lane_owner == page_owner[slot], low[p * PAGE : (p + 1) * PAGE], 0.0)
            )
        low_rank = jnp.concatenate(kept, axis=0).astype(jnp.bfloat16)
        rows = both[:, :cols] + jnp.dot(
            low_rank, up_ref[...], preferred_element_type=jnp.float32
        )
        rows = rows.astype(jnp.bfloat16)
        q_cols = q_ref.shape[1]
        q_ref[...] = rows[:, :q_cols]
        keys = rows[:, q_cols : 2 * q_cols]
        values = rows[:, 2 * q_cols :]
        for p in range(pages):
            here = slice(p * PAGE, (p + 1) * PAGE)
            kv_ref[p, :PAIR, :] = keys[here].T
            kv_ref[p, PAIR:, :] = values[here]

    for i in range(parts):
        pl.when(piece == i)(functools.partial(block, x_refs[i], kv_refs[i]))


def project(counts, table, owners, bases, xs, weight, down, up, per_piece):
    tok, width = xs[0].shape
    cols = weight.shape[1]
    pages = 2
    rows_step = pages * PAGE
    slots = table.shape[0]
    parts = len(xs)
    each = tok // rows_step
    total = tok * parts
    whole = lambda i, *_: (0, 0)
    rows = lambda i, *_: (i, 0)

    def own(part, *zeros):
        return lambda i, *_: (jnp.clip(i - part * each, 0, each - 1), 0, *zeros)

    return pl.pallas_call(
        functools.partial(
            project_kernel,
            requests=counts.shape[0], slots=slots, pages=pages, per_piece=per_piece, parts=parts,
        ),
        grid_spec=pltpu.PrefetchScalarGridSpec(
            num_scalar_prefetch=4,
            grid=(total // rows_step,),
            in_specs=[pl.BlockSpec((rows_step, width), own(i)) for i in range(parts)]
            + [
                pl.BlockSpec(weight.shape, whole),
                pl.BlockSpec(down.shape, whole),
                pl.BlockSpec(up.shape, whole),
            ],
            out_specs=[
                pl.BlockSpec((rows_step, cols // 3), rows),
            ]
            + [pl.BlockSpec((pages, PAIR + PAGE, PAIR), own(i, 0)) for i in range(parts)],
            scratch_shapes=[
                pltpu.VMEM((width, cols + down.shape[1]), jnp.bfloat16),
                pltpu.SMEM((slots,), jnp.int32),
            ],
        ),
        out_shape=[
            jax.ShapeDtypeStruct((total, cols // 3), jnp.bfloat16),
        ]
        + [jax.ShapeDtypeStruct((tok // PAGE, PAIR + PAGE, PAIR), jnp.bfloat16)] * parts,
        compiler_params=params(62),
        cost_estimate=pl.CostEstimate(
            flops=2 * total * width * cols, bytes_accessed=2 * total * (width + cols),
            transcendentals=0,
        ),
        name="project",
    )(counts, table, owners, bases, *xs, weight, down, up)


def attend_kernel(
    counts, table, q_bases, kv_bases, q_hbm, *refs,
    requests, slots, q_size, q_from, state_from, arrays, sizes, first, last, group,
):
    refs = list(refs)
    kv_hbm = [refs.pop(0) for _ in arrays]
    state_hbm = [] if first else [refs.pop(0), refs.pop(0)]
    if last:
        out_ref = refs.pop(0)
    else:
        acc_out, stat_out = refs.pop(0), refs.pop(0)
    kv, scores, listed, amount, asked, q_amount, sems, q_ref = refs[:8]
    if not first:
        acc_in, stat_in = refs[8:]
    tok = q_ref.shape[0]
    targets = [(q_hbm.at[pl.ds(q_from, tok)], q_ref)]
    offset = 0
    for i, size in enumerate(arrays):
        targets.append((kv_hbm[i], kv.at[pl.ds(offset, size)]))
        offset += size
    targets += [(ref.at[pl.ds(state_from, tok)], own) for ref, own in zip(state_hbm, refs[8:])]
    copies = [
        pltpu.make_async_copy(source, target, sems.at[n])
        for n, (source, target) in enumerate(targets)
    ]
    for copy in copies:
        copy.start()
    for r in range(requests):
        amount[r] = 0
        q_amount[r] = 0

    def place_of(slot, bases, extents):
        place = jnp.int32(-1)
        offset = 0
        for i, size in enumerate(extents):
            near = slot - bases[i]
            place = jnp.where((near >= 0) & (near < size), near + offset, place)
            offset += size
        return place

    q_sizes = (q_size,) * (q_ref.shape[0] // (q_size * PAGE))

    def fill(k, carry):
        r = request_of(k, counts, requests)
        slot = table[k]
        place = place_of(slot, kv_bases, sizes)
        q_place = place_of(slot, q_bases, q_sizes)

        @pl.when(place >= 0)
        def _():
            n = amount[r]
            listed[r, n] = place
            amount[r] = n + 1

        @pl.when(q_place >= 0)
        def _():
            n = q_amount[r]
            asked[r, n] = q_place
            q_amount[r] = n + 1

        return carry

    lax.fori_loop(0, slots, fill, 0)
    for copy in copies:
        copy.wait()
    lane = lax.broadcasted_iota(jnp.int32, (PAGE, PAIR), 1)
    low_lane = lane < HEAD_DIM
    rows = 4 * PAGE

    def one_pair(r, p):
        n = amount[r]
        full = n // group
        blocks = (n + group - 1) // group
        count = q_amount[r]
        a = asked[r, 2 * p]
        b = asked[r, jnp.minimum(2 * p + 1, count - 1)]
        spots = [pl.ds(pl.multiple_of(t * PAGE, PAGE), PAGE) for t in (a, b)]
        parts = []
        for spot in spots:
            q = q_ref[spot, :]
            zero = jnp.zeros_like(q)
            parts += [jnp.where(low_lane, q, zero), jnp.where(low_lane, zero, q)]
        stacked = jnp.concatenate(parts, axis=0)

        def page_of(j, i):
            return listed[r, jnp.minimum(j * group + i, n - 1)]

        def score(masked, j, top):
            keys = jnp.concatenate(
                [kv[page_of(j, i), :PAIR, :] for i in range(group)], axis=1
            )
            s = jnp.dot(stacked, keys, preferred_element_type=jnp.float32)
            for i in range(group):
                piece = s[:, i * PAGE : (i + 1) * PAGE]
                if masked and i:
                    piece = jnp.where(j * group + i < n, piece, NEG)
                scores[j, :, i * PAGE : (i + 1) * PAGE] = piece
                top = jnp.maximum(top, piece)
            return top

        top = jnp.full((rows, PAGE), NEG, jnp.float32)
        top = lax.fori_loop(0, full, functools.partial(score, False), top)
        top = lax.fori_loop(full, blocks, functools.partial(score, True), top)
        peak = jnp.max(top, axis=1, keepdims=True)
        if not first:
            old = jnp.concatenate(
                [stat_in[spot, h : h + 1] for spot in spots for h in (0, 1)], axis=0
            )
            peak = jnp.maximum(peak, old)
        shift = peak * EXP_SCALE

        def weigh(j, carry):
            total, acc = carry
            w = jnp.exp2(scores[j] * EXP_SCALE - shift)
            for i in range(group):
                total = total + w[:, i * PAGE : (i + 1) * PAGE]
            values = jnp.concatenate(
                [kv[page_of(j, i), PAIR:, :] for i in range(group)], axis=0
            )
            acc = acc + jnp.dot(
                w.astype(jnp.bfloat16), values, preferred_element_type=jnp.float32
            )
            return total, acc

        total, acc = lax.fori_loop(
            0, blocks, weigh,
            (jnp.zeros((rows, PAGE), jnp.float32), jnp.zeros((rows, PAIR), jnp.float32)),
        )
        total = jnp.sum(total, axis=1, keepdims=True)
        if not first:
            shrink = jnp.exp2((old - peak) * EXP_SCALE)
            total = total + shrink * jnp.concatenate(
                [stat_in[spot, h : h + 1] for spot in spots for h in (2, 3)], axis=0
            )
        for t, spot in enumerate(spots):
            h0 = slice(2 * t * PAGE, (2 * t + 1) * PAGE)
            h1 = slice((2 * t + 1) * PAGE, (2 * t + 2) * PAGE)
            value = jnp.where(low_lane, acc[h0], acc[h1])
            if not first:
                value = value + acc_in[spot, :] * jnp.where(low_lane, shrink[h0], shrink[h1])
            if last:
                value = value / jnp.where(low_lane, total[h0], total[h1])
                out_ref[spot, :] = value.astype(jnp.bfloat16)
            else:
                acc_out[spot, :] = value
                stat = jnp.where(lane == 0, peak[h0], peak[h1])
                stat = jnp.where(lane == 2, total[h0], stat)
                stat_out[spot, :] = jnp.where(lane == 3, total[h1], stat)

    def visit_request(r, carry):
        def visit(p, inner):
            one_pair(r, p)
            return inner

        return lax.fori_loop(0, (q_amount[r] + 1) // 2, visit, carry)

    lax.fori_loop(0, requests, visit_request, 0)


def attend(counts, table, q_bases, kv_bases, q, pieces, state, last, q_size, q_from=0):
    tok = q_bases.shape[0] * q_size * PAGE
    state_from = 0 if state is None or state[0].shape[0] == tok else q_from
    arrays = tuple(p.shape[0] for p in pieces)
    sizes = (sum(arrays) // kv_bases.shape[0],) * kv_bases.shape[0]
    first = state is None
    group = 4
    slots = table.shape[0]
    requests = counts.shape[0]
    most = min(sum(sizes), slots)
    state_shape = [jax.ShapeDtypeStruct((tok, PAIR), jnp.float32)] * 2
    out = pl.pallas_call(
        functools.partial(
            attend_kernel,
            requests=requests, slots=slots, q_size=q_size, q_from=q_from, state_from=state_from, arrays=arrays, sizes=sizes,
            first=first, last=last, group=group,
        ),
        grid_spec=pltpu.PrefetchScalarGridSpec(
            num_scalar_prefetch=4,
            grid=(1,),
            in_specs=[pl.BlockSpec(memory_space=pl.ANY)] * (len(pieces) + (1 if first else 3)),
            out_specs=[pl.BlockSpec((tok, PAIR), lambda i, *_: (0, 0))] * (1 if last else 2),
            scratch_shapes=[
                pltpu.VMEM((sum(sizes), PAIR + PAGE, PAIR), jnp.bfloat16),
                pltpu.VMEM(((most + group - 1) // group, 4 * PAGE, group * PAGE), jnp.float32),
                pltpu.SMEM((requests, sum(sizes)), jnp.int32),
                pltpu.SMEM((requests,), jnp.int32),
                pltpu.SMEM((requests, tok // PAGE), jnp.int32),
                pltpu.SMEM((requests,), jnp.int32),
                pltpu.SemaphoreType.DMA((len(pieces) + 3,)),
                pltpu.VMEM((tok, PAIR), jnp.bfloat16),
            ]
            + ([] if first else [pltpu.VMEM((tok, PAIR), jnp.float32)] * 2),
        ),
        out_shape=[jax.ShapeDtypeStruct((tok, PAIR), jnp.bfloat16)] if last else state_shape,
        compiler_params=params(62),
        cost_estimate=pl.CostEstimate(
            flops=tok * PAIR, bytes_accessed=4 * tok * PAIR, transcendentals=0,
        ),
        name="attend",
    )(counts, table, q_bases, kv_bases, q, *pieces, *([] if first else state))
    return out[0] if last else out


def finish_kernel(place, x_ref, *refs, parts, counts, last_step):
    refs = list(refs)
    ctx_refs, refs = refs[:parts], refs[parts:]
    out_w_refs, refs = refs[:parts], refs[parts:]
    gain1_ref, bias1_ref, bias_ref = refs[:3]
    refs = refs[3:]
    sets = []
    for n1, n2 in counts:
        w1s, refs = refs[:n1], refs[n1:]
        w2s, refs = refs[:n2], refs[n2:]
        sets.append((w1s, w2s))
    b2_ref, gain_ref, bias2_ref, next_w_ref, next_b_ref = refs[:5]
    layer_ref, next_ref, joined, normed_ref, acc, done = refs[5:]
    step = pl.program_id(0)
    tok = normed_ref.shape[0]
    block = min(512, tok)
    halves = len(sets)
    groups = (last_step + 1) // halves

    @pl.when(step == 0)
    def _():
        near = joined.shape[1] // parts
        for i in range(parts):
            joined[:, i * near : (i + 1) * near] = out_w_refs[i][:, :near]
        for t in range(tok // block):
            rows = slice(t * block, (t + 1) * block)
            mixed = x_ref[rows, :].astype(jnp.float32)
            for j in range(joined.shape[0]):
                ctx = jnp.concatenate([ref[j, rows, :] for ref in ctx_refs], axis=1)
                mixed = mixed + jnp.dot(ctx, joined[j], preferred_element_type=jnp.float32)
            normed = normalize(mixed, gain1_ref[...], bias1_ref[...]).astype(jnp.bfloat16)
            normed_ref[rows, :] = normed
            acc[rows, :] = normed.astype(jnp.float32) + b2_ref[...]

    def absorb(h, w1_refs, w2_refs):
        if len(w1_refs) == 1:
            w1 = w1_refs[0][0]
            starts, cols = [0], w1.shape[1]
        else:
            diagonal = jnp.concatenate([w1_refs[3][0], w1_refs[4][0]], axis=0)
            w1 = jnp.concatenate([ref[0] for ref in w1_refs[:3]] + [diagonal], axis=1)
            cols = diagonal.shape[1]
            core = place[2] if h == 0 else 1 - place[2]
            starts = [
                pl.multiple_of((core * 4 + (place[1] ^ r)) * cols, cols) for r in range(4)
            ]
        w2 = jnp.concatenate([ref[0] for ref in w2_refs], axis=0)
        bias = jnp.concatenate(
            [
                jnp.sum(
                    bias_ref[0, :, pl.ds(start, cols)].astype(jnp.float32), axis=0, keepdims=True
                )
                for start in starts
            ],
            axis=1,
        )
        for t in range(tok // block):
            rows = slice(t * block, (t + 1) * block)
            pre = jnp.dot(normed_ref[rows, :], w1, preferred_element_type=jnp.float32) + bias
            hidden = 0.5 * pre * (1.0 + lax.erf(pre * math.sqrt(0.5)))
            acc[rows, :] += jnp.dot(
                hidden.astype(jnp.bfloat16), w2, preferred_element_type=jnp.float32
            )

    for h in range(halves):
        pl.when(step // groups == h)(functools.partial(absorb, h, *sets[h]))

    @pl.when(step == last_step)
    def _():
        for t in range(tok // block):
            rows = slice(t * block, (t + 1) * block)
            layer = normalize(acc[rows, :], gain_ref[...], bias2_ref[...]).astype(jnp.bfloat16)
            done[rows, :] = layer
            next_ref[rows, :] = (
                jnp.dot(layer, next_w_ref[...], preferred_element_type=jnp.float32)
                + next_b_ref[...]
            ).astype(jnp.bfloat16)
        share = layer_ref.shape[0]
        layer_ref[...] = done[pl.ds(pl.multiple_of(place[0] * share, share), share), :]


def finish(
    place, x, contexts, outs, gain1, bias1, bias, sets, b2, gain, bias2, next_w, next_b, share
):
    tok, width = x.shape
    halves = len(sets)
    groups = bias.shape[0]
    ctx_cols = sum(ctx.shape[2] for ctx in contexts)
    cols = bias.shape[2] // halves
    steps = halves * groups

    def whole(array):
        return pl.BlockSpec(
            array.shape, lambda i, *_: (0,) * array.ndim, pipeline_mode=pl.Buffered(1)
        )

    specs, arrays = [], []
    for h, (w1s, w2s) in enumerate(sets):
        at = lambda i, *_, h=h: (jnp.clip(i - h * groups, 0, groups - 1), 0, 0)
        for array in (*w1s, *w2s):
            specs.append(pl.BlockSpec((1,) + array.shape[1:], at))
            arrays.append(array)
    head = [x, *contexts, *outs, gain1[None], bias1[None]]
    tail = [b2[None], gain[None], bias2[None], next_w, next_b[None]]
    next_cols = next_w.shape[1]
    fixed = lambda i, *_: (0, 0)
    return pl.pallas_call(
        functools.partial(
            finish_kernel,
            parts=len(outs),
            counts=tuple((len(w1s), len(w2s)) for w1s, w2s in sets),
            last_step=steps - 1,
        ),
        grid_spec=pltpu.PrefetchScalarGridSpec(
            num_scalar_prefetch=1,
            grid=(steps,),
            in_specs=[whole(array) for array in head]
            + [
                pl.BlockSpec(
                    (1, 16, bias.shape[2]),
                    lambda i, *_: (i % groups, bias.shape[1] // 16 - 1, 0),
                ),
            ]
            + specs
            + [whole(array) for array in tail],
            out_specs=[
                pl.BlockSpec((share, width), fixed),
                pl.BlockSpec((tok, next_cols), fixed),
            ],
            scratch_shapes=[
                pltpu.VMEM((groups, ctx_cols, width), jnp.bfloat16),
                pltpu.VMEM((tok, width), jnp.bfloat16),
                pltpu.VMEM((tok, width), jnp.float32),
                pltpu.VMEM((tok, width), jnp.bfloat16),
            ],
        ),
        out_shape=[
            jax.ShapeDtypeStruct((share, width), jnp.bfloat16),
            jax.ShapeDtypeStruct((tok, next_cols), jnp.bfloat16),
        ],
        compiler_params=params(62),
        cost_estimate=pl.CostEstimate(
            flops=4 * tok * width * cols * steps, bytes_accessed=4 * width * cols * steps,
            transcendentals=tok * cols * steps,
        ),
        name="finish",
    )(place, *head, bias, *arrays, *tail)


def three_parts(values):
    high = lax.reduce_precision(values, 8, 7)
    middle = lax.reduce_precision(values - high, 8, 7)
    rest = values - high - middle
    return [part.astype(jnp.bfloat16) for part in (high, middle, rest)]


def local(
    tokens,
    query_key_value_weight,
    adapter_down_weight,
    adapter_up_weight,
    attention_out_weight,
    first_norm_gain,
    first_norm_bias,
    first_feed_weight,
    first_feed_bias,
    second_feed_weight,
    second_feed_bias,
    second_norm_gain,
    second_norm_bias,
    following_qkv_weight,
    following_bias,
    request_page_count,
    page_slot_table,
    request_adapter,
):
    tok_rows, width = tokens.shape
    dp_count = lax.axis_size("dp")
    mp_count = lax.axis_size("mp")
    dp_index = lax.axis_index("dp")
    mp_index = lax.axis_index("mp")
    kept_values = adapter_down_weight.shape[1] // ADAPTER_RANK
    heads_dev = query_key_value_weight.shape[1] // (3 * HEAD_DIM)
    pages = tok_rows // PAGE
    shared = dp_count == 8 and heads_dev == 4

    owners = request_adapter // kept_values
    level = jnp.sum(jnp.where(owners == mp_index, request_adapter % kept_values, 0))
    down = lax.dynamic_slice_in_dim(
        adapter_down_weight, level * ADAPTER_RANK, ADAPTER_RANK, 1
    )
    up = lax.dynamic_slice_in_dim(adapter_up_weight, level * ADAPTER_RANK, ADAPTER_RANK, 0)
    up_cols = up.shape[1] // mp_count
    sent = jnp.concatenate(
        [
            jnp.broadcast_to(down.T[:, None, :], (ADAPTER_RANK, mp_count, width)),
            up.reshape(ADAPTER_RANK, mp_count, up_cols),
        ],
        axis=2,
    ).reshape(ADAPTER_RANK, mp_count * (width + up_cols))
    got = lax.all_to_all(sent, "mp", split_axis=1, concat_axis=0, tiled=True)

    def by_kind(matrix):
        split = matrix.reshape(matrix.shape[0], heads_dev, 3, HEAD_DIM)
        if shared:
            split = lax.dynamic_slice_in_dim(split, (dp_index % 2) * 2, 2, 1)
        return jnp.swapaxes(split, 1, 2).reshape(matrix.shape[0], -1)

    place = jnp.stack(
        [mp_index] + ([dp_index // 2, dp_index % 2] if shared else [0, 0])
    ).astype(jnp.int32)
    hidden_dev = first_feed_weight.shape[1]
    downs = got[:, :width].T
    ups = got[:, width:]
    weight = by_kind(query_key_value_weight)
    ups = by_kind(ups)
    if shared:
        swap = [(i, i ^ 1) for i in range(8)]
        across = [(i, i ^ 2) for i in range(8)]
        along = [(i, i ^ 4) for i in range(8)]
        move = lambda value, pairs: lax.ppermute(value, "dp", pairs)
        xs = [tokens, move(tokens, swap)]
        at = lambda flip: (dp_index ^ flip) * pages
        bases = jnp.stack([at(0), at(1)])
    else:
        xs = [tokens]
        bases = jnp.stack([dp_index * pages])
    args = (request_page_count, page_slot_table)
    q, *kvs = project(*args, owners, bases, xs, weight, downs, ups, pages)
    bias_rows = jnp.pad(jnp.stack(three_parts(first_feed_bias)), ((0, 13), (0, 0)))
    out_rows = attention_out_weight.shape[0]
    if shared:
        unit = hidden_dev // 8
        turn = (dp_index % 2) * 4 + dp_index // 2
        kv_x = [move(kv, across) for kv in kvs]
        kv_y = [move(kv, along) for kv in kvs]
        first = lax.dynamic_slice_in_dim(first_feed_weight, turn * unit, unit, 1)
        first, kvs = lax.optimization_barrier((first, kvs))
        first = lax.all_gather(first, "mp", axis=0)
        step = functools.partial(attend, *args)
        state = step(bases, bases, q, kvs, None, False, pages)
        second = lax.dynamic_slice_in_dim(second_feed_weight, turn * unit, unit, 0)
        out_half = jnp.concatenate(
            [
                lax.dynamic_slice_in_dim(
                    attention_out_weight, (dp_index % 2) * (out_rows // 2), out_rows // 2, 0
                ),
                bias_rows,
            ],
            axis=0,
        )
        kv_x, kv_y, state, first, second, out_half = lax.optimization_barrier(
            (kv_x, kv_y, state, first, second, out_half)
        )
        second = lax.all_gather(second, "mp", axis=0)
        out_mine = lax.all_gather(out_half, "mp", axis=0)
        kv_d0 = move(kv_y[0], across)
        kv_d1 = move(kv_x[1], along)
        first_x = move(first, across)
        first_y = move(first, along)
        near = [at(2), at(3), at(4), at(5)]
        far = [at(6), at(7)]
        swapped, own = bases[1:], bases[:1]
        late = step(
            swapped, jnp.stack(near), q, [*kv_x, *kv_y], state, False, pages, q_from=tok_rows
        )
        kv_d0, kv_d1, late = lax.optimization_barrier((kv_d0, kv_d1, late))
        theirs = step(
            swapped, jnp.stack(far), q, [kv_d0, kv_d1], late, True, pages, q_from=tok_rows
        )
        theirs, first_x, first_y, second = lax.optimization_barrier(
            (theirs, first_x, first_y, second)
        )
        cut = width // 2
        first_d0 = move(first_y[:, :cut], across)
        first_d1 = move(first_x[:, cut:], along)
        second_x = move(second, across)
        second_y = move(second, along)
        near_others = [move(piece, swap) for piece in (first, first_x, first_y, second)]
        theirs = lax.all_gather(move(theirs, swap), "mp", axis=0)
        mine = step(
            own, jnp.stack(near + far), q, [*kv_x, *kv_y, kv_d0, kv_d1], state, True, pages
        )
        mine, first_d0, first_d1, near_others, second_x, second_y, out_mine = (
            lax.optimization_barrier(
                (mine, first_d0, first_d1, near_others, second_x, second_y, out_mine)
            )
        )
        contexts = [lax.all_gather(mine, "mp", axis=0), theirs]
        bias_rows = out_mine
        half = unit // 2
        second_d0 = move(second_y[:, :half], across)
        second_d1 = move(second_x[:, half:], along)
        firsts = [first, first_x, first_y, first_d0, first_d1]
        moved = [move(piece, swap) for piece in (first_d0, first_d1, second_x, second_y, out_mine)]
        first_others = [*near_others[:3], *moved[:2]]
        out_other = moved[4]
        seconds = [second, second_x, second_y, second_d0, second_d1]
        second_others = [
            near_others[3], *moved[2:4], move(second_d0, swap), move(second_d1, swap)
        ]
        sets = [(firsts, seconds), (first_others, second_others)]
        outs = [out_mine, out_other]
    else:
        everything = lax.all_gather(kvs[0], "dp", axis=0, tiled=True)
        context = attend(
            *args, bases, jnp.zeros((1,), jnp.int32), q, [everything], None, True, pages
        )
        second = lax.all_gather(second_feed_weight, "mp", axis=0)
        bias_rows = lax.all_gather(bias_rows, "mp", axis=0)
        sets = [([lax.all_gather(first_feed_weight, "mp", axis=0)], [second])]
        outs = [lax.all_gather(attention_out_weight, "mp", axis=0)]
        contexts = [lax.all_gather(context, "mp", axis=0)]
    layer_rows, next_proj = finish(
        place, tokens, contexts, outs, first_norm_gain, first_norm_bias, bias_rows, sets,
        second_feed_bias, second_norm_gain, second_norm_bias, following_qkv_weight,
        following_bias, tok_rows // mp_count,
    )
    return (layer_rows, next_proj)


def solution(mesh):
    placed = (
        P("dp", None),
        P(None, "mp"),
        P(None, "mp"),
        P("mp", None),
        P("mp", None),
        P(),
        P(),
        P(None, "mp"),
        P("mp"),
        P("mp", None),
        P(),
        P(),
        P(),
        P(None, "mp"),
        P("mp"),
        P(),
        P(),
        P(),
    )
    return jax.shard_map(
        local,
        mesh=mesh,
        in_specs=placed,
        out_specs=(P(("dp", "mp"), None), P("dp", "mp")),
        check_vma=False,
    )
```

```python
import functools
import math

import jax
import jax.numpy as jnp
from jax import lax
from jax.experimental import pallas as pl
from jax.experimental.pallas import tpu as pltpu
from jax.sharding import PartitionSpec as P

HEAD_DIM = 64
ADAPTER_RANK = 16
PAGE = 128
PAIR = 2 * HEAD_DIM
NEG = -1e30
EXP_SCALE = math.log2(math.e) * HEAD_DIM**-0.5
MIB = 1 << 20


def params(vmem):
    return pltpu.CompilerParams(
        dimension_semantics=("arbitrary",), vmem_limit_bytes=vmem * MIB
    )


def request_of(k, counts, requests):
    end = counts[0]
    request = (k >= end).astype(jnp.int32)
    for r in range(1, requests - 1):
        end = end + counts[r]
        request = request + (k >= end).astype(jnp.int32)
    return request


def normalize(values, gain_row, bias_row):
    average = jnp.mean(values, axis=-1, keepdims=True)
    centered = values - average
    variance = jnp.mean(centered * centered, axis=-1, keepdims=True)
    return centered * lax.rsqrt(variance + 1e-05) * gain_row + bias_row


def project_kernel(
    counts, table, owners, bases, *refs, requests, slots, pages, per_piece, parts,
):
    x_refs = refs[:parts]
    w_ref, down_ref, up_ref, q_ref = refs[parts : parts + 4]
    kv_refs = refs[parts + 4 : 2 * parts + 4]
    joined, page_owner = refs[2 * parts + 4 :]
    step = pl.program_id(0)
    cols = w_ref.shape[1]

    @pl.when(step == 0)
    def _():
        joined[:, :cols] = w_ref[...]
        joined[:, cols:] = down_ref[...]

        def fill(k, carry):
            page_owner[table[k]] = owners[request_of(k, counts, requests)]
            return carry

        lax.fori_loop(0, slots, fill, 0)

    piece = step * pages // per_piece

    def block(x_ref, kv_ref):
        both = jnp.dot(x_ref[...], joined[...], preferred_element_type=jnp.float32)
        low = both[:, cols:]
        lane_owner = lax.broadcasted_iota(jnp.int32, (PAGE, low.shape[1]), 1) // ADAPTER_RANK
        kept = []
        for p in range(pages):
            page = step * pages + p
            slot = bases[page // per_piece] + page % per_piece
            kept.append(
                jnp.where(lane_owner == page_owner[slot], low[p * PAGE : (p + 1) * PAGE], 0.0)
            )
        low_rank = jnp.concatenate(kept, axis=0).astype(jnp.bfloat16)
        rows = both[:, :cols] + jnp.dot(
            low_rank, up_ref[...], preferred_element_type=jnp.float32
        )
        rows = rows.astype(jnp.bfloat16)
        q_cols = q_ref.shape[1]
        q_ref[...] = rows[:, :q_cols]
        keys = rows[:, q_cols : 2 * q_cols]
        values = rows[:, 2 * q_cols :]
        for p in range(pages):
            here = slice(p * PAGE, (p + 1) * PAGE)
            kv_ref[p, :PAIR, :] = keys[here].T
            kv_ref[p, PAIR:, :] = values[here]

    for i in range(parts):
        pl.when(piece == i)(functools.partial(block, x_refs[i], kv_refs[i]))


def project(counts, table, owners, bases, xs, weight, down, up, per_piece):
    tok, width = xs[0].shape
    cols = weight.shape[1]
    pages = 2
    rows_step = pages * PAGE
    slots = table.shape[0]
    parts = len(xs)
    each = tok // rows_step
    total = tok * parts
    whole = lambda i, *_: (0, 0)
    rows = lambda i, *_: (i, 0)

    def own(part, *zeros):
        return lambda i, *_: (jnp.clip(i - part * each, 0, each - 1), 0, *zeros)

    return pl.pallas_call(
        functools.partial(
            project_kernel,
            requests=counts.shape[0], slots=slots, pages=pages, per_piece=per_piece, parts=parts,
        ),
        grid_spec=pltpu.PrefetchScalarGridSpec(
            num_scalar_prefetch=4,
            grid=(total // rows_step,),
            in_specs=[pl.BlockSpec((rows_step, width), own(i)) for i in range(parts)]
            + [
                pl.BlockSpec(weight.shape, whole),
                pl.BlockSpec(down.shape, whole),
                pl.BlockSpec(up.shape, whole),
            ],
            out_specs=[
                pl.BlockSpec((rows_step, cols // 3), rows),
            ]
            + [pl.BlockSpec((pages, PAIR + PAGE, PAIR), own(i, 0)) for i in range(parts)],
            scratch_shapes=[
                pltpu.VMEM((width, cols + down.shape[1]), jnp.bfloat16),
                pltpu.SMEM((slots,), jnp.int32),
            ],
        ),
        out_shape=[
            jax.ShapeDtypeStruct((total, cols // 3), jnp.bfloat16),
        ]
        + [jax.ShapeDtypeStruct((tok // PAGE, PAIR + PAGE, PAIR), jnp.bfloat16)] * parts,
        compiler_params=params(62),
        cost_estimate=pl.CostEstimate(
            flops=2 * total * width * cols, bytes_accessed=2 * total * (width + cols),
            transcendentals=0,
        ),
        name="project",
    )(counts, table, owners, bases, *xs, weight, down, up)


def attend_kernel(
    counts, table, q_bases, kv_bases, q_hbm, *refs,
    requests, slots, q_size, q_from, state_from, arrays, sizes, first, last, group,
):
    refs = list(refs)
    kv_hbm = [refs.pop(0) for _ in arrays]
    state_hbm = [] if first else [refs.pop(0), refs.pop(0)]
    if last:
        out_ref = refs.pop(0)
    else:
        acc_out, stat_out = refs.pop(0), refs.pop(0)
    kv, scores, listed, amount, asked, q_amount, sems, q_ref = refs[:8]
    if not first:
        acc_in, stat_in = refs[8:]
    tok = q_ref.shape[0]
    targets = [(q_hbm.at[pl.ds(q_from, tok)], q_ref)]
    offset = 0
    for i, size in enumerate(arrays):
        targets.append((kv_hbm[i], kv.at[pl.ds(offset, size)]))
        offset += size
    targets += [(ref.at[pl.ds(state_from, tok)], own) for ref, own in zip(state_hbm, refs[8:])]
    copies = [
        pltpu.make_async_copy(source, target, sems.at[n])
        for n, (source, target) in enumerate(targets)
    ]
    for copy in copies:
        copy.start()
    for r in range(requests):
        amount[r] = 0
        q_amount[r] = 0

    def place_of(slot, bases, extents):
        place = jnp.int32(-1)
        offset = 0
        for i, size in enumerate(extents):
            near = slot - bases[i]
            place = jnp.where((near >= 0) & (near < size), near + offset, place)
            offset += size
        return place

    q_sizes = (q_size,) * (q_ref.shape[0] // (q_size * PAGE))

    def fill(k, carry):
        r = request_of(k, counts, requests)
        slot = table[k]
        place = place_of(slot, kv_bases, sizes)
        q_place = place_of(slot, q_bases, q_sizes)

        @pl.when(place >= 0)
        def _():
            n = amount[r]
            listed[r, n] = place
            amount[r] = n + 1

        @pl.when(q_place >= 0)
        def _():
            n = q_amount[r]
            asked[r, n] = q_place
            q_amount[r] = n + 1

        return carry

    lax.fori_loop(0, slots, fill, 0)
    for copy in copies:
        copy.wait()
    lane = lax.broadcasted_iota(jnp.int32, (PAGE, PAIR), 1)
    low_lane = lane < HEAD_DIM
    rows = 4 * PAGE

    def one_pair(r, p):
        n = amount[r]
        full = n // group
        blocks = (n + group - 1) // group
        count = q_amount[r]
        a = asked[r, 2 * p]
        b = asked[r, jnp.minimum(2 * p + 1, count - 1)]
        spots = [pl.ds(pl.multiple_of(t * PAGE, PAGE), PAGE) for t in (a, b)]
        parts = []
        for spot in spots:
            q = q_ref[spot, :]
            zero = jnp.zeros_like(q)
            parts += [jnp.where(low_lane, q, zero), jnp.where(low_lane, zero, q)]
        stacked = jnp.concatenate(parts, axis=0)

        def page_of(j, i):
            return listed[r, jnp.minimum(j * group + i, n - 1)]

        def score(masked, j, top):
            keys = jnp.concatenate(
                [kv[page_of(j, i), :PAIR, :] for i in range(group)], axis=1
            )
            s = jnp.dot(stacked, keys, preferred_element_type=jnp.float32)
            for i in range(group):
                piece = s[:, i * PAGE : (i + 1) * PAGE]
                if masked and i:
                    piece = jnp.where(j * group + i < n, piece, NEG)
                scores[j, :, i * PAGE : (i + 1) * PAGE] = piece
                top = jnp.maximum(top, piece)
            return top

        top = jnp.full((rows, PAGE), NEG, jnp.float32)
        top = lax.fori_loop(0, full, functools.partial(score, False), top)
        top = lax.fori_loop(full, blocks, functools.partial(score, True), top)
        peak = jnp.max(top, axis=1, keepdims=True)
        if not first:
            old = jnp.concatenate(
                [stat_in[spot, h : h + 1] for spot in spots for h in (0, 1)], axis=0
            )
            peak = jnp.maximum(peak, old)
        shift = peak * EXP_SCALE

        def weigh(j, carry):
            total, acc = carry
            w = jnp.exp2(scores[j] * EXP_SCALE - shift)
            for i in range(group):
                total = total + w[:, i * PAGE : (i + 1) * PAGE]
            values = jnp.concatenate(
                [kv[page_of(j, i), PAIR:, :] for i in range(group)], axis=0
            )
            acc = acc + jnp.dot(
                w.astype(jnp.bfloat16), values, preferred_element_type=jnp.float32
            )
            return total, acc

        total, acc = lax.fori_loop(
            0, blocks, weigh,
            (jnp.zeros((rows, PAGE), jnp.float32), jnp.zeros((rows, PAIR), jnp.float32)),
        )
        total = jnp.sum(total, axis=1, keepdims=True)
        if not first:
            shrink = jnp.exp2((old - peak) * EXP_SCALE)
            total = total + shrink * jnp.concatenate(
                [stat_in[spot, h : h + 1] for spot in spots for h in (2, 3)], axis=0
            )
        for t, spot in enumerate(spots):
            h0 = slice(2 * t * PAGE, (2 * t + 1) * PAGE)
            h1 = slice((2 * t + 1) * PAGE, (2 * t + 2) * PAGE)
            value = jnp.where(low_lane, acc[h0], acc[h1])
            if not first:
                value = value + acc_in[spot, :] * jnp.where(low_lane, shrink[h0], shrink[h1])
            if last:
                value = value / jnp.where(low_lane, total[h0], total[h1])
                out_ref[spot, :] = value.astype(jnp.bfloat16)
            else:
                acc_out[spot, :] = value
                stat = jnp.where(lane == 0, peak[h0], peak[h1])
                stat = jnp.where(lane == 2, total[h0], stat)
                stat_out[spot, :] = jnp.where(lane == 3, total[h1], stat)

    def visit_request(r, carry):
        def visit(p, inner):
            one_pair(r, p)
            return inner

        return lax.fori_loop(0, (q_amount[r] + 1) // 2, visit, carry)

    lax.fori_loop(0, requests, visit_request, 0)


def attend(counts, table, q_bases, kv_bases, q, pieces, state, last, q_size, q_from=0):
    tok = q_bases.shape[0] * q_size * PAGE
    state_from = 0 if state is None or state[0].shape[0] == tok else q_from
    arrays = tuple(p.shape[0] for p in pieces)
    sizes = (sum(arrays) // kv_bases.shape[0],) * kv_bases.shape[0]
    first = state is None
    group = 4
    slots = table.shape[0]
    requests = counts.shape[0]
    most = min(sum(sizes), slots)
    state_shape = [jax.ShapeDtypeStruct((tok, PAIR), jnp.float32)] * 2
    out = pl.pallas_call(
        functools.partial(
            attend_kernel,
            requests=requests, slots=slots, q_size=q_size, q_from=q_from, state_from=state_from, arrays=arrays, sizes=sizes,
            first=first, last=last, group=group,
        ),
        grid_spec=pltpu.PrefetchScalarGridSpec(
            num_scalar_prefetch=4,
            grid=(1,),
            in_specs=[pl.BlockSpec(memory_space=pl.ANY)] * (len(pieces) + (1 if first else 3)),
            out_specs=[pl.BlockSpec((tok, PAIR), lambda i, *_: (0, 0))] * (1 if last else 2),
            scratch_shapes=[
                pltpu.VMEM((sum(sizes), PAIR + PAGE, PAIR), jnp.bfloat16),
                pltpu.VMEM(((most + group - 1) // group, 4 * PAGE, group * PAGE), jnp.float32),
                pltpu.SMEM((requests, sum(sizes)), jnp.int32),
                pltpu.SMEM((requests,), jnp.int32),
                pltpu.SMEM((requests, tok // PAGE), jnp.int32),
                pltpu.SMEM((requests,), jnp.int32),
                pltpu.SemaphoreType.DMA((len(pieces) + 3,)),
                pltpu.VMEM((tok, PAIR), jnp.bfloat16),
            ]
            + ([] if first else [pltpu.VMEM((tok, PAIR), jnp.float32)] * 2),
        ),
        out_shape=[jax.ShapeDtypeStruct((tok, PAIR), jnp.bfloat16)] if last else state_shape,
        compiler_params=params(62),
        cost_estimate=pl.CostEstimate(
            flops=tok * PAIR, bytes_accessed=4 * tok * PAIR, transcendentals=0,
        ),
        name="attend",
    )(counts, table, q_bases, kv_bases, q, *pieces, *([] if first else state))
    return out[0] if last else out


def finish_kernel(place, x_ref, *refs, parts, counts, last_step):
    refs = list(refs)
    ctx_refs, refs = refs[:parts], refs[parts:]
    out_w_refs, refs = refs[:parts], refs[parts:]
    gain1_ref, bias1_ref, bias_ref = refs[:3]
    refs = refs[3:]
    sets = []
    for n1, n2 in counts:
        w1s, refs = refs[:n1], refs[n1:]
        w2s, refs = refs[:n2], refs[n2:]
        sets.append((w1s, w2s))
    b2_ref, gain_ref, bias2_ref, next_w_ref, next_b_ref = refs[:5]
    layer_ref, next_ref, joined, normed_ref, acc, done = refs[5:]
    step = pl.program_id(0)
    tok = normed_ref.shape[0]
    block = min(512, tok)
    halves = len(sets)
    groups = (last_step + 1) // halves

    @pl.when(step == 0)
    def _():
        near = joined.shape[1] // parts
        for i in range(parts):
            joined[:, i * near : (i + 1) * near] = out_w_refs[i][:, :near]
        for t in range(tok // block):
            rows = slice(t * block, (t + 1) * block)
            mixed = x_ref[rows, :].astype(jnp.float32)
            for j in range(joined.shape[0]):
                ctx = jnp.concatenate([ref[j, rows, :] for ref in ctx_refs], axis=1)
                mixed = mixed + jnp.dot(ctx, joined[j], preferred_element_type=jnp.float32)
            normed = normalize(mixed, gain1_ref[...], bias1_ref[...]).astype(jnp.bfloat16)
            normed_ref[rows, :] = normed
            acc[rows, :] = normed.astype(jnp.float32) + b2_ref[...]

    def absorb(h, w1_refs, w2_refs):
        if len(w1_refs) == 1:
            w1 = w1_refs[0][0]
            starts, cols = [0], w1.shape[1]
        else:
            diagonal = jnp.concatenate([w1_refs[3][0], w1_refs[4][0]], axis=0)
            w1 = jnp.concatenate([ref[0] for ref in w1_refs[:3]] + [diagonal], axis=1)
            cols = diagonal.shape[1]
            core = place[2] if h == 0 else 1 - place[2]
            starts = [
                pl.multiple_of((core * 4 + (place[1] ^ r)) * cols, cols) for r in range(4)
            ]
        w2 = jnp.concatenate([ref[0] for ref in w2_refs], axis=0)
        bias = jnp.concatenate(
            [
                jnp.sum(
                    bias_ref[0, :, pl.ds(start, cols)].astype(jnp.float32), axis=0, keepdims=True
                )
                for start in starts
            ],
            axis=1,
        )
        for t in range(tok // block):
            rows = slice(t * block, (t + 1) * block)
            pre = jnp.dot(normed_ref[rows, :], w1, preferred_element_type=jnp.float32) + bias
            hidden = 0.5 * pre * (1.0 + lax.erf(pre * math.sqrt(0.5)))
            acc[rows, :] += jnp.dot(
                hidden.astype(jnp.bfloat16), w2, preferred_element_type=jnp.float32
            )

    for h in range(halves):
        pl.when(step // groups == h)(functools.partial(absorb, h, *sets[h]))

    @pl.when(step == last_step)
    def _():
        for t in range(tok // block):
            rows = slice(t * block, (t + 1) * block)
            layer = normalize(acc[rows, :], gain_ref[...], bias2_ref[...]).astype(jnp.bfloat16)
            done[rows, :] = layer
            next_ref[rows, :] = (
                jnp.dot(layer, next_w_ref[...], preferred_element_type=jnp.float32)
                + next_b_ref[...]
            ).astype(jnp.bfloat16)
        share = layer_ref.shape[0]
        layer_ref[...] = done[pl.ds(pl.multiple_of(place[0] * share, share), share), :]


def finish(
    place, x, contexts, outs, gain1, bias1, bias, sets, b2, gain, bias2, next_w, next_b, share
):
    tok, width = x.shape
    halves = len(sets)
    groups = bias.shape[0]
    ctx_cols = sum(ctx.shape[2] for ctx in contexts)
    cols = bias.shape[2] // halves
    steps = halves * groups
    out_at = 1 if len(outs) > 1 else 0

    def whole(array):
        return pl.BlockSpec(
            array.shape, lambda i, *_: (0,) * array.ndim, pipeline_mode=pl.Buffered(1)
        )

    specs, arrays = [], []
    for h, (w1s, w2s) in enumerate(sets):
        at = lambda i, *_, h=h: (jnp.clip(i - h * groups, 0, groups - 1), 0, 0)
        for n, array in enumerate((*w1s, *w2s)):
            rows = array.shape[1]
            if len(w1s) > 1 and n == len(w1s):
                rows = w1s[0].shape[2]
            specs.append(pl.BlockSpec((1, rows, array.shape[2]), at))
            arrays.append(array)
    head = [x, *contexts, *outs, gain1[None], bias1[None]]
    tail = [b2[None], gain[None], bias2[None], next_w, next_b[None]]
    next_cols = next_w.shape[1]
    fixed = lambda i, *_: (0, 0)
    return pl.pallas_call(
        functools.partial(
            finish_kernel,
            parts=len(outs),
            counts=tuple((len(w1s), len(w2s)) for w1s, w2s in sets),
            last_step=steps - 1,
        ),
        grid_spec=pltpu.PrefetchScalarGridSpec(
            num_scalar_prefetch=1,
            grid=(steps,),
            in_specs=[whole(array) for array in head[: 1 + len(contexts)]]
            + [
                pl.BlockSpec(
                    (groups, ctx_cols // len(outs), width), lambda i, *_: (0, out_at, 0),
                    pipeline_mode=pl.Buffered(1),
                )
                for _ in outs
            ]
            + [whole(array) for array in head[1 + len(contexts) + len(outs) :]]
            + [
                pl.BlockSpec(
                    (1, 16, bias.shape[2]),
                    lambda i, *_: (i % groups, bias.shape[1] // 16 - 1, 0),
                ),
            ]
            + specs
            + [whole(array) for array in tail],
            out_specs=[
                pl.BlockSpec((share, width), fixed),
                pl.BlockSpec((tok, next_cols), fixed),
            ],
            scratch_shapes=[
                pltpu.VMEM((groups, ctx_cols, width), jnp.bfloat16),
                pltpu.VMEM((tok, width), jnp.bfloat16),
                pltpu.VMEM((tok, width), jnp.float32),
                pltpu.VMEM((tok, width), jnp.bfloat16),
            ],
        ),
        out_shape=[
            jax.ShapeDtypeStruct((share, width), jnp.bfloat16),
            jax.ShapeDtypeStruct((tok, next_cols), jnp.bfloat16),
        ],
        compiler_params=params(62),
        cost_estimate=pl.CostEstimate(
            flops=4 * tok * width * cols * steps, bytes_accessed=4 * width * cols * steps,
            transcendentals=tok * cols * steps,
        ),
        name="finish",
    )(place, *head, bias, *arrays, *tail)


def three_parts(values):
    high = lax.reduce_precision(values, 8, 7)
    middle = lax.reduce_precision(values - high, 8, 7)
    rest = values - high - middle
    return [part.astype(jnp.bfloat16) for part in (high, middle, rest)]


def local(
    tokens,
    query_key_value_weight,
    adapter_down_weight,
    adapter_up_weight,
    attention_out_weight,
    first_norm_gain,
    first_norm_bias,
    first_feed_weight,
    first_feed_bias,
    second_feed_weight,
    second_feed_bias,
    second_norm_gain,
    second_norm_bias,
    following_qkv_weight,
    following_bias,
    request_page_count,
    page_slot_table,
    request_adapter,
):
    tok_rows, width = tokens.shape
    dp_count = lax.axis_size("dp")
    mp_count = lax.axis_size("mp")
    dp_index = lax.axis_index("dp")
    mp_index = lax.axis_index("mp")
    kept_values = adapter_down_weight.shape[1] // ADAPTER_RANK
    heads_dev = query_key_value_weight.shape[1] // (3 * HEAD_DIM)
    pages = tok_rows // PAGE
    shared = dp_count == 8 and heads_dev == 4

    owners = request_adapter // kept_values
    level = jnp.sum(jnp.where(owners == mp_index, request_adapter % kept_values, 0))
    down = lax.dynamic_slice_in_dim(
        adapter_down_weight, level * ADAPTER_RANK, ADAPTER_RANK, 1
    )
    up = lax.dynamic_slice_in_dim(adapter_up_weight, level * ADAPTER_RANK, ADAPTER_RANK, 0)
    up_cols = up.shape[1] // mp_count
    sent = jnp.concatenate(
        [
            jnp.broadcast_to(down.T[:, None, :], (ADAPTER_RANK, mp_count, width)),
            up.reshape(ADAPTER_RANK, mp_count, up_cols),
        ],
        axis=2,
    ).reshape(ADAPTER_RANK, mp_count * (width + up_cols))
    got = lax.all_to_all(sent, "mp", split_axis=1, concat_axis=0, tiled=True)

    def by_kind(matrix):
        split = matrix.reshape(matrix.shape[0], heads_dev, 3, HEAD_DIM)
        if shared:
            split = lax.dynamic_slice_in_dim(split, (dp_index % 2) * 2, 2, 1)
        return jnp.swapaxes(split, 1, 2).reshape(matrix.shape[0], -1)

    place = jnp.stack(
        [mp_index] + ([dp_index // 2, dp_index % 2] if shared else [0, 0])
    ).astype(jnp.int32)
    hidden_dev = first_feed_weight.shape[1]
    downs = got[:, :width].T
    ups = got[:, width:]
    weight = by_kind(query_key_value_weight)
    ups = by_kind(ups)
    if shared:
        swap = [(i, i ^ 1) for i in range(8)]
        across = [(i, i ^ 2) for i in range(8)]
        along = [(i, i ^ 4) for i in range(8)]
        move = lambda value, pairs: lax.ppermute(value, "dp", pairs)
        xs = [tokens, move(tokens, swap)]
        at = lambda flip: (dp_index ^ flip) * pages
        bases = jnp.stack([at(0), at(1)])
    else:
        xs = [tokens]
        bases = jnp.stack([dp_index * pages])
    args = (request_page_count, page_slot_table)
    q, *kvs = project(*args, owners, bases, xs, weight, downs, ups, pages)
    bias_rows = jnp.pad(jnp.stack(three_parts(first_feed_bias)), ((0, 13), (0, 0)))
    out_rows = attention_out_weight.shape[0]
    if shared:
        unit = hidden_dev // 8
        turn = (dp_index % 2) * 4 + dp_index // 2
        kv_x = [move(kv, across) for kv in kvs]
        kv_y = [move(kv, along) for kv in kvs]
        first = lax.dynamic_slice_in_dim(first_feed_weight, turn * unit, unit, 1)
        first, _, _ = lax.optimization_barrier((first, ups, weight))
        first = lax.all_gather(first, "mp", axis=0)
        step = functools.partial(attend, *args)
        state = step(bases, bases, q, kvs, None, False, pages)
        rest = jnp.concatenate(
            [
                lax.dynamic_slice_in_dim(second_feed_weight, turn * unit, unit, 0),
                lax.dynamic_slice_in_dim(
                    attention_out_weight, (dp_index % 2) * (out_rows // 2), out_rows // 2, 0
                ),
                bias_rows,
            ],
            axis=0,
        )
        rest, _ = lax.optimization_barrier((rest, kvs))
        rest = lax.all_gather(rest, "mp", axis=0)
        kv_x, kv_y, state, first = lax.optimization_barrier((kv_x, kv_y, state, first))
        kv_d0 = move(kv_y[0], across)
        kv_d1 = move(kv_x[1], along)
        near = [at(2), at(3), at(4), at(5)]
        far = [at(6), at(7)]
        swapped, own = bases[1:], bases[:1]
        late = step(
            swapped, jnp.stack(near), q, [*kv_x, *kv_y], state, False, pages, q_from=tok_rows
        )
        first_other = move(first, swap)
        kv_d0, kv_d1, late, first, first_other = lax.optimization_barrier(
            (kv_d0, kv_d1, late, first, first_other)
        )
        first_x = move(first, across)
        first_y = move(first, along)
        theirs = step(
            swapped, jnp.stack(far), q, [kv_d0, kv_d1], late, True, pages, q_from=tok_rows
        )
        theirs, rest, first_x, first_y = lax.optimization_barrier((theirs, rest, first_x, first_y))
        second = rest[:, :unit]
        second_x = move(second, across)
        second_y = move(second, along)
        cut = width // 2
        first_d0 = move(first_y[:, :cut], across)
        first_d1 = move(first_x[:, cut:], along)
        rest_other = move(rest, swap)
        theirs, state = lax.optimization_barrier((move(theirs, swap), state))
        theirs = lax.all_gather(theirs, "mp", axis=0)
        mine = step(
            own, jnp.stack(near + far), q, [*kv_x, *kv_y, kv_d0, kv_d1], state, True, pages
        )
        mine_all = lax.all_gather(mine, "mp", axis=0)
        theirs, _, first_x, first_y, first_d0, first_d1, second_x, second_y, rest_other = (
            lax.optimization_barrier(
                (
                    theirs, mine, first_x, first_y, first_d0, first_d1, second_x, second_y,
                    rest_other,
                )
            )
        )
        half = unit // 2
        second_d0 = move(second_y[:, :half], across)
        second_d1 = move(second_x[:, half:], along)
        firsts = [first, first_x, first_y, first_d0, first_d1]
        first_others = [first_other] + [move(piece, swap) for piece in firsts[1:]]
        seconds = [second_x, second_y, second_d0, second_d1]
        second_others = [move(piece, swap) for piece in seconds[:3]]
        last, mine_all = lax.optimization_barrier((second_d1, mine_all))
        second_others.append(move(last, swap))
        contexts = [mine_all, theirs]
        bias_rows = rest
        seconds = [rest, *seconds]
        second_others = [rest_other, *second_others]
        sets = [(firsts, seconds), (first_others, second_others)]
        outs = [rest, rest_other]
    else:
        everything = lax.all_gather(kvs[0], "dp", axis=0, tiled=True)
        context = attend(
            *args, bases, jnp.zeros((1,), jnp.int32), q, [everything], None, True, pages
        )
        second = lax.all_gather(second_feed_weight, "mp", axis=0)
        bias_rows = lax.all_gather(bias_rows, "mp", axis=0)
        sets = [([lax.all_gather(first_feed_weight, "mp", axis=0)], [second])]
        outs = [lax.all_gather(attention_out_weight, "mp", axis=0)]
        contexts = [lax.all_gather(context, "mp", axis=0)]
    layer_rows, next_proj = finish(
        place, tokens, contexts, outs, first_norm_gain, first_norm_bias, bias_rows, sets,
        second_feed_bias, second_norm_gain, second_norm_bias, following_qkv_weight,
        following_bias, tok_rows // mp_count,
    )
    return (layer_rows, next_proj)


def solution(mesh):
    placed = (
        P("dp", None),
        P(None, "mp"),
        P(None, "mp"),
        P("mp", None),
        P("mp", None),
        P(),
        P(),
        P(None, "mp"),
        P("mp"),
        P("mp", None),
        P(),
        P(),
        P(),
        P(None, "mp"),
        P("mp"),
        P(),
        P(),
        P(),
    )
    return jax.shard_map(
        local,
        mesh=mesh,
        in_specs=placed,
        out_specs=(P(("dp", "mp"), None), P("dp", "mp")),
        check_vma=False,
    )
```

```python
import functools
import math

import jax
import jax.numpy as jnp
from jax import lax
from jax.experimental import pallas as pl
from jax.experimental.pallas import tpu as pltpu
from jax.sharding import PartitionSpec as P

HEAD_DIM = 64
ADAPTER_RANK = 16
PAGE = 128
PAIR = 2 * HEAD_DIM
NEG = -1e30
EXP_SCALE = math.log2(math.e) * HEAD_DIM**-0.5
MIB = 1 << 20


def params(vmem):
    return pltpu.CompilerParams(
        dimension_semantics=("arbitrary",), vmem_limit_bytes=vmem * MIB
    )


def request_of(k, counts, requests):
    end = counts[0]
    request = (k >= end).astype(jnp.int32)
    for r in range(1, requests - 1):
        end = end + counts[r]
        request = request + (k >= end).astype(jnp.int32)
    return request


def normalize(values, gain_row, bias_row):
    average = jnp.mean(values, axis=-1, keepdims=True)
    centered = values - average
    variance = jnp.mean(centered * centered, axis=-1, keepdims=True)
    return centered * lax.rsqrt(variance + 1e-05) * gain_row + bias_row


def project_kernel(
    counts, table, owners, bases, *refs, requests, slots, pages, per_piece, parts,
):
    x_refs = refs[:parts]
    w_ref, down_ref, up_ref, q_ref = refs[parts : parts + 4]
    kv_refs = refs[parts + 4 : 2 * parts + 4]
    joined, page_owner = refs[2 * parts + 4 :]
    step = pl.program_id(0)
    cols = w_ref.shape[1]

    @pl.when(step == 0)
    def _():
        joined[:, :cols] = w_ref[...]
        joined[:, cols:] = down_ref[...]

        def fill(k, carry):
            page_owner[table[k]] = owners[request_of(k, counts, requests)]
            return carry

        lax.fori_loop(0, slots, fill, 0)

    piece = step * pages // per_piece

    def block(x_ref, kv_ref):
        both = jnp.dot(x_ref[...], joined[...], preferred_element_type=jnp.float32)
        low = both[:, cols:]
        lane_owner = lax.broadcasted_iota(jnp.int32, (PAGE, low.shape[1]), 1) // ADAPTER_RANK
        kept = []
        for p in range(pages):
            page = step * pages + p
            slot = bases[page // per_piece] + page % per_piece
            kept.append(
                jnp.where(lane_owner == page_owner[slot], low[p * PAGE : (p + 1) * PAGE], 0.0)
            )
        low_rank = jnp.concatenate(kept, axis=0).astype(jnp.bfloat16)
        rows = both[:, :cols] + jnp.dot(
            low_rank, up_ref[...], preferred_element_type=jnp.float32
        )
        rows = rows.astype(jnp.bfloat16)
        q_cols = q_ref.shape[1]
        q_ref[...] = rows[:, :q_cols]
        keys = rows[:, q_cols : 2 * q_cols]
        values = rows[:, 2 * q_cols :]
        for p in range(pages):
            here = slice(p * PAGE, (p + 1) * PAGE)
            kv_ref[p, :PAIR, :] = keys[here].T
            kv_ref[p, PAIR:, :] = values[here]

    for i in range(parts):
        pl.when(piece == i)(functools.partial(block, x_refs[i], kv_refs[i]))


def project(counts, table, owners, bases, xs, weight, down, up, per_piece):
    tok, width = xs[0].shape
    cols = weight.shape[1]
    pages = min(4, tok // PAGE)
    rows_step = pages * PAGE
    slots = table.shape[0]
    parts = len(xs)
    each = tok // rows_step
    total = tok * parts
    whole = lambda i, *_: (0, 0)
    rows = lambda i, *_: (i, 0)

    def own(part, *zeros):
        return lambda i, *_: (jnp.clip(i - part * each, 0, each - 1), 0, *zeros)

    return pl.pallas_call(
        functools.partial(
            project_kernel,
            requests=counts.shape[0], slots=slots, pages=pages, per_piece=per_piece, parts=parts,
        ),
        grid_spec=pltpu.PrefetchScalarGridSpec(
            num_scalar_prefetch=4,
            grid=(total // rows_step,),
            in_specs=[pl.BlockSpec((rows_step, width), own(i)) for i in range(parts)]
            + [
                pl.BlockSpec(weight.shape, whole),
                pl.BlockSpec(down.shape, whole),
                pl.BlockSpec(up.shape, whole),
            ],
            out_specs=[
                pl.BlockSpec((rows_step, cols // 3), rows),
            ]
            + [pl.BlockSpec((pages, PAIR + PAGE, PAIR), own(i, 0)) for i in range(parts)],
            scratch_shapes=[
                pltpu.VMEM((width, cols + down.shape[1]), jnp.bfloat16),
                pltpu.SMEM((slots,), jnp.int32),
            ],
        ),
        out_shape=[
            jax.ShapeDtypeStruct((total, cols // 3), jnp.bfloat16),
        ]
        + [jax.ShapeDtypeStruct((tok // PAGE, PAIR + PAGE, PAIR), jnp.bfloat16)] * parts,
        compiler_params=params(62),
        cost_estimate=pl.CostEstimate(
            flops=2 * total * width * cols, bytes_accessed=2 * total * (width + cols),
            transcendentals=0,
        ),
        name="project",
    )(counts, table, owners, bases, *xs, weight, down, up)


def attend_kernel(
    counts, table, q_bases, kv_bases, q_hbm, *refs,
    requests, slots, q_size, q_from, state_from, arrays, sizes, first, last, group,
):
    refs = list(refs)
    kv_hbm = [refs.pop(0) for _ in arrays]
    state_hbm = [] if first else [refs.pop(0), refs.pop(0)]
    if last:
        out_ref = refs.pop(0)
    else:
        acc_out, stat_out = refs.pop(0), refs.pop(0)
    kv, scores, listed, amount, asked, q_amount, sems, q_ref = refs[:8]
    if not first:
        acc_in, stat_in = refs[8:]
    tok = q_ref.shape[0]
    targets = [(q_hbm.at[pl.ds(q_from, tok)], q_ref)]
    offset = 0
    for i, size in enumerate(arrays):
        targets.append((kv_hbm[i], kv.at[pl.ds(offset, size)]))
        offset += size
    targets += [(ref.at[pl.ds(state_from, tok)], own) for ref, own in zip(state_hbm, refs[8:])]
    copies = [
        pltpu.make_async_copy(source, target, sems.at[n])
        for n, (source, target) in enumerate(targets)
    ]
    for copy in copies:
        copy.start()
    for r in range(requests):
        amount[r] = 0
        q_amount[r] = 0

    def place_of(slot, bases, extents):
        place = jnp.int32(-1)
        offset = 0
        for i, size in enumerate(extents):
            near = slot - bases[i]
            place = jnp.where((near >= 0) & (near < size), near + offset, place)
            offset += size
        return place

    q_sizes = (q_size,) * (q_ref.shape[0] // (q_size * PAGE))

    def fill(k, carry):
        r = request_of(k, counts, requests)
        slot = table[k]
        place = place_of(slot, kv_bases, sizes)
        q_place = place_of(slot, q_bases, q_sizes)

        @pl.when(place >= 0)
        def _():
            n = amount[r]
            listed[r, n] = place
            amount[r] = n + 1

        @pl.when(q_place >= 0)
        def _():
            n = q_amount[r]
            asked[r, n] = q_place
            q_amount[r] = n + 1

        return carry

    lax.fori_loop(0, slots, fill, 0)
    for copy in copies:
        copy.wait()
    lane = lax.broadcasted_iota(jnp.int32, (PAGE, PAIR), 1)
    low_lane = lane < HEAD_DIM
    rows = 4 * PAGE

    def one_pair(r, p):
        n = amount[r]
        full = n // group
        blocks = (n + group - 1) // group
        count = q_amount[r]
        a = asked[r, 2 * p]
        b = asked[r, jnp.minimum(2 * p + 1, count - 1)]
        spots = [pl.ds(pl.multiple_of(t * PAGE, PAGE), PAGE) for t in (a, b)]
        parts = []
        for spot in spots:
            q = q_ref[spot, :]
            zero = jnp.zeros_like(q)
            parts += [jnp.where(low_lane, q, zero), jnp.where(low_lane, zero, q)]
        stacked = jnp.concatenate(parts, axis=0)

        def page_of(j, i):
            return listed[r, jnp.minimum(j * group + i, n - 1)]

        def score(masked, j, top):
            keys = jnp.concatenate(
                [kv[page_of(j, i), :PAIR, :] for i in range(group)], axis=1
            )
            s = jnp.dot(stacked, keys, preferred_element_type=jnp.float32)
            for i in range(group):
                piece = s[:, i * PAGE : (i + 1) * PAGE]
                if masked and i:
                    piece = jnp.where(j * group + i < n, piece, NEG)
                scores[j, :, i * PAGE : (i + 1) * PAGE] = piece
                top = jnp.maximum(top, piece)
            return top

        top = jnp.full((rows, PAGE), NEG, jnp.float32)
        top = lax.fori_loop(0, full, functools.partial(score, False), top)
        top = lax.fori_loop(full, blocks, functools.partial(score, True), top)
        peak = jnp.max(top, axis=1, keepdims=True)
        if not first:
            old = jnp.concatenate(
                [stat_in[spot, h : h + 1] for spot in spots for h in (0, 1)], axis=0
            )
            peak = jnp.maximum(peak, old)
        shift = peak * EXP_SCALE

        def weigh(j, carry):
            total, acc = carry
            w = jnp.exp2(scores[j] * EXP_SCALE - shift)
            for i in range(group):
                total = total + w[:, i * PAGE : (i + 1) * PAGE]
            values = jnp.concatenate(
                [kv[page_of(j, i), PAIR:, :] for i in range(group)], axis=0
            )
            acc = acc + jnp.dot(
                w.astype(jnp.bfloat16), values, preferred_element_type=jnp.float32
            )
            return total, acc

        total, acc = lax.fori_loop(
            0, blocks, weigh,
            (jnp.zeros((rows, PAGE), jnp.float32), jnp.zeros((rows, PAIR), jnp.float32)),
        )
        total = jnp.sum(total, axis=1, keepdims=True)
        if not first:
            shrink = jnp.exp2((old - peak) * EXP_SCALE)
            total = total + shrink * jnp.concatenate(
                [stat_in[spot, h : h + 1] for spot in spots for h in (2, 3)], axis=0
            )
        for t, spot in enumerate(spots):
            h0 = slice(2 * t * PAGE, (2 * t + 1) * PAGE)
            h1 = slice((2 * t + 1) * PAGE, (2 * t + 2) * PAGE)
            value = jnp.where(low_lane, acc[h0], acc[h1])
            if not first:
                value = value + acc_in[spot, :] * jnp.where(low_lane, shrink[h0], shrink[h1])
            if last:
                value = value / jnp.where(low_lane, total[h0], total[h1])
                out_ref[spot, :] = value.astype(jnp.bfloat16)
            else:
                acc_out[spot, :] = value
                stat = jnp.where(lane == 0, peak[h0], peak[h1])
                stat = jnp.where(lane == 2, total[h0], stat)
                stat_out[spot, :] = jnp.where(lane == 3, total[h1], stat)

    def visit_request(r, carry):
        def visit(p, inner):
            one_pair(r, p)
            return inner

        return lax.fori_loop(0, (q_amount[r] + 1) // 2, visit, carry)

    lax.fori_loop(0, requests, visit_request, 0)


def attend(counts, table, q_bases, kv_bases, q, pieces, state, last, q_size, q_from=0):
    tok = q_bases.shape[0] * q_size * PAGE
    state_from = 0 if state is None or state[0].shape[0] == tok else q_from
    arrays = tuple(p.shape[0] for p in pieces)
    sizes = (sum(arrays) // kv_bases.shape[0],) * kv_bases.shape[0]
    first = state is None
    group = 4
    slots = table.shape[0]
    requests = counts.shape[0]
    most = min(sum(sizes), slots)
    state_shape = [jax.ShapeDtypeStruct((tok, PAIR), jnp.float32)] * 2
    out = pl.pallas_call(
        functools.partial(
            attend_kernel,
            requests=requests, slots=slots, q_size=q_size, q_from=q_from, state_from=state_from, arrays=arrays, sizes=sizes,
            first=first, last=last, group=group,
        ),
        grid_spec=pltpu.PrefetchScalarGridSpec(
            num_scalar_prefetch=4,
            grid=(1,),
            in_specs=[pl.BlockSpec(memory_space=pl.ANY)] * (len(pieces) + (1 if first else 3)),
            out_specs=[pl.BlockSpec((tok, PAIR), lambda i, *_: (0, 0))] * (1 if last else 2),
            scratch_shapes=[
                pltpu.VMEM((sum(sizes), PAIR + PAGE, PAIR), jnp.bfloat16),
                pltpu.VMEM(((most + group - 1) // group, 4 * PAGE, group * PAGE), jnp.float32),
                pltpu.SMEM((requests, sum(sizes)), jnp.int32),
                pltpu.SMEM((requests,), jnp.int32),
                pltpu.SMEM((requests, tok // PAGE), jnp.int32),
                pltpu.SMEM((requests,), jnp.int32),
                pltpu.SemaphoreType.DMA((len(pieces) + 3,)),
                pltpu.VMEM((tok, PAIR), jnp.bfloat16),
            ]
            + ([] if first else [pltpu.VMEM((tok, PAIR), jnp.float32)] * 2),
        ),
        out_shape=[jax.ShapeDtypeStruct((tok, PAIR), jnp.bfloat16)] if last else state_shape,
        compiler_params=params(62),
        cost_estimate=pl.CostEstimate(
            flops=tok * PAIR, bytes_accessed=4 * tok * PAIR, transcendentals=0,
        ),
        name="attend",
    )(counts, table, q_bases, kv_bases, q, *pieces, *([] if first else state))
    return out[0] if last else out


def finish_kernel(place, x_ref, *refs, parts, counts, last_step):
    refs = list(refs)
    ctx_refs, refs = refs[:parts], refs[parts:]
    out_w_refs, refs = refs[:parts], refs[parts:]
    gain1_ref, bias1_ref, bias_ref = refs[:3]
    refs = refs[3:]
    sets = []
    for n1, n2 in counts:
        w1s, refs = refs[:n1], refs[n1:]
        w2s, refs = refs[:n2], refs[n2:]
        sets.append((w1s, w2s))
    b2_ref, gain_ref, bias2_ref, next_w_ref, next_b_ref = refs[:5]
    layer_ref, next_ref, joined, normed_ref, acc, done = refs[5:]
    step = pl.program_id(0)
    tok = normed_ref.shape[0]
    block = min(512, tok)
    halves = len(sets)
    groups = (last_step + 1) // halves

    @pl.when(step == 0)
    def _():
        near = joined.shape[1] // parts
        for i in range(parts):
            joined[:, i * near : (i + 1) * near] = out_w_refs[i][:, :near]
        for t in range(tok // block):
            rows = slice(t * block, (t + 1) * block)
            mixed = x_ref[rows, :].astype(jnp.float32)
            for j in range(joined.shape[0]):
                ctx = jnp.concatenate([ref[j, rows, :] for ref in ctx_refs], axis=1)
                mixed = mixed + jnp.dot(ctx, joined[j], preferred_element_type=jnp.float32)
            normed = normalize(mixed, gain1_ref[...], bias1_ref[...]).astype(jnp.bfloat16)
            normed_ref[rows, :] = normed
            acc[rows, :] = normed.astype(jnp.float32) + b2_ref[...]

    def absorb(h, w1_refs, w2_refs):
        if len(w1_refs) == 1:
            w1 = w1_refs[0][0]
            starts, cols = [0], w1.shape[1]
        else:
            diagonal = jnp.concatenate([w1_refs[3][0], w1_refs[4][0]], axis=0)
            w1 = jnp.concatenate([ref[0] for ref in w1_refs[:3]] + [diagonal], axis=1)
            cols = diagonal.shape[1]
            core = place[2] if h == 0 else 1 - place[2]
            starts = [
                pl.multiple_of((core * 4 + (place[1] ^ r)) * cols, cols) for r in range(4)
            ]
        w2 = jnp.concatenate([ref[0] for ref in w2_refs], axis=0)
        bias = jnp.concatenate(
            [
                jnp.sum(
                    bias_ref[0, :, pl.ds(start, cols)].astype(jnp.float32), axis=0, keepdims=True
                )
                for start in starts
            ],
            axis=1,
        )
        for t in range(tok // block):
            rows = slice(t * block, (t + 1) * block)
            pre = jnp.dot(normed_ref[rows, :], w1, preferred_element_type=jnp.float32) + bias
            hidden = 0.5 * pre * (1.0 + lax.erf(pre * math.sqrt(0.5)))
            acc[rows, :] += jnp.dot(
                hidden.astype(jnp.bfloat16), w2, preferred_element_type=jnp.float32
            )

    for h in range(halves):
        pl.when(step // groups == h)(functools.partial(absorb, h, *sets[h]))

    @pl.when(step == last_step)
    def _():
        for t in range(tok // block):
            rows = slice(t * block, (t + 1) * block)
            layer = normalize(acc[rows, :], gain_ref[...], bias2_ref[...]).astype(jnp.bfloat16)
            done[rows, :] = layer
            next_ref[rows, :] = (
                jnp.dot(layer, next_w_ref[...], preferred_element_type=jnp.float32)
                + next_b_ref[...]
            ).astype(jnp.bfloat16)
        share = layer_ref.shape[0]
        layer_ref[...] = done[pl.ds(pl.multiple_of(place[0] * share, share), share), :]


def finish(
    place, x, contexts, outs, gain1, bias1, bias, sets, b2, gain, bias2, next_w, next_b, share
):
    tok, width = x.shape
    halves = len(sets)
    groups = bias.shape[0]
    ctx_cols = sum(ctx.shape[2] for ctx in contexts)
    cols = bias.shape[2] // halves
    steps = halves * groups
    out_at = 1 if len(outs) > 1 else 0

    def whole(array):
        return pl.BlockSpec(
            array.shape, lambda i, *_: (0,) * array.ndim, pipeline_mode=pl.Buffered(1)
        )

    specs, arrays = [], []
    for h, (w1s, w2s) in enumerate(sets):
        at = lambda i, *_, h=h: (jnp.clip(i - h * groups, 0, groups - 1), 0, 0)
        for n, array in enumerate((*w1s, *w2s)):
            rows = array.shape[1]
            if len(w1s) > 1 and n == len(w1s):
                rows = w1s[0].shape[2]
            specs.append(pl.BlockSpec((1, rows, array.shape[2]), at))
            arrays.append(array)
    head = [x, *contexts, *outs, gain1[None], bias1[None]]
    tail = [b2[None], gain[None], bias2[None], next_w, next_b[None]]
    next_cols = next_w.shape[1]
    fixed = lambda i, *_: (0, 0)
    return pl.pallas_call(
        functools.partial(
            finish_kernel,
            parts=len(outs),
            counts=tuple((len(w1s), len(w2s)) for w1s, w2s in sets),
            last_step=steps - 1,
        ),
        grid_spec=pltpu.PrefetchScalarGridSpec(
            num_scalar_prefetch=1,
            grid=(steps,),
            in_specs=[whole(array) for array in head[: 1 + len(contexts)]]
            + [
                pl.BlockSpec(
                    (groups, ctx_cols // len(outs), width), lambda i, *_: (0, out_at, 0),
                    pipeline_mode=pl.Buffered(1),
                )
                for _ in outs
            ]
            + [whole(array) for array in head[1 + len(contexts) + len(outs) :]]
            + [
                pl.BlockSpec(
                    (1, 16, bias.shape[2]),
                    lambda i, *_: (i % groups, bias.shape[1] // 16 - 1, 0),
                ),
            ]
            + specs
            + [whole(array) for array in tail],
            out_specs=[
                pl.BlockSpec((share, width), fixed),
                pl.BlockSpec((tok, next_cols), fixed),
            ],
            scratch_shapes=[
                pltpu.VMEM((groups, ctx_cols, width), jnp.bfloat16),
                pltpu.VMEM((tok, width), jnp.bfloat16),
                pltpu.VMEM((tok, width), jnp.float32),
                pltpu.VMEM((tok, width), jnp.bfloat16),
            ],
        ),
        out_shape=[
            jax.ShapeDtypeStruct((share, width), jnp.bfloat16),
            jax.ShapeDtypeStruct((tok, next_cols), jnp.bfloat16),
        ],
        compiler_params=params(62),
        cost_estimate=pl.CostEstimate(
            flops=4 * tok * width * cols * steps, bytes_accessed=4 * width * cols * steps,
            transcendentals=tok * cols * steps,
        ),
        name="finish",
    )(place, *head, bias, *arrays, *tail)


def three_parts(values):
    high = lax.reduce_precision(values, 8, 7)
    middle = lax.reduce_precision(values - high, 8, 7)
    rest = values - high - middle
    return [part.astype(jnp.bfloat16) for part in (high, middle, rest)]


def local(
    tokens,
    query_key_value_weight,
    adapter_down_weight,
    adapter_up_weight,
    attention_out_weight,
    first_norm_gain,
    first_norm_bias,
    first_feed_weight,
    first_feed_bias,
    second_feed_weight,
    second_feed_bias,
    second_norm_gain,
    second_norm_bias,
    following_qkv_weight,
    following_bias,
    request_page_count,
    page_slot_table,
    request_adapter,
):
    tok_rows, width = tokens.shape
    dp_count = lax.axis_size("dp")
    mp_count = lax.axis_size("mp")
    dp_index = lax.axis_index("dp")
    mp_index = lax.axis_index("mp")
    kept_values = adapter_down_weight.shape[1] // ADAPTER_RANK
    heads_dev = query_key_value_weight.shape[1] // (3 * HEAD_DIM)
    pages = tok_rows // PAGE
    shared = dp_count == 8 and heads_dev == 4

    owners = request_adapter // kept_values
    level = jnp.sum(jnp.where(owners == mp_index, request_adapter % kept_values, 0))
    down = lax.dynamic_slice_in_dim(
        adapter_down_weight, level * ADAPTER_RANK, ADAPTER_RANK, 1
    )
    up = lax.dynamic_slice_in_dim(adapter_up_weight, level * ADAPTER_RANK, ADAPTER_RANK, 0)
    up_cols = up.shape[1] // mp_count
    sent = jnp.concatenate(
        [
            jnp.broadcast_to(down.T[:, None, :], (ADAPTER_RANK, mp_count, width)),
            up.reshape(ADAPTER_RANK, mp_count, up_cols),
        ],
        axis=2,
    ).reshape(ADAPTER_RANK, mp_count * (width + up_cols))
    got = lax.all_to_all(sent, "mp", split_axis=1, concat_axis=0, tiled=True)

    def by_kind(matrix):
        split = matrix.reshape(matrix.shape[0], heads_dev, 3, HEAD_DIM)
        if shared:
            split = lax.dynamic_slice_in_dim(split, (dp_index % 2) * 2, 2, 1)
        return jnp.swapaxes(split, 1, 2).reshape(matrix.shape[0], -1)

    place = jnp.stack(
        [mp_index] + ([dp_index // 2, dp_index % 2] if shared else [0, 0])
    ).astype(jnp.int32)
    hidden_dev = first_feed_weight.shape[1]
    downs = got[:, :width].T
    ups = got[:, width:]
    weight = by_kind(query_key_value_weight)
    ups = by_kind(ups)
    if shared:
        swap = [(i, i ^ 1) for i in range(8)]
        across = [(i, i ^ 2) for i in range(8)]
        along = [(i, i ^ 4) for i in range(8)]
        move = lambda value, pairs: lax.ppermute(value, "dp", pairs)
        xs = [tokens, move(tokens, swap)]
        at = lambda flip: (dp_index ^ flip) * pages
        bases = jnp.stack([at(0), at(1)])
    else:
        xs = [tokens]
        bases = jnp.stack([dp_index * pages])
    args = (request_page_count, page_slot_table)
    q, *kvs = project(*args, owners, bases, xs, weight, downs, ups, pages)
    bias_rows = jnp.pad(jnp.stack(three_parts(first_feed_bias)), ((0, 13), (0, 0)))
    out_rows = attention_out_weight.shape[0]
    if shared:
        unit = hidden_dev // 8
        turn = (dp_index % 2) * 4 + dp_index // 2
        kv_x = [move(kv, across) for kv in kvs]
        kv_y = [move(kv, along) for kv in kvs]
        first = lax.dynamic_slice_in_dim(first_feed_weight, turn * unit, unit, 1)
        first, _, _ = lax.optimization_barrier((first, ups, weight))
        first = lax.all_gather(first, "mp", axis=0)
        step = functools.partial(attend, *args)
        state = step(bases, bases, q, kvs, None, False, pages)
        second_map, out_map, bias_rows, _ = lax.optimization_barrier(
            (second_feed_weight, attention_out_weight, bias_rows, kvs)
        )
        rest = jnp.concatenate(
            [
                lax.dynamic_slice_in_dim(second_map, turn * unit, unit, 0),
                lax.dynamic_slice_in_dim(
                    out_map, (dp_index % 2) * (out_rows // 2), out_rows // 2, 0
                ),
                bias_rows,
            ],
            axis=0,
        )
        rest = lax.all_gather(rest, "mp", axis=0)
        kv_x, kv_y, state, first = lax.optimization_barrier((kv_x, kv_y, state, first))
        kv_d0 = move(kv_y[0], across)
        kv_d1 = move(kv_x[1], along)
        first_x = move(first, across)
        first_y = move(first, along)
        near = [at(2), at(3), at(4), at(5)]
        far = [at(6), at(7)]
        swapped, own = bases[1:], bases[:1]
        late = step(
            swapped, jnp.stack(near), q, [*kv_x, *kv_y], state, False, pages, q_from=tok_rows
        )
        own_late = step(own, jnp.stack(near), q, [*kv_x, *kv_y], state, False, pages)
        kv_d0, kv_d1, late, own_late = lax.optimization_barrier((kv_d0, kv_d1, late, own_late))
        theirs = step(
            swapped, jnp.stack(far), q, [kv_d0, kv_d1], late, True, pages, q_from=tok_rows
        )
        theirs, rest, first_x, first_y = lax.optimization_barrier((theirs, rest, first_x, first_y))
        second = rest[:, :unit]
        second_x = move(second, across)
        second_y = move(second, along)
        cut = width // 2
        first_d0 = move(first_y[:, :cut], across)
        first_d1 = move(first_x[:, cut:], along)
        theirs, own_late, rest = lax.optimization_barrier((move(theirs, swap), own_late, rest))
        rest_other = move(rest, swap)
        theirs = lax.all_gather(theirs, "mp", axis=0)
        mine = step(own, jnp.stack(far), q, [kv_d0, kv_d1], own_late, True, pages)
        mine_all = lax.all_gather(mine, "mp", axis=0)
        theirs, _, first, first_x, first_y, first_d0, first_d1, second_x, second_y, rest_other = (
            lax.optimization_barrier(
                (
                    theirs, mine, first, first_x, first_y, first_d0, first_d1, second_x,
                    second_y, rest_other,
                )
            )
        )
        half = unit // 2
        second_d0 = move(second_y[:, :half], across)
        second_d1 = move(second_x[:, half:], along)
        firsts = [first, first_x, first_y, first_d0, first_d1]
        first_others = [move(piece, swap) for piece in firsts]
        seconds = [second_x, second_y, second_d0, second_d1]
        second_others = [move(piece, swap) for piece in seconds[:3]]
        last, mine_all = lax.optimization_barrier((second_d1, mine_all))
        second_others.append(move(last, swap))
        contexts = [mine_all, theirs]
        bias_rows = rest
        seconds = [rest, *seconds]
        second_others = [rest_other, *second_others]
        sets = [(firsts, seconds), (first_others, second_others)]
        outs = [rest, rest_other]
    else:
        everything = lax.all_gather(kvs[0], "dp", axis=0, tiled=True)
        context = attend(
            *args, bases, jnp.zeros((1,), jnp.int32), q, [everything], None, True, pages
        )
        second = lax.all_gather(second_feed_weight, "mp", axis=0)
        bias_rows = lax.all_gather(bias_rows, "mp", axis=0)
        sets = [([lax.all_gather(first_feed_weight, "mp", axis=0)], [second])]
        outs = [lax.all_gather(attention_out_weight, "mp", axis=0)]
        contexts = [lax.all_gather(context, "mp", axis=0)]
    layer_rows, next_proj = finish(
        place, tokens, contexts, outs, first_norm_gain, first_norm_bias, bias_rows, sets,
        second_feed_bias, second_norm_gain, second_norm_bias, following_qkv_weight,
        following_bias, tok_rows // mp_count,
    )
    return (layer_rows, next_proj)


def solution(mesh):
    placed = (
        P("dp", None),
        P(None, "mp"),
        P(None, "mp"),
        P("mp", None),
        P("mp", None),
        P(),
        P(),
        P(None, "mp"),
        P("mp"),
        P("mp", None),
        P(),
        P(),
        P(),
        P(None, "mp"),
        P("mp"),
        P(),
        P(),
        P(),
    )
    return jax.shard_map(
        local,
        mesh=mesh,
        in_specs=placed,
        out_specs=(P(("dp", "mp"), None), P("dp", "mp")),
        check_vma=False,
    )
```

```python
import functools
import math

import jax
import jax.numpy as jnp
from jax import lax
from jax.experimental import pallas as pl
from jax.experimental.pallas import tpu as pltpu
from jax.sharding import PartitionSpec as P

HEAD_DIM = 64
ADAPTER_RANK = 16
PAGE = 128
PAIR = 2 * HEAD_DIM
NEG = -1e30
EXP_SCALE = math.log2(math.e) * HEAD_DIM**-0.5
MIB = 1 << 20


def params(vmem):
    return pltpu.CompilerParams(
        dimension_semantics=("arbitrary",), vmem_limit_bytes=vmem * MIB
    )


def request_of(k, counts, requests):
    end = counts[0]
    request = (k >= end).astype(jnp.int32)
    for r in range(1, requests - 1):
        end = end + counts[r]
        request = request + (k >= end).astype(jnp.int32)
    return request


def normalize(values, gain_row, bias_row):
    average = jnp.mean(values, axis=-1, keepdims=True)
    centered = values - average
    variance = jnp.mean(centered * centered, axis=-1, keepdims=True)
    return centered * lax.rsqrt(variance + 1e-05) * gain_row + bias_row


def project_kernel(
    counts, table, owners, bases, *refs, requests, slots, pages, per_piece, parts,
):
    x_refs = refs[:parts]
    w_ref, down_ref, up_ref, q_ref = refs[parts : parts + 4]
    kv_refs = refs[parts + 4 : 2 * parts + 4]
    joined, page_owner = refs[2 * parts + 4 :]
    step = pl.program_id(0)
    cols = w_ref.shape[1]

    @pl.when(step == 0)
    def _():
        joined[:, :cols] = w_ref[...]
        joined[:, cols:] = down_ref[...]

        def fill(k, carry):
            page_owner[table[k]] = owners[request_of(k, counts, requests)]
            return carry

        lax.fori_loop(0, slots, fill, 0)

    piece = step * pages // per_piece

    def block(x_ref, kv_ref):
        both = jnp.dot(x_ref[...], joined[...], preferred_element_type=jnp.float32)
        low = both[:, cols:]
        lane_owner = lax.broadcasted_iota(jnp.int32, (PAGE, low.shape[1]), 1) // ADAPTER_RANK
        kept = []
        for p in range(pages):
            page = step * pages + p
            slot = bases[page // per_piece] + page % per_piece
            kept.append(
                jnp.where(lane_owner == page_owner[slot], low[p * PAGE : (p + 1) * PAGE], 0.0)
            )
        low_rank = jnp.concatenate(kept, axis=0).astype(jnp.bfloat16)
        rows = both[:, :cols] + jnp.dot(
            low_rank, up_ref[...], preferred_element_type=jnp.float32
        )
        rows = rows.astype(jnp.bfloat16)
        q_cols = q_ref.shape[1]
        q_ref[...] = rows[:, :q_cols]
        keys = rows[:, q_cols : 2 * q_cols]
        values = rows[:, 2 * q_cols :]
        for p in range(pages):
            here = slice(p * PAGE, (p + 1) * PAGE)
            kv_ref[p, :PAIR, :] = keys[here].T
            kv_ref[p, PAIR:, :] = values[here]

    for i in range(parts):
        pl.when(piece == i)(functools.partial(block, x_refs[i], kv_refs[i]))


def project(counts, table, owners, bases, xs, weight, down, up, per_piece):
    tok, width = xs[0].shape
    cols = weight.shape[1]
    pages = min(4, tok // PAGE)
    rows_step = pages * PAGE
    slots = table.shape[0]
    parts = len(xs)
    each = tok // rows_step
    total = tok * parts
    whole = lambda i, *_: (0, 0)
    rows = lambda i, *_: (i, 0)

    def own(part, *zeros):
        return lambda i, *_: (jnp.clip(i - part * each, 0, each - 1), 0, *zeros)

    return pl.pallas_call(
        functools.partial(
            project_kernel,
            requests=counts.shape[0], slots=slots, pages=pages, per_piece=per_piece, parts=parts,
        ),
        grid_spec=pltpu.PrefetchScalarGridSpec(
            num_scalar_prefetch=4,
            grid=(total // rows_step,),
            in_specs=[pl.BlockSpec((rows_step, width), own(i)) for i in range(parts)]
            + [
                pl.BlockSpec(weight.shape, whole),
                pl.BlockSpec(down.shape, whole),
                pl.BlockSpec(up.shape, whole),
            ],
            out_specs=[
                pl.BlockSpec((rows_step, cols // 3), rows),
            ]
            + [pl.BlockSpec((pages, PAIR + PAGE, PAIR), own(i, 0)) for i in range(parts)],
            scratch_shapes=[
                pltpu.VMEM((width, cols + down.shape[1]), jnp.bfloat16),
                pltpu.SMEM((slots,), jnp.int32),
            ],
        ),
        out_shape=[
            jax.ShapeDtypeStruct((total, cols // 3), jnp.bfloat16),
        ]
        + [jax.ShapeDtypeStruct((tok // PAGE, PAIR + PAGE, PAIR), jnp.bfloat16)] * parts,
        compiler_params=params(62),
        cost_estimate=pl.CostEstimate(
            flops=2 * total * width * cols, bytes_accessed=2 * total * (width + cols),
            transcendentals=0,
        ),
        name="project",
    )(counts, table, owners, bases, *xs, weight, down, up)


def attend_kernel(
    counts, table, q_bases, kv_bases, q_hbm, *refs,
    requests, slots, q_size, q_from, state_from, arrays, sizes, first, last, group,
):
    refs = list(refs)
    kv_hbm = [refs.pop(0) for _ in arrays]
    state_hbm = [] if first else [refs.pop(0), refs.pop(0)]
    if last:
        out_ref = refs.pop(0)
    else:
        acc_out, stat_out = refs.pop(0), refs.pop(0)
    kv, scores, listed, amount, asked, q_amount, sems, q_ref = refs[:8]
    if not first:
        acc_in, stat_in = refs[8:]
    tok = q_ref.shape[0]
    targets = [(q_hbm.at[pl.ds(q_from, tok)], q_ref)]
    offset = 0
    for i, size in enumerate(arrays):
        targets.append((kv_hbm[i], kv.at[pl.ds(offset, size)]))
        offset += size
    targets += [(ref.at[pl.ds(state_from, tok)], own) for ref, own in zip(state_hbm, refs[8:])]
    copies = [
        pltpu.make_async_copy(source, target, sems.at[n])
        for n, (source, target) in enumerate(targets)
    ]
    for copy in copies:
        copy.start()
    for r in range(requests):
        amount[r] = 0
        q_amount[r] = 0

    def place_of(slot, bases, extents):
        place = jnp.int32(-1)
        offset = 0
        for i, size in enumerate(extents):
            near = slot - bases[i]
            place = jnp.where((near >= 0) & (near < size), near + offset, place)
            offset += size
        return place

    q_sizes = (q_size,) * (q_ref.shape[0] // (q_size * PAGE))

    def fill(k, carry):
        r = request_of(k, counts, requests)
        slot = table[k]
        place = place_of(slot, kv_bases, sizes)
        q_place = place_of(slot, q_bases, q_sizes)

        @pl.when(place >= 0)
        def _():
            n = amount[r]
            listed[r, n] = place
            amount[r] = n + 1

        @pl.when(q_place >= 0)
        def _():
            n = q_amount[r]
            asked[r, n] = q_place
            q_amount[r] = n + 1

        return carry

    lax.fori_loop(0, slots, fill, 0)
    for copy in copies:
        copy.wait()
    lane = lax.broadcasted_iota(jnp.int32, (PAGE, PAIR), 1)
    low_lane = lane < HEAD_DIM
    rows = 4 * PAGE

    def one_pair(r, p):
        n = amount[r]
        full = n // group
        blocks = (n + group - 1) // group
        count = q_amount[r]
        a = asked[r, 2 * p]
        b = asked[r, jnp.minimum(2 * p + 1, count - 1)]
        spots = [pl.ds(pl.multiple_of(t * PAGE, PAGE), PAGE) for t in (a, b)]
        parts = []
        for spot in spots:
            q = q_ref[spot, :]
            zero = jnp.zeros_like(q)
            parts += [jnp.where(low_lane, q, zero), jnp.where(low_lane, zero, q)]
        stacked = jnp.concatenate(parts, axis=0)

        def page_of(j, i):
            return listed[r, jnp.minimum(j * group + i, n - 1)]

        def score(masked, j, top):
            keys = jnp.concatenate(
                [kv[page_of(j, i), :PAIR, :] for i in range(group)], axis=1
            )
            s = jnp.dot(stacked, keys, preferred_element_type=jnp.float32)
            for i in range(group):
                piece = s[:, i * PAGE : (i + 1) * PAGE]
                if masked and i:
                    piece = jnp.where(j * group + i < n, piece, NEG)
                scores[j, :, i * PAGE : (i + 1) * PAGE] = piece
                top = jnp.maximum(top, piece)
            return top

        top = jnp.full((rows, PAGE), NEG, jnp.float32)
        top = lax.fori_loop(0, full, functools.partial(score, False), top)
        top = lax.fori_loop(full, blocks, functools.partial(score, True), top)
        peak = jnp.max(top, axis=1, keepdims=True)
        if not first:
            old = jnp.concatenate(
                [stat_in[spot, h : h + 1] for spot in spots for h in (0, 1)], axis=0
            )
            peak = jnp.maximum(peak, old)
        shift = peak * EXP_SCALE

        def weigh(j, carry):
            total, acc = carry
            w = jnp.exp2(scores[j] * EXP_SCALE - shift)
            for i in range(group):
                total = total + w[:, i * PAGE : (i + 1) * PAGE]
            values = jnp.concatenate(
                [kv[page_of(j, i), PAIR:, :] for i in range(group)], axis=0
            )
            acc = acc + jnp.dot(
                w.astype(jnp.bfloat16), values, preferred_element_type=jnp.float32
            )
            return total, acc

        total, acc = lax.fori_loop(
            0, blocks, weigh,
            (jnp.zeros((rows, PAGE), jnp.float32), jnp.zeros((rows, PAIR), jnp.float32)),
        )
        total = jnp.sum(total, axis=1, keepdims=True)
        if not first:
            shrink = jnp.exp2((old - peak) * EXP_SCALE)
            total = total + shrink * jnp.concatenate(
                [stat_in[spot, h : h + 1] for spot in spots for h in (2, 3)], axis=0
            )
        for t, spot in enumerate(spots):
            h0 = slice(2 * t * PAGE, (2 * t + 1) * PAGE)
            h1 = slice((2 * t + 1) * PAGE, (2 * t + 2) * PAGE)
            value = jnp.where(low_lane, acc[h0], acc[h1])
            if not first:
                value = value + acc_in[spot, :] * jnp.where(low_lane, shrink[h0], shrink[h1])
            if last:
                value = value / jnp.where(low_lane, total[h0], total[h1])
                out_ref[spot, :] = value.astype(jnp.bfloat16)
            else:
                acc_out[spot, :] = value
                stat = jnp.where(lane == 0, peak[h0], peak[h1])
                stat = jnp.where(lane == 2, total[h0], stat)
                stat_out[spot, :] = jnp.where(lane == 3, total[h1], stat)

    def visit_request(r, carry):
        def visit(p, inner):
            one_pair(r, p)
            return inner

        return lax.fori_loop(0, (q_amount[r] + 1) // 2, visit, carry)

    lax.fori_loop(0, requests, visit_request, 0)


def attend(counts, table, q_bases, kv_bases, q, pieces, state, last, q_size, q_from=0):
    tok = q_bases.shape[0] * q_size * PAGE
    state_from = 0 if state is None or state[0].shape[0] == tok else q_from
    arrays = tuple(p.shape[0] for p in pieces)
    sizes = (sum(arrays) // kv_bases.shape[0],) * kv_bases.shape[0]
    first = state is None
    group = 4
    slots = table.shape[0]
    requests = counts.shape[0]
    most = min(sum(sizes), slots)
    state_shape = [jax.ShapeDtypeStruct((tok, PAIR), jnp.float32)] * 2
    out = pl.pallas_call(
        functools.partial(
            attend_kernel,
            requests=requests, slots=slots, q_size=q_size, q_from=q_from, state_from=state_from, arrays=arrays, sizes=sizes,
            first=first, last=last, group=group,
        ),
        grid_spec=pltpu.PrefetchScalarGridSpec(
            num_scalar_prefetch=4,
            grid=(1,),
            in_specs=[pl.BlockSpec(memory_space=pl.ANY)] * (len(pieces) + (1 if first else 3)),
            out_specs=[pl.BlockSpec((tok, PAIR), lambda i, *_: (0, 0))] * (1 if last else 2),
            scratch_shapes=[
                pltpu.VMEM((sum(sizes), PAIR + PAGE, PAIR), jnp.bfloat16),
                pltpu.VMEM(((most + group - 1) // group, 4 * PAGE, group * PAGE), jnp.float32),
                pltpu.SMEM((requests, sum(sizes)), jnp.int32),
                pltpu.SMEM((requests,), jnp.int32),
                pltpu.SMEM((requests, tok // PAGE), jnp.int32),
                pltpu.SMEM((requests,), jnp.int32),
                pltpu.SemaphoreType.DMA((len(pieces) + 3,)),
                pltpu.VMEM((tok, PAIR), jnp.bfloat16),
            ]
            + ([] if first else [pltpu.VMEM((tok, PAIR), jnp.float32)] * 2),
        ),
        out_shape=[jax.ShapeDtypeStruct((tok, PAIR), jnp.bfloat16)] if last else state_shape,
        compiler_params=params(62),
        cost_estimate=pl.CostEstimate(
            flops=tok * PAIR, bytes_accessed=4 * tok * PAIR, transcendentals=0,
        ),
        name="attend",
    )(counts, table, q_bases, kv_bases, q, *pieces, *([] if first else state))
    return out[0] if last else out


def finish_kernel(place, x_ref, *refs, parts, counts, last_step):
    refs = list(refs)
    ctx_refs, refs = refs[:parts], refs[parts:]
    out_w_refs, refs = refs[:parts], refs[parts:]
    gain1_ref, bias1_ref, bias_ref = refs[:3]
    refs = refs[3:]
    sets = []
    for n1, n2 in counts:
        w1s, refs = refs[:n1], refs[n1:]
        w2s, refs = refs[:n2], refs[n2:]
        sets.append((w1s, w2s))
    b2_ref, gain_ref, bias2_ref, next_w_ref, next_b_ref = refs[:5]
    layer_ref, next_ref, joined, normed_ref, acc, done = refs[5:]
    step = pl.program_id(0)
    tok = normed_ref.shape[0]
    block = min(512, tok)
    halves = len(sets)
    groups = (last_step + 1) // halves

    @pl.when(step == 0)
    def _():
        near = joined.shape[1] // parts
        for i in range(parts):
            joined[:, i * near : (i + 1) * near] = out_w_refs[i][:, :near]
        for t in range(tok // block):
            rows = slice(t * block, (t + 1) * block)
            mixed = x_ref[rows, :].astype(jnp.float32)
            for j in range(joined.shape[0]):
                ctx = jnp.concatenate([ref[j, rows, :] for ref in ctx_refs], axis=1)
                mixed = mixed + jnp.dot(ctx, joined[j], preferred_element_type=jnp.float32)
            normed = normalize(mixed, gain1_ref[...], bias1_ref[...]).astype(jnp.bfloat16)
            normed_ref[rows, :] = normed
            acc[rows, :] = normed.astype(jnp.float32) + b2_ref[...]

    def absorb(h, w1_refs, w2_refs):
        if len(w1_refs) == 1:
            w1 = w1_refs[0][0]
            starts, cols = [0], w1.shape[1]
        else:
            diagonal = jnp.concatenate([w1_refs[3][0], w1_refs[4][0]], axis=0)
            w1 = jnp.concatenate([ref[0] for ref in w1_refs[:3]] + [diagonal], axis=1)
            cols = diagonal.shape[1]
            core = place[2] if h == 0 else 1 - place[2]
            starts = [
                pl.multiple_of((core * 4 + (place[1] ^ r)) * cols, cols) for r in range(4)
            ]
        w2 = jnp.concatenate([ref[0] for ref in w2_refs], axis=0)
        bias = jnp.concatenate(
            [
                jnp.sum(
                    bias_ref[0, :, pl.ds(start, cols)].astype(jnp.float32), axis=0, keepdims=True
                )
                for start in starts
            ],
            axis=1,
        )
        for t in range(tok // block):
            rows = slice(t * block, (t + 1) * block)
            pre = jnp.dot(normed_ref[rows, :], w1, preferred_element_type=jnp.float32) + bias
            hidden = 0.5 * pre * (1.0 + lax.erf(pre * math.sqrt(0.5)))
            acc[rows, :] += jnp.dot(
                hidden.astype(jnp.bfloat16), w2, preferred_element_type=jnp.float32
            )

    for h in range(halves):
        pl.when(step // groups == h)(functools.partial(absorb, h, *sets[h]))

    @pl.when(step == last_step)
    def _():
        for t in range(tok // block):
            rows = slice(t * block, (t + 1) * block)
            layer = normalize(acc[rows, :], gain_ref[...], bias2_ref[...]).astype(jnp.bfloat16)
            done[rows, :] = layer
            next_ref[rows, :] = (
                jnp.dot(layer, next_w_ref[...], preferred_element_type=jnp.float32)
                + next_b_ref[...]
            ).astype(jnp.bfloat16)
        share = layer_ref.shape[0]
        layer_ref[...] = done[pl.ds(pl.multiple_of(place[0] * share, share), share), :]


def finish(
    place, x, contexts, outs, gain1, bias1, bias, sets, b2, gain, bias2, next_w, next_b, share
):
    tok, width = x.shape
    halves = len(sets)
    groups = bias.shape[0]
    ctx_cols = sum(ctx.shape[2] for ctx in contexts)
    cols = bias.shape[2] // halves
    steps = halves * groups
    out_at = 1 if len(outs) > 1 else 0

    def whole(array):
        return pl.BlockSpec(
            array.shape, lambda i, *_: (0,) * array.ndim, pipeline_mode=pl.Buffered(1)
        )

    specs, arrays = [], []
    for h, (w1s, w2s) in enumerate(sets):
        at = lambda i, *_, h=h: (jnp.clip(i - h * groups, 0, groups - 1), 0, 0)
        for n, array in enumerate((*w1s, *w2s)):
            rows = array.shape[1]
            if len(w1s) > 1 and n == len(w1s):
                rows = w1s[0].shape[2]
            specs.append(pl.BlockSpec((1, rows, array.shape[2]), at))
            arrays.append(array)
    head = [x, *contexts, *outs, gain1[None], bias1[None]]
    tail = [b2[None], gain[None], bias2[None], next_w, next_b[None]]
    next_cols = next_w.shape[1]
    fixed = lambda i, *_: (0, 0)
    return pl.pallas_call(
        functools.partial(
            finish_kernel,
            parts=len(outs),
            counts=tuple((len(w1s), len(w2s)) for w1s, w2s in sets),
            last_step=steps - 1,
        ),
        grid_spec=pltpu.PrefetchScalarGridSpec(
            num_scalar_prefetch=1,
            grid=(steps,),
            in_specs=[whole(array) for array in head[: 1 + len(contexts)]]
            + [
                pl.BlockSpec(
                    (groups, ctx_cols // len(outs), width), lambda i, *_: (0, out_at, 0),
                    pipeline_mode=pl.Buffered(1),
                )
                for _ in outs
            ]
            + [whole(array) for array in head[1 + len(contexts) + len(outs) :]]
            + [
                pl.BlockSpec(
                    (1, 16, bias.shape[2]),
                    lambda i, *_: (i % groups, bias.shape[1] // 16 - 1, 0),
                ),
            ]
            + specs
            + [whole(array) for array in tail],
            out_specs=[
                pl.BlockSpec((share, width), fixed),
                pl.BlockSpec((tok, next_cols), fixed),
            ],
            scratch_shapes=[
                pltpu.VMEM((groups, ctx_cols, width), jnp.bfloat16),
                pltpu.VMEM((tok, width), jnp.bfloat16),
                pltpu.VMEM((tok, width), jnp.float32),
                pltpu.VMEM((tok, width), jnp.bfloat16),
            ],
        ),
        out_shape=[
            jax.ShapeDtypeStruct((share, width), jnp.bfloat16),
            jax.ShapeDtypeStruct((tok, next_cols), jnp.bfloat16),
        ],
        compiler_params=params(62),
        cost_estimate=pl.CostEstimate(
            flops=4 * tok * width * cols * steps, bytes_accessed=4 * width * cols * steps,
            transcendentals=tok * cols * steps,
        ),
        name="finish",
    )(place, *head, bias, *arrays, *tail)


def three_parts(values):
    high = lax.reduce_precision(values, 8, 7)
    middle = lax.reduce_precision(values - high, 8, 7)
    rest = values - high - middle
    return [part.astype(jnp.bfloat16) for part in (high, middle, rest)]


def local(
    tokens,
    query_key_value_weight,
    adapter_down_weight,
    adapter_up_weight,
    attention_out_weight,
    first_norm_gain,
    first_norm_bias,
    first_feed_weight,
    first_feed_bias,
    second_feed_weight,
    second_feed_bias,
    second_norm_gain,
    second_norm_bias,
    following_qkv_weight,
    following_bias,
    request_page_count,
    page_slot_table,
    request_adapter,
):
    tok_rows, width = tokens.shape
    dp_count = lax.axis_size("dp")
    mp_count = lax.axis_size("mp")
    dp_index = lax.axis_index("dp")
    mp_index = lax.axis_index("mp")
    kept_values = adapter_down_weight.shape[1] // ADAPTER_RANK
    heads_dev = query_key_value_weight.shape[1] // (3 * HEAD_DIM)
    pages = tok_rows // PAGE
    shared = dp_count == 8 and heads_dev == 4

    owners = request_adapter // kept_values
    level = jnp.sum(jnp.where(owners == mp_index, request_adapter % kept_values, 0))
    down = lax.dynamic_slice_in_dim(
        adapter_down_weight, level * ADAPTER_RANK, ADAPTER_RANK, 1
    )
    up = lax.dynamic_slice_in_dim(adapter_up_weight, level * ADAPTER_RANK, ADAPTER_RANK, 0)
    up_cols = up.shape[1] // mp_count
    sent = jnp.concatenate(
        [
            jnp.broadcast_to(down.T[:, None, :], (ADAPTER_RANK, mp_count, width)),
            up.reshape(ADAPTER_RANK, mp_count, up_cols),
        ],
        axis=2,
    ).reshape(ADAPTER_RANK, mp_count * (width + up_cols))
    got = lax.all_to_all(sent, "mp", split_axis=1, concat_axis=0, tiled=True)

    def by_kind(matrix):
        split = matrix.reshape(matrix.shape[0], heads_dev, 3, HEAD_DIM)
        if shared:
            split = lax.dynamic_slice_in_dim(split, (dp_index % 2) * 2, 2, 1)
        return jnp.swapaxes(split, 1, 2).reshape(matrix.shape[0], -1)

    place = jnp.stack(
        [mp_index] + ([dp_index // 2, dp_index % 2] if shared else [0, 0])
    ).astype(jnp.int32)
    hidden_dev = first_feed_weight.shape[1]
    downs = got[:, :width].T
    ups = got[:, width:]
    weight = by_kind(query_key_value_weight)
    ups = by_kind(ups)
    if shared:
        swap = [(i, i ^ 1) for i in range(8)]
        across = [(i, i ^ 2) for i in range(8)]
        along = [(i, i ^ 4) for i in range(8)]
        move = lambda value, pairs: lax.ppermute(value, "dp", pairs)
        xs = [tokens, move(tokens, swap)]
        at = lambda flip: (dp_index ^ flip) * pages
        bases = jnp.stack([at(0), at(1)])
    else:
        xs = [tokens]
        bases = jnp.stack([dp_index * pages])
    args = (request_page_count, page_slot_table)
    q, *kvs = project(*args, owners, bases, xs, weight, downs, ups, pages)
    bias_rows = jnp.pad(jnp.stack(three_parts(first_feed_bias)), ((0, 13), (0, 0)))
    out_rows = attention_out_weight.shape[0]
    if shared:
        unit = hidden_dev // 8
        turn = (dp_index % 2) * 4 + dp_index // 2
        kv_x = [move(kv, across) for kv in kvs]
        kv_y = [move(kv, along) for kv in kvs]
        first = lax.dynamic_slice_in_dim(first_feed_weight, turn * unit, unit, 1)
        first, _, _ = lax.optimization_barrier((first, ups, weight))
        first = lax.all_gather(first, "mp", axis=0)
        step = functools.partial(attend, *args)
        state = step(bases, bases, q, kvs, None, False, pages)
        second_map, out_map, bias_rows, _ = lax.optimization_barrier(
            (second_feed_weight, attention_out_weight, bias_rows, kvs)
        )
        rest = jnp.concatenate(
            [
                lax.dynamic_slice_in_dim(second_map, turn * unit, unit, 0),
                lax.dynamic_slice_in_dim(
                    out_map, (dp_index % 2) * (out_rows // 2), out_rows // 2, 0
                ),
                bias_rows,
            ],
            axis=0,
        )
        rest = lax.all_gather(rest, "mp", axis=0)
        kv_x, kv_y, state, first = lax.optimization_barrier((kv_x, kv_y, state, first))
        kv_d0 = move(kv_y[0], across)
        kv_d1 = move(kv_x[1], along)
        near = [at(2), at(3), at(4), at(5)]
        far = [at(6), at(7)]
        swapped, own = bases[1:], bases[:1]
        late = step(
            swapped, jnp.stack(near), q, [*kv_x, *kv_y], state, False, pages, q_from=tok_rows
        )
        first_other = move(first, swap)
        kv_d0, kv_d1, late, first, first_other = lax.optimization_barrier(
            (kv_d0, kv_d1, late, first, first_other)
        )
        first_x = move(first, across)
        first_y = move(first, along)
        theirs = step(
            swapped, jnp.stack(far), q, [kv_d0, kv_d1], late, True, pages, q_from=tok_rows
        )
        theirs, rest, first_x, first_y = lax.optimization_barrier((theirs, rest, first_x, first_y))
        second = rest[:, :unit]
        second_x = move(second, across)
        second_y = move(second, along)
        cut = width // 2
        first_d0 = move(first_y[:, :cut], across)
        first_d1 = move(first_x[:, cut:], along)
        rest_other = move(rest, swap)
        theirs, state = lax.optimization_barrier((move(theirs, swap), state))
        theirs = lax.all_gather(theirs, "mp", axis=0)
        mine = step(
            own, jnp.stack(near + far), q, [*kv_x, *kv_y, kv_d0, kv_d1], state, True, pages
        )
        mine_all = lax.all_gather(mine, "mp", axis=0)
        theirs, _, first_x, first_y, first_d0, first_d1, second_x, second_y, rest_other = (
            lax.optimization_barrier(
                (
                    theirs, mine, first_x, first_y, first_d0, first_d1, second_x, second_y,
                    rest_other,
                )
            )
        )
        half = unit // 2
        second_d0 = move(second_y[:, :half], across)
        second_d1 = move(second_x[:, half:], along)
        firsts = [first, first_x, first_y, first_d0, first_d1]
        first_others = [first_other] + [move(piece, swap) for piece in firsts[1:]]
        seconds = [second_x, second_y, second_d0, second_d1]
        second_others = [move(piece, swap) for piece in seconds[:3]]
        last, mine_all = lax.optimization_barrier((second_d1, mine_all))
        second_others.append(move(last, swap))
        contexts = [mine_all, theirs]
        bias_rows = rest
        seconds = [rest, *seconds]
        second_others = [rest_other, *second_others]
        sets = [(firsts, seconds), (first_others, second_others)]
        outs = [rest, rest_other]
    else:
        everything = lax.all_gather(kvs[0], "dp", axis=0, tiled=True)
        context = attend(
            *args, bases, jnp.zeros((1,), jnp.int32), q, [everything], None, True, pages
        )
        second = lax.all_gather(second_feed_weight, "mp", axis=0)
        bias_rows = lax.all_gather(bias_rows, "mp", axis=0)
        sets = [([lax.all_gather(first_feed_weight, "mp", axis=0)], [second])]
        outs = [lax.all_gather(attention_out_weight, "mp", axis=0)]
        contexts = [lax.all_gather(context, "mp", axis=0)]
    layer_rows, next_proj = finish(
        place, tokens, contexts, outs, first_norm_gain, first_norm_bias, bias_rows, sets,
        second_feed_bias, second_norm_gain, second_norm_bias, following_qkv_weight,
        following_bias, tok_rows // mp_count,
    )
    return (layer_rows, next_proj)


def solution(mesh):
    placed = (
        P("dp", None),
        P(None, "mp"),
        P(None, "mp"),
        P("mp", None),
        P("mp", None),
        P(),
        P(),
        P(None, "mp"),
        P("mp"),
        P("mp", None),
        P(),
        P(),
        P(),
        P(None, "mp"),
        P("mp"),
        P(),
        P(),
        P(),
    )
    return jax.shard_map(
        local,
        mesh=mesh,
        in_specs=placed,
        out_specs=(P(("dp", "mp"), None), P("dp", "mp")),
        check_vma=False,
    )
```

```python
import functools
import math

import jax
import jax.numpy as jnp
from jax import lax
from jax.experimental import pallas as pl
from jax.experimental.pallas import tpu as pltpu
from jax.sharding import PartitionSpec as P

HEAD_DIM = 64
ADAPTER_RANK = 16
PAGE = 128
PAIR = 2 * HEAD_DIM
NEG = -1e30
EXP_SCALE = math.log2(math.e) * HEAD_DIM**-0.5
MIB = 1 << 20


def params(vmem):
    return pltpu.CompilerParams(
        dimension_semantics=("arbitrary",), vmem_limit_bytes=vmem * MIB
    )


def request_of(k, counts, requests):
    end = counts[0]
    request = (k >= end).astype(jnp.int32)
    for r in range(1, requests - 1):
        end = end + counts[r]
        request = request + (k >= end).astype(jnp.int32)
    return request


def normalize(values, gain_row, bias_row):
    average = jnp.mean(values, axis=-1, keepdims=True)
    centered = values - average
    variance = jnp.mean(centered * centered, axis=-1, keepdims=True)
    return centered * lax.rsqrt(variance + 1e-05) * gain_row + bias_row


def project_kernel(
    counts, table, owners, bases, *refs, requests, slots, pages, per_piece, parts,
):
    x_refs = refs[:parts]
    w_ref, down_ref, up_ref, q_ref = refs[parts : parts + 4]
    kv_refs = refs[parts + 4 : 2 * parts + 4]
    joined, page_owner = refs[2 * parts + 4 :]
    step = pl.program_id(0)
    cols = w_ref.shape[1]

    @pl.when(step == 0)
    def _():
        joined[:, :cols] = w_ref[...]
        joined[:, cols:] = down_ref[...]

        def fill(k, carry):
            page_owner[table[k]] = owners[request_of(k, counts, requests)]
            return carry

        lax.fori_loop(0, slots, fill, 0)

    piece = step * pages // per_piece

    def block(x_ref, kv_ref):
        both = jnp.dot(x_ref[...], joined[...], preferred_element_type=jnp.float32)
        low = both[:, cols:]
        lane_owner = lax.broadcasted_iota(jnp.int32, (PAGE, low.shape[1]), 1) // ADAPTER_RANK
        kept = []
        for p in range(pages):
            page = step * pages + p
            slot = bases[page // per_piece] + page % per_piece
            kept.append(
                jnp.where(lane_owner == page_owner[slot], low[p * PAGE : (p + 1) * PAGE], 0.0)
            )
        low_rank = jnp.concatenate(kept, axis=0).astype(jnp.bfloat16)
        rows = both[:, :cols] + jnp.dot(
            low_rank, up_ref[...], preferred_element_type=jnp.float32
        )
        rows = rows.astype(jnp.bfloat16)
        q_cols = q_ref.shape[1]
        q_ref[...] = rows[:, :q_cols]
        keys = rows[:, q_cols : 2 * q_cols]
        values = rows[:, 2 * q_cols :]
        for p in range(pages):
            here = slice(p * PAGE, (p + 1) * PAGE)
            kv_ref[p, :PAIR, :] = keys[here].T
            kv_ref[p, PAIR:, :] = values[here]

    for i in range(parts):
        pl.when(piece == i)(functools.partial(block, x_refs[i], kv_refs[i]))


def project(counts, table, owners, bases, xs, weight, down, up, per_piece):
    tok, width = xs[0].shape
    cols = weight.shape[1]
    pages = min(4, tok // PAGE)
    rows_step = pages * PAGE
    slots = table.shape[0]
    parts = len(xs)
    each = tok // rows_step
    total = tok * parts
    whole = lambda i, *_: (0, 0)
    rows = lambda i, *_: (i, 0)

    def own(part, *zeros):
        return lambda i, *_: (jnp.clip(i - part * each, 0, each - 1), 0, *zeros)

    return pl.pallas_call(
        functools.partial(
            project_kernel,
            requests=counts.shape[0], slots=slots, pages=pages, per_piece=per_piece, parts=parts,
        ),
        grid_spec=pltpu.PrefetchScalarGridSpec(
            num_scalar_prefetch=4,
            grid=(total // rows_step,),
            in_specs=[pl.BlockSpec((rows_step, width), own(i)) for i in range(parts)]
            + [
                pl.BlockSpec(weight.shape, whole),
                pl.BlockSpec(down.shape, whole),
                pl.BlockSpec(up.shape, whole),
            ],
            out_specs=[
                pl.BlockSpec((rows_step, cols // 3), rows),
            ]
            + [pl.BlockSpec((pages, PAIR + PAGE, PAIR), own(i, 0)) for i in range(parts)],
            scratch_shapes=[
                pltpu.VMEM((width, cols + down.shape[1]), jnp.bfloat16),
                pltpu.SMEM((slots,), jnp.int32),
            ],
        ),
        out_shape=[
            jax.ShapeDtypeStruct((total, cols // 3), jnp.bfloat16),
        ]
        + [jax.ShapeDtypeStruct((tok // PAGE, PAIR + PAGE, PAIR), jnp.bfloat16)] * parts,
        compiler_params=params(62),
        cost_estimate=pl.CostEstimate(
            flops=2 * total * width * cols, bytes_accessed=2 * total * (width + cols),
            transcendentals=0,
        ),
        name="project",
    )(counts, table, owners, bases, *xs, weight, down, up)


def attend_kernel(
    counts, table, q_bases, kv_bases, q_hbm, *refs,
    requests, slots, q_size, q_from, state_from, arrays, sizes, first, last, group,
):
    refs = list(refs)
    kv_hbm = [refs.pop(0) for _ in arrays]
    state_hbm = [] if first else [refs.pop(0), refs.pop(0)]
    if last:
        out_ref = refs.pop(0)
    else:
        acc_out, stat_out = refs.pop(0), refs.pop(0)
    kv, scores, listed, amount, asked, q_amount, sems, q_ref = refs[:8]
    if not first:
        acc_in, stat_in = refs[8:]
    tok = q_ref.shape[0]
    targets = [(q_hbm.at[pl.ds(q_from, tok)], q_ref)]
    offset = 0
    for i, size in enumerate(arrays):
        targets.append((kv_hbm[i], kv.at[pl.ds(offset, size)]))
        offset += size
    targets += [(ref.at[pl.ds(state_from, tok)], own) for ref, own in zip(state_hbm, refs[8:])]
    copies = [
        pltpu.make_async_copy(source, target, sems.at[n])
        for n, (source, target) in enumerate(targets)
    ]
    for copy in copies:
        copy.start()
    for r in range(requests):
        amount[r] = 0
        q_amount[r] = 0

    def place_of(slot, bases, extents):
        place = jnp.int32(-1)
        offset = 0
        for i, size in enumerate(extents):
            near = slot - bases[i]
            place = jnp.where((near >= 0) & (near < size), near + offset, place)
            offset += size
        return place

    q_sizes = (q_size,) * (q_ref.shape[0] // (q_size * PAGE))

    def fill(k, carry):
        r = request_of(k, counts, requests)
        slot = table[k]
        place = place_of(slot, kv_bases, sizes)
        q_place = place_of(slot, q_bases, q_sizes)

        @pl.when(place >= 0)
        def _():
            n = amount[r]
            listed[r, n] = place
            amount[r] = n + 1

        @pl.when(q_place >= 0)
        def _():
            n = q_amount[r]
            asked[r, n] = q_place
            q_amount[r] = n + 1

        return carry

    lax.fori_loop(0, slots, fill, 0)
    for copy in copies:
        copy.wait()
    lane = lax.broadcasted_iota(jnp.int32, (PAGE, PAIR), 1)
    low_lane = lane < HEAD_DIM
    rows = 4 * PAGE

    def one_pair(r, p):
        n = amount[r]
        full = n // group
        blocks = (n + group - 1) // group
        count = q_amount[r]
        a = asked[r, 2 * p]
        b = asked[r, jnp.minimum(2 * p + 1, count - 1)]
        spots = [pl.ds(pl.multiple_of(t * PAGE, PAGE), PAGE) for t in (a, b)]
        parts = []
        for spot in spots:
            q = q_ref[spot, :]
            zero = jnp.zeros_like(q)
            parts += [jnp.where(low_lane, q, zero), jnp.where(low_lane, zero, q)]
        stacked = jnp.concatenate(parts, axis=0)

        def page_of(j, i):
            return listed[r, jnp.minimum(j * group + i, n - 1)]

        def score(masked, j, top):
            keys = jnp.concatenate(
                [kv[page_of(j, i), :PAIR, :] for i in range(group)], axis=1
            )
            s = jnp.dot(stacked, keys, preferred_element_type=jnp.float32)
            for i in range(group):
                piece = s[:, i * PAGE : (i + 1) * PAGE]
                if masked and i:
                    piece = jnp.where(j * group + i < n, piece, NEG)
                scores[j, :, i * PAGE : (i + 1) * PAGE] = piece
                top = jnp.maximum(top, piece)
            return top

        top = jnp.full((rows, PAGE), NEG, jnp.float32)
        top = lax.fori_loop(0, full, functools.partial(score, False), top)
        top = lax.fori_loop(full, blocks, functools.partial(score, True), top)
        peak = jnp.max(top, axis=1, keepdims=True)
        if not first:
            old = jnp.concatenate(
                [stat_in[spot, h : h + 1] for spot in spots for h in (0, 1)], axis=0
            )
            peak = jnp.maximum(peak, old)
        shift = peak * EXP_SCALE

        def weigh(j, carry):
            total, acc = carry
            w = jnp.exp2(scores[j] * EXP_SCALE - shift)
            for i in range(group):
                total = total + w[:, i * PAGE : (i + 1) * PAGE]
            values = jnp.concatenate(
                [kv[page_of(j, i), PAIR:, :] for i in range(group)], axis=0
            )
            acc = acc + jnp.dot(
                w.astype(jnp.bfloat16), values, preferred_element_type=jnp.float32
            )
            return total, acc

        total, acc = lax.fori_loop(
            0, blocks, weigh,
            (jnp.zeros((rows, PAGE), jnp.float32), jnp.zeros((rows, PAIR), jnp.float32)),
        )
        total = jnp.sum(total, axis=1, keepdims=True)
        if not first:
            shrink = jnp.exp2((old - peak) * EXP_SCALE)
            total = total + shrink * jnp.concatenate(
                [stat_in[spot, h : h + 1] for spot in spots for h in (2, 3)], axis=0
            )
        for t, spot in enumerate(spots):
            h0 = slice(2 * t * PAGE, (2 * t + 1) * PAGE)
            h1 = slice((2 * t + 1) * PAGE, (2 * t + 2) * PAGE)
            value = jnp.where(low_lane, acc[h0], acc[h1])
            if not first:
                value = value + acc_in[spot, :] * jnp.where(low_lane, shrink[h0], shrink[h1])
            if last:
                value = value / jnp.where(low_lane, total[h0], total[h1])
                out_ref[spot, :] = value.astype(jnp.bfloat16)
            else:
                acc_out[spot, :] = value
                stat = jnp.where(lane == 0, peak[h0], peak[h1])
                stat = jnp.where(lane == 2, total[h0], stat)
                stat_out[spot, :] = jnp.where(lane == 3, total[h1], stat)

    def visit_request(r, carry):
        def visit(p, inner):
            one_pair(r, p)
            return inner

        return lax.fori_loop(0, (q_amount[r] + 1) // 2, visit, carry)

    lax.fori_loop(0, requests, visit_request, 0)


def attend(counts, table, q_bases, kv_bases, q, pieces, state, last, q_size, q_from=0):
    tok = q_bases.shape[0] * q_size * PAGE
    state_from = 0 if state is None or state[0].shape[0] == tok else q_from
    arrays = tuple(p.shape[0] for p in pieces)
    sizes = (sum(arrays) // kv_bases.shape[0],) * kv_bases.shape[0]
    first = state is None
    group = 4
    slots = table.shape[0]
    requests = counts.shape[0]
    most = min(sum(sizes), slots)
    state_shape = [jax.ShapeDtypeStruct((tok, PAIR), jnp.float32)] * 2
    out = pl.pallas_call(
        functools.partial(
            attend_kernel,
            requests=requests, slots=slots, q_size=q_size, q_from=q_from, state_from=state_from, arrays=arrays, sizes=sizes,
            first=first, last=last, group=group,
        ),
        grid_spec=pltpu.PrefetchScalarGridSpec(
            num_scalar_prefetch=4,
            grid=(1,),
            in_specs=[pl.BlockSpec(memory_space=pl.ANY)] * (len(pieces) + (1 if first else 3)),
            out_specs=[pl.BlockSpec((tok, PAIR), lambda i, *_: (0, 0))] * (1 if last else 2),
            scratch_shapes=[
                pltpu.VMEM((sum(sizes), PAIR + PAGE, PAIR), jnp.bfloat16),
                pltpu.VMEM(((most + group - 1) // group, 4 * PAGE, group * PAGE), jnp.float32),
                pltpu.SMEM((requests, sum(sizes)), jnp.int32),
                pltpu.SMEM((requests,), jnp.int32),
                pltpu.SMEM((requests, tok // PAGE), jnp.int32),
                pltpu.SMEM((requests,), jnp.int32),
                pltpu.SemaphoreType.DMA((len(pieces) + 3,)),
                pltpu.VMEM((tok, PAIR), jnp.bfloat16),
            ]
            + ([] if first else [pltpu.VMEM((tok, PAIR), jnp.float32)] * 2),
        ),
        out_shape=[jax.ShapeDtypeStruct((tok, PAIR), jnp.bfloat16)] if last else state_shape,
        compiler_params=params(62),
        cost_estimate=pl.CostEstimate(
            flops=tok * PAIR, bytes_accessed=4 * tok * PAIR, transcendentals=0,
        ),
        name="attend",
    )(counts, table, q_bases, kv_bases, q, *pieces, *([] if first else state))
    return out[0] if last else out


def finish_kernel(place, x_ref, *refs, parts, counts, last_step):
    refs = list(refs)
    ctx_refs, refs = refs[:parts], refs[parts:]
    out_w_refs, refs = refs[:parts], refs[parts:]
    gain1_ref, bias1_ref, bias_ref = refs[:3]
    refs = refs[3:]
    sets = []
    for n1, n2 in counts:
        w1s, refs = refs[:n1], refs[n1:]
        w2s, refs = refs[:n2], refs[n2:]
        sets.append((w1s, w2s))
    b2_ref, gain_ref, bias2_ref, next_w_ref, next_b_ref = refs[:5]
    layer_ref, next_ref, joined, normed_ref, acc, done = refs[5:]
    step = pl.program_id(0)
    tok = normed_ref.shape[0]
    block = min(512, tok)
    halves = len(sets)
    groups = (last_step + 1) // halves

    @pl.when(step == 0)
    def _():
        near = joined.shape[1] // parts
        for i in range(parts):
            joined[:, i * near : (i + 1) * near] = out_w_refs[i][:, :near]
        for t in range(tok // block):
            rows = slice(t * block, (t + 1) * block)
            mixed = x_ref[rows, :].astype(jnp.float32)
            for j in range(joined.shape[0]):
                ctx = jnp.concatenate([ref[j, rows, :] for ref in ctx_refs], axis=1)
                mixed = mixed + jnp.dot(ctx, joined[j], preferred_element_type=jnp.float32)
            normed = normalize(mixed, gain1_ref[...], bias1_ref[...]).astype(jnp.bfloat16)
            normed_ref[rows, :] = normed
            acc[rows, :] = normed.astype(jnp.float32) + b2_ref[...]

    def absorb(h, w1_refs, w2_refs):
        if len(w1_refs) == 1:
            w1 = w1_refs[0][0]
            starts, cols = [0], w1.shape[1]
        else:
            diagonal = jnp.concatenate([w1_refs[3][0], w1_refs[4][0]], axis=0)
            w1 = jnp.concatenate([ref[0] for ref in w1_refs[:3]] + [diagonal], axis=1)
            cols = diagonal.shape[1]
            core = place[2] if h == 0 else 1 - place[2]
            starts = [
                pl.multiple_of((core * 4 + (place[1] ^ r)) * cols, cols) for r in range(4)
            ]
        w2 = jnp.concatenate([ref[0] for ref in w2_refs], axis=0)
        bias = jnp.concatenate(
            [
                jnp.sum(
                    bias_ref[0, :, pl.ds(start, cols)].astype(jnp.float32), axis=0, keepdims=True
                )
                for start in starts
            ],
            axis=1,
        )
        for t in range(tok // block):
            rows = slice(t * block, (t + 1) * block)
            pre = jnp.dot(normed_ref[rows, :], w1, preferred_element_type=jnp.float32) + bias
            hidden = 0.5 * pre * (1.0 + lax.erf(pre * math.sqrt(0.5)))
            acc[rows, :] += jnp.dot(
                hidden.astype(jnp.bfloat16), w2, preferred_element_type=jnp.float32
            )

    for h in range(halves):
        pl.when(step // groups == h)(functools.partial(absorb, h, *sets[h]))

    @pl.when(step == last_step)
    def _():
        for t in range(tok // block):
            rows = slice(t * block, (t + 1) * block)
            layer = normalize(acc[rows, :], gain_ref[...], bias2_ref[...]).astype(jnp.bfloat16)
            done[rows, :] = layer
            next_ref[rows, :] = (
                jnp.dot(layer, next_w_ref[...], preferred_element_type=jnp.float32)
                + next_b_ref[...]
            ).astype(jnp.bfloat16)
        share = layer_ref.shape[0]
        layer_ref[...] = done[pl.ds(pl.multiple_of(place[0] * share, share), share), :]


def finish(
    place, x, contexts, outs, gain1, bias1, bias, sets, b2, gain, bias2, next_w, next_b, share
):
    tok, width = x.shape
    halves = len(sets)
    groups = bias.shape[0]
    ctx_cols = sum(ctx.shape[2] for ctx in contexts)
    cols = bias.shape[2] // halves
    steps = halves * groups
    out_at = 1 if len(outs) > 1 else 0

    def whole(array):
        return pl.BlockSpec(
            array.shape, lambda i, *_: (0,) * array.ndim, pipeline_mode=pl.Buffered(1)
        )

    specs, arrays = [], []
    for h, (w1s, w2s) in enumerate(sets):
        at = lambda i, *_, h=h: (jnp.clip(i - h * groups, 0, groups - 1), 0, 0)
        for n, array in enumerate((*w1s, *w2s)):
            rows = array.shape[1]
            if len(w1s) > 1 and n == len(w1s):
                rows = w1s[0].shape[2]
            specs.append(pl.BlockSpec((1, rows, array.shape[2]), at))
            arrays.append(array)
    head = [x, *contexts, *outs, gain1[None], bias1[None]]
    tail = [b2[None], gain[None], bias2[None], next_w, next_b[None]]
    next_cols = next_w.shape[1]
    fixed = lambda i, *_: (0, 0)
    return pl.pallas_call(
        functools.partial(
            finish_kernel,
            parts=len(outs),
            counts=tuple((len(w1s), len(w2s)) for w1s, w2s in sets),
            last_step=steps - 1,
        ),
        grid_spec=pltpu.PrefetchScalarGridSpec(
            num_scalar_prefetch=1,
            grid=(steps,),
            in_specs=[whole(array) for array in head[: 1 + len(contexts)]]
            + [
                pl.BlockSpec(
                    (groups, ctx_cols // len(outs), width), lambda i, *_: (0, out_at, 0),
                    pipeline_mode=pl.Buffered(1),
                )
                for _ in outs
            ]
            + [whole(array) for array in head[1 + len(contexts) + len(outs) :]]
            + [
                pl.BlockSpec(
                    (1, 16, bias.shape[2]),
                    lambda i, *_: (i % groups, bias.shape[1] // 16 - 1, 0),
                ),
            ]
            + specs
            + [whole(array) for array in tail],
            out_specs=[
                pl.BlockSpec((share, width), fixed),
                pl.BlockSpec((tok, next_cols), fixed),
            ],
            scratch_shapes=[
                pltpu.VMEM((groups, ctx_cols, width), jnp.bfloat16),
                pltpu.VMEM((tok, width), jnp.bfloat16),
                pltpu.VMEM((tok, width), jnp.float32),
                pltpu.VMEM((tok, width), jnp.bfloat16),
            ],
        ),
        out_shape=[
            jax.ShapeDtypeStruct((share, width), jnp.bfloat16),
            jax.ShapeDtypeStruct((tok, next_cols), jnp.bfloat16),
        ],
        compiler_params=params(62),
        cost_estimate=pl.CostEstimate(
            flops=4 * tok * width * cols * steps, bytes_accessed=4 * width * cols * steps,
            transcendentals=tok * cols * steps,
        ),
        name="finish",
    )(place, *head, bias, *arrays, *tail)


def three_parts(values):
    high = lax.reduce_precision(values, 8, 7)
    middle = lax.reduce_precision(values - high, 8, 7)
    rest = values - high - middle
    return [part.astype(jnp.bfloat16) for part in (high, middle, rest)]


def local(
    tokens,
    query_key_value_weight,
    adapter_down_weight,
    adapter_up_weight,
    attention_out_weight,
    first_norm_gain,
    first_norm_bias,
    first_feed_weight,
    first_feed_bias,
    second_feed_weight,
    second_feed_bias,
    second_norm_gain,
    second_norm_bias,
    following_qkv_weight,
    following_bias,
    request_page_count,
    page_slot_table,
    request_adapter,
):
    tok_rows, width = tokens.shape
    dp_count = lax.axis_size("dp")
    mp_count = lax.axis_size("mp")
    dp_index = lax.axis_index("dp")
    mp_index = lax.axis_index("mp")
    kept_values = adapter_down_weight.shape[1] // ADAPTER_RANK
    heads_dev = query_key_value_weight.shape[1] // (3 * HEAD_DIM)
    pages = tok_rows // PAGE
    shared = dp_count == 8 and heads_dev == 4

    owners = request_adapter // kept_values
    level = jnp.sum(jnp.where(owners == mp_index, request_adapter % kept_values, 0))
    down = lax.dynamic_slice_in_dim(
        adapter_down_weight, level * ADAPTER_RANK, ADAPTER_RANK, 1
    )
    up = lax.dynamic_slice_in_dim(adapter_up_weight, level * ADAPTER_RANK, ADAPTER_RANK, 0)
    up_cols = up.shape[1] // mp_count
    sent = jnp.concatenate(
        [
            jnp.broadcast_to(down.T[:, None, :], (ADAPTER_RANK, mp_count, width)),
            up.reshape(ADAPTER_RANK, mp_count, up_cols),
        ],
        axis=2,
    ).reshape(ADAPTER_RANK, mp_count * (width + up_cols))
    got = lax.all_to_all(sent, "mp", split_axis=1, concat_axis=0, tiled=True)

    def by_kind(matrix):
        split = matrix.reshape(matrix.shape[0], heads_dev, 3, HEAD_DIM)
        if shared:
            split = lax.dynamic_slice_in_dim(split, (dp_index % 2) * 2, 2, 1)
        return jnp.swapaxes(split, 1, 2).reshape(matrix.shape[0], -1)

    place = jnp.stack(
        [mp_index] + ([dp_index // 2, dp_index % 2] if shared else [0, 0])
    ).astype(jnp.int32)
    hidden_dev = first_feed_weight.shape[1]
    downs = got[:, :width].T
    ups = got[:, width:]
    weight = by_kind(query_key_value_weight)
    ups = by_kind(ups)
    if shared:
        swap = [(i, i ^ 1) for i in range(8)]
        across = [(i, i ^ 2) for i in range(8)]
        along = [(i, i ^ 4) for i in range(8)]
        move = lambda value, pairs: lax.ppermute(value, "dp", pairs)
        xs = [tokens, move(tokens, swap)]
        at = lambda flip: (dp_index ^ flip) * pages
        bases = jnp.stack([at(0), at(1)])
    else:
        xs = [tokens]
        bases = jnp.stack([dp_index * pages])
    args = (request_page_count, page_slot_table)
    q, *kvs = project(*args, owners, bases, xs, weight, downs, ups, pages)
    bias_rows = jnp.pad(jnp.stack(three_parts(first_feed_bias)), ((0, 13), (0, 0)))
    out_rows = attention_out_weight.shape[0]
    if shared:
        unit = hidden_dev // 8
        turn = (dp_index % 2) * 4 + dp_index // 2
        kv_x = [move(kv, across) for kv in kvs]
        kv_y = [move(kv, along) for kv in kvs]
        first = lax.dynamic_slice_in_dim(first_feed_weight, turn * unit, unit, 1)
        first, _, _ = lax.optimization_barrier((first, ups, weight))
        first = lax.all_gather(first, "mp", axis=0)
        step = functools.partial(attend, *args)
        state = step(bases, bases, q, kvs, None, False, pages)
        second_map, out_map, bias_rows, _ = lax.optimization_barrier(
            (second_feed_weight, attention_out_weight, bias_rows, kvs)
        )
        rest = jnp.concatenate(
            [
                lax.dynamic_slice_in_dim(second_map, turn * unit, unit, 0),
                lax.dynamic_slice_in_dim(
                    out_map, (dp_index % 2) * (out_rows // 2), out_rows // 2, 0
                ),
                bias_rows,
            ],
            axis=0,
        )
        rest = lax.all_gather(rest, "mp", axis=0)
        kv_x, kv_y, state, first = lax.optimization_barrier((kv_x, kv_y, state, first))
        kv_d0 = move(kv_y[0], across)
        kv_d1 = move(kv_x[1], along)
        near = [at(2), at(3), at(4), at(5)]
        far = [at(6), at(7)]
        swapped, own = bases[1:], bases[:1]
        late = step(
            swapped, jnp.stack(near), q, [*kv_x, *kv_y], state, False, pages, q_from=tok_rows
        )
        first_other = move(first, swap)
        kv_d0, kv_d1, late, first, first_other = lax.optimization_barrier(
            (kv_d0, kv_d1, late, first, first_other)
        )
        first_x = move(first, across)
        first_y = move(first, along)
        theirs = step(
            swapped, jnp.stack(far), q, [kv_d0, kv_d1], late, True, pages, q_from=tok_rows
        )
        theirs, rest, first_x, first_y = lax.optimization_barrier((theirs, rest, first_x, first_y))
        second = rest[:, :unit]
        second_x = move(second, across)
        second_y = move(second, along)
        rest_other = move(rest, swap)
        theirs, state = lax.optimization_barrier((move(theirs, swap), state))
        theirs = lax.all_gather(theirs, "mp", axis=0)
        mine = step(
            own, jnp.stack(near + far), q, [*kv_x, *kv_y, kv_d0, kv_d1], state, True, pages
        )
        mine_all = lax.all_gather(mine, "mp", axis=0)
        theirs, _, first_x, first_y, second_x, second_y, rest_other = lax.optimization_barrier(
            (theirs, mine, first_x, first_y, second_x, second_y, rest_other)
        )
        cut = width // 2
        first_d0 = move(first_y[:, :cut], across)
        first_d1 = move(first_x[:, cut:], along)
        half = unit // 2
        second_d0 = move(second_y[:, :half], across)
        second_d1 = move(second_x[:, half:], along)
        firsts = [first, first_x, first_y, first_d0, first_d1]
        first_others = [first_other] + [move(piece, swap) for piece in firsts[1:]]
        seconds = [second_x, second_y, second_d0, second_d1]
        second_others = [move(piece, swap) for piece in seconds[:3]]
        last, mine_all = lax.optimization_barrier((second_d1, mine_all))
        second_others.append(move(last, swap))
        contexts = [mine_all, theirs]
        bias_rows = rest
        seconds = [rest, *seconds]
        second_others = [rest_other, *second_others]
        sets = [(firsts, seconds), (first_others, second_others)]
        outs = [rest, rest_other]
    else:
        everything = lax.all_gather(kvs[0], "dp", axis=0, tiled=True)
        context = attend(
            *args, bases, jnp.zeros((1,), jnp.int32), q, [everything], None, True, pages
        )
        second = lax.all_gather(second_feed_weight, "mp", axis=0)
        bias_rows = lax.all_gather(bias_rows, "mp", axis=0)
        sets = [([lax.all_gather(first_feed_weight, "mp", axis=0)], [second])]
        outs = [lax.all_gather(attention_out_weight, "mp", axis=0)]
        contexts = [lax.all_gather(context, "mp", axis=0)]
    layer_rows, next_proj = finish(
        place, tokens, contexts, outs, first_norm_gain, first_norm_bias, bias_rows, sets,
        second_feed_bias, second_norm_gain, second_norm_bias, following_qkv_weight,
        following_bias, tok_rows // mp_count,
    )
    return (layer_rows, next_proj)


def solution(mesh):
    placed = (
        P("dp", None),
        P(None, "mp"),
        P(None, "mp"),
        P("mp", None),
        P("mp", None),
        P(),
        P(),
        P(None, "mp"),
        P("mp"),
        P("mp", None),
        P(),
        P(),
        P(),
        P(None, "mp"),
        P("mp"),
        P(),
        P(),
        P(),
    )
    return jax.shard_map(
        local,
        mesh=mesh,
        in_specs=placed,
        out_specs=(P(("dp", "mp"), None), P("dp", "mp")),
        check_vma=False,
    )
```
